512 devices in a mesh: space: 64 (over x_hi, z, core), sub: 8 (over y, x_lo).
Axes of the slice: x: 4 (x_hi: 2, x_lo: 2; x = x_hi * 2 + x_lo), y: 4, z: 16, core: 2. Of those that a mesh axis runs over, the one named last changes fastest.
Arguments:
- positions: float32 [3, 128, 16, 3, 128], P(None, 'space', 'sub'), may hold values from 0 to 1
- charges: float32 [128, 16, 3, 128], P('space', 'sub'), may hold values from -0.6 to 0.6
- counts: int32 [128, 16, 3], P('space', 'sub'), may hold values from 64 to 128
Outputs:
- forces: float32 [3, 128, 16, 3, 128], P(None, 'space', 'sub')
The draws below stay inside these ranges and needn't reach their ends.
Inputs may be any that keep to these rules, and one draw needn't show every extreme that they name: `counts`: slots 0 to count - 1 of a cell hold atoms; the others are padding.
All inputs are finite; a program needn't handle non-finite values.
Results may differ from the reference program's by a relative error of at most 0.0003.
Values sent between devices are 32-bit elements; how exact they have to be, the bound alone decides.
A program may use at most 64 MiB of HBM per device.

```python
import math
import jax
import jax.numpy as jnp
from jax import lax

ATOMS = 128
POINTS = 4
REACH = 4
CELLS_X = 128
CELLS_Y = 16
CELLS_Z = 3


def with_ends(drawn, rng, smallest, top_value):
    dims = drawn.shape
    spot = [jax.random.randint(jax.random.fold_in(rng, axis), (), 0, dims[axis]) for axis in range(len(dims))]
    drawn = drawn.at[tuple(spot)].set(smallest)
    longest = dims.index(max(dims))
    spot[longest] = (spot[longest] + 1) % dims[longest]
    return drawn.at[tuple(spot)].set(top_value)


def levels(rng, extent, cuts, least, high):
    loudness = 1.0
    for position, blocks in cuts:
        heights = jax.random.uniform(jax.random.fold_in(jax.random.fold_in(rng, 6), position), (blocks,), jnp.float32, least / len(cuts), high / len(cuts))
        loudness = loudness * jnp.repeat(jnp.exp(heights), extent[position] // blocks).reshape((-1,) + (1,) * (len(extent) - 1 - position))
    return loudness


def bell_draw(key, extent, scale, bound, cuts=(), dtype=jnp.bfloat16):
    entries = scale * jax.random.normal(key, extent, jnp.float32)
    if cuts:
        entries = entries * levels(key, extent, cuts, -0.22, 0.18)
    return jnp.clip(entries, -bound, bound).astype(dtype)


def setup_inputs(seed: int = 0) -> dict:
    arg_keys = jax.random.split(jax.random.key(seed), 4)
    return {
        "positions": jnp.clip(1.0 * jax.random.uniform(arg_keys[0], (3, CELLS_X, CELLS_Y, CELLS_Z, ATOMS), jnp.float32) ** levels(arg_keys[0], (3, CELLS_X, CELLS_Y, CELLS_Z, ATOMS), ((1, 64), (2, 8)), -0.2, 0.2), 0.0, 1.0),
        "charges": bell_draw(arg_keys[1], (CELLS_X, CELLS_Y, CELLS_Z, ATOMS), 0.1, 0.6, ((0, 64), (1, 8)), jnp.float32),
        "counts": with_ends(jax.random.randint(arg_keys[2], (CELLS_X, CELLS_Y, CELLS_Z), ATOMS // 2, ATOMS + 1), jax.random.fold_in(arg_keys[2], 1), ATOMS // 2, ATOMS).astype(jnp.int32),
    }


SOFT_SQUARE = 0.0625
SPLIT_RATE = 0.8
FINE_WIDTHS = (1.0, 2.0)
FINE_WEIGHTS = (2.0, 0.5)
COARSE_FRACTIONS = (8.0, 4.0)
COARSE_WEIGHTS = (4.0, 2.0)
HIGHEST = lax.Precision.HIGHEST

def pair_force(own_pos, own_charge, other_pos, other_charge, offset_vec):
    shifted = own_pos - offset_vec.reshape((3,) + (1,) * (own_pos.ndim - 1))
    spread = shifted[..., :, None] - other_pos[..., None, :]
    square = lax.optimization_barrier(jnp.sum(spread * spread, axis=0)) + SOFT_SQUARE
    length = jnp.sqrt(square)
    factor = jax.scipy.special.erfc(SPLIT_RATE * length) / (square * length)
    factor = factor + 2.0 * SPLIT_RATE / math.sqrt(math.pi) * jnp.exp(-SPLIT_RATE * SPLIT_RATE * square) / square
    stacked = jnp.concatenate([other_charge[None], other_charge[None] * other_pos], axis=0)
    moments = jnp.einsum('...ab,c...b->c...a', factor, stacked, precision=HIGHEST)
    return own_charge * (shifted * moments[0][None] - moments[1:])

def spline(shifted):
    magnitude = jnp.abs(shifted)
    inner = (4.0 - 6.0 * magnitude * magnitude + 3.0 * magnitude * magnitude * magnitude) / 6.0
    outer = (2.0 - magnitude) * (2.0 - magnitude) * (2.0 - magnitude) / 6.0
    return jnp.where(magnitude < 1.0, inner, jnp.where(magnitude < 2.0, outer, 0.0))

def spline_slope(shifted):
    magnitude = jnp.abs(shifted)
    inner = (9.0 * magnitude * magnitude - 12.0 * magnitude) / 6.0
    outer = -(2.0 - magnitude) * (2.0 - magnitude) / 2.0
    return jnp.sign(shifted) * jnp.where(magnitude < 1.0, inner, jnp.where(magnitude < 2.0, outer, 0.0))

def spline_tables(fraction):
    offsets = lax.iota(jnp.int32, POINTS + 3).astype(jnp.float32) - 1.0
    shifted = POINTS * fraction[..., None] - offsets
    return (spline(shifted), spline_slope(shifted))

def make_boxes(coords, charged):
    weight_x = spline_tables(coords[0])[0]
    weight_y = spline_tables(coords[1])[0]
    weight_z = spline_tables(coords[2])[0]
    first = (charged[..., None] * weight_x)[..., :, None] * weight_y[..., None, :]
    return jnp.einsum('...aef,...ag->...efg', first, weight_z, precision=HIGHEST)

def placement_table():
    shape = (POINTS + 3, POINTS, 3)
    entry = lax.broadcasted_iota(jnp.int32, shape, 0)
    inside = lax.broadcasted_iota(jnp.int32, shape, 1)
    which = lax.broadcasted_iota(jnp.int32, shape, 2)
    return (entry - 1 == (which - 1) * POINTS + inside).astype(jnp.float32)

def pick_table(cells, length, first, period):
    shape = (cells, POINTS + 3, length)
    cell_idx = lax.broadcasted_iota(jnp.int32, shape, 0)
    entry = lax.broadcasted_iota(jnp.int32, shape, 1)
    point = lax.broadcasted_iota(jnp.int32, shape, 2)
    return (jnp.mod(POINTS * cell_idx + first + entry, period) == point).astype(jnp.float32)

def gauss_matrix(length, width, first_row, rows):
    row_idx = first_row + lax.broadcasted_iota(jnp.int32, (rows, length), 0)
    col_idx = lax.broadcasted_iota(jnp.int32, (rows, length), 1)
    dist = jnp.mod(row_idx - col_idx, length)
    dist = jnp.minimum(dist, length - dist).astype(jnp.float32)
    return jnp.exp(-dist * dist / (2.0 * width * width))

def taps_for(width):
    return [math.exp(-(step * step) / (2.0 * width * width)) for step in range(-REACH, REACH + 1)]

def long_forces(coords, charged, point_box):
    weight_x, slope_x = spline_tables(coords[0])
    weight_y, slope_y = spline_tables(coords[1])
    weight_z, slope_z = spline_tables(coords[2])
    along_z = jnp.einsum('xyzag,xyzefg->xyzaef', weight_z, point_box, precision=HIGHEST)
    sloped_z = jnp.einsum('xyzag,xyzefg->xyzaef', slope_z, point_box, precision=HIGHEST)
    force_x = jnp.einsum('xyzae,xyzaf,xyzaef->xyza', slope_x, weight_y, along_z, precision=HIGHEST)
    force_y = jnp.einsum('xyzae,xyzaf,xyzaef->xyza', weight_x, slope_y, along_z, precision=HIGHEST)
    force_z = jnp.einsum('xyzae,xyzaf,xyzaef->xyza', weight_x, weight_y, sloped_z, precision=HIGHEST)
    return -POINTS * charged * jnp.stack([force_x, force_y, force_z])

def reference(positions, charges, counts):
    live_mask = (lax.broadcasted_iota(jnp.int32, charges.shape, 3) < counts[..., None]).astype(jnp.float32)
    charged = charges * live_mask
    short = jnp.zeros(positions.shape, jnp.float32)
    for offset in range(27):
        steps_xyz = (offset // 9 - 1, offset // 3 % 3 - 1, offset % 3 - 1)
        back = tuple((-step for step in steps_xyz))
        near_pos = jnp.roll(positions, back, axis=(1, 2, 3))
        near_charge = jnp.roll(charged, back, axis=(0, 1, 2))
        offset_vec = jnp.array(steps_xyz, jnp.float32)

        def slab_force(members, offset_vec=offset_vec):
            return pair_force(members[0], members[1], members[2], members[3], offset_vec)
        result = lax.map(slab_force, (jnp.moveaxis(positions, 1, 0), charged, jnp.moveaxis(near_pos, 1, 0), near_charge))
        short = short + jnp.moveaxis(result, 0, 1)
    boxes = make_boxes(positions, charged)
    table = placement_table()
    placed_x = sum((jnp.einsum('XYZefg,ej->XYZjfg', jnp.roll(boxes, which - 1, axis=0), table[:, :, which], precision=HIGHEST) for which in range(3)))
    placed_y = sum((jnp.einsum('XYZjfg,fl->XYZjlg', jnp.roll(placed_x, which - 1, axis=1), table[:, :, which], precision=HIGHEST) for which in range(3)))
    placed_z = sum((jnp.einsum('XYZjlg,gm->XYZjlm', jnp.roll(placed_y, which - 1, axis=2), table[:, :, which], precision=HIGHEST) for which in range(3)))
    grid_x, grid_y, grid_z = (POINTS * CELLS_X, POINTS * CELLS_Y, POINTS * CELLS_Z)
    charge_grid = placed_z.transpose(0, 3, 1, 4, 2, 5).reshape(grid_x, grid_y, grid_z)
    fine = jnp.zeros(charge_grid.shape, jnp.float32)
    for width, weight in zip(FINE_WIDTHS, FINE_WEIGHTS):
        taps = taps_for(width)
        section = charge_grid
        for axis_num in range(3):
            section = sum((taps[step + REACH] * jnp.roll(section, -step, axis=axis_num) for step in range(-REACH, REACH + 1)))
        fine = fine + weight * section
    coarse_charge = charge_grid.reshape(grid_x // 2, 2, grid_y // 2, 2, grid_z // 2, 2).sum(axis=(1, 3, 5)) * 0.125
    coarse = jnp.zeros(coarse_charge.shape, jnp.float32)
    for fraction, weight in zip(COARSE_FRACTIONS, COARSE_WEIGHTS):
        matrix_x = gauss_matrix(grid_x // 2, grid_x // 2 / fraction, 0, grid_x // 2)
        matrix_y = gauss_matrix(grid_y // 2, grid_y // 2 / fraction, 0, grid_y // 2)
        matrix_z = gauss_matrix(grid_z // 2, grid_z // 2 / fraction, 0, grid_z // 2)
        section = jnp.einsum('ri,ijk->rjk', matrix_x, coarse_charge, precision=HIGHEST)
        section = jnp.einsum('sj,rjk->rsk', matrix_y, section, precision=HIGHEST)
        section = jnp.einsum('tk,rsk->rst', matrix_z, section, precision=HIGHEST)
        coarse = coarse + weight * section
    lifted = jnp.repeat(jnp.repeat(jnp.repeat(coarse, 2, axis=0), 2, axis=1), 2, axis=2)
    potential = fine + lifted
    pick_x = pick_table(CELLS_X, grid_x, -1, grid_x)
    pick_y = pick_table(CELLS_Y, grid_y, -1, grid_y)
    pick_z = pick_table(CELLS_Z, grid_z, -1, grid_z)
    point_box = jnp.einsum('Xei,ijk->Xejk', pick_x, potential, precision=HIGHEST)
    point_box = jnp.einsum('Yfj,Xejk->XYefk', pick_y, point_box, precision=HIGHEST)
    point_box = jnp.einsum('Zgk,XYefk->XYZefg', pick_z, point_box, precision=HIGHEST)
    return short + long_forces(positions, charged, point_box)
```

```python
import functools
import math

import jax
import jax.numpy as jnp
import numpy as np
from jax import lax
from jax.experimental import pallas as pl
from jax.experimental.pallas import tpu as pltpu
from jax.sharding import PartitionSpec as P

F32 = jnp.float32
BF16 = jnp.bfloat16
MESH = pl.DeviceIdType.MESH
HIGHEST = lax.Precision.HIGHEST
SPLIT_RATE = 0.8
SOFT_SQUARE = 0.0625
FINE_WIDTHS = (1.0, 2.0)
FINE_WEIGHTS = (2.0, 0.5)
COARSE_FRACTIONS = (8.0, 4.0)
COARSE_WEIGHTS = (4.0, 2.0)
REACH = 4
SIDES = [(dx, dy) for dx in (-1, 0, 1) for dy in (-1, 0, 1)]
NEAR = [side for side in SIDES if side != (0, 0)]
LAPS = (1, 2, 3, 4, -1, -2, -3, -4)
CELLS = 12


def two_parts(table):
    table = np.asarray(table, np.float32)
    high = table.astype(jnp.bfloat16)
    low = (table - high.astype(np.float32)).astype(jnp.bfloat16)
    return high, low


def constants(sub_size):
    place = np.zeros((4, 2, 64, 128), np.float32)
    for x in range(2):
        for y in range(2):
            for e in range(7):
                for f in range(7):
                    place[2 * x + y, :, 8 * e + f, 11 * (4 * x + e) + 4 * y + f] = 1.0
    place = place.reshape(512, 128).astype(jnp.bfloat16)
    tap = np.arange(11)
    spread = np.zeros((2, 128, 9, 128), np.float32)
    for number, (width, weight) in enumerate(zip(FINE_WIDTHS, FINE_WEIGHTS)):
        for place_num, (dx, dy) in enumerate(SIDES):
            per_axis = []
            for step in (dx, dy):
                dist = np.abs(tap[None, :] + 8 * step - tap[:, None]).astype(np.float64)
                per_axis.append(np.where(dist <= REACH, np.exp(-dist * dist / (2 * width * width)), 0.0))
            both = weight * np.kron(per_axis[0], per_axis[1])
            spread[number, :121, place_num, :121] = both
    spread = two_parts(spread.reshape(256, 9 * 128))
    ring = np.zeros((2, 16, 16), np.float32)
    for number, width in enumerate(FINE_WIDTHS):
        dist = np.abs(np.arange(12)[:, None] - np.arange(12)[None, :])
        dist = np.minimum(dist, 12 - dist).astype(np.float64)
        ring[number, :12, :12] = np.where(dist <= REACH, np.exp(-dist * dist / (2 * width * width)), 0.0)
    ring = ring.reshape(32, 16)
    select = np.zeros((2, 12, 8, 128), np.float32)
    for y in range(2):
        for x in range(11):
            for f in range(7):
                select[y, x, f, 11 * x + 4 * y + f] = 1.0
    select = select.reshape(192, 128).astype(jnp.bfloat16)
    total_y = 4 * sub_size
    coarse = np.zeros((2, 8, 8, sub_size, 16, 8), np.float32)
    for number, (fraction, weight) in enumerate(zip(COARSE_FRACTIONS, COARSE_WEIGHTS)):
        dist = np.abs(np.arange(6)[:, None] - np.arange(6)[None, :])
        dist = np.minimum(dist, 6 - dist).astype(np.float64)
        along_z = np.exp(-dist * dist / (2 * (6 / fraction) ** 2))
        for step in range(sub_size):
            dist = np.mod(4 * step + np.arange(6)[None, :] - np.arange(6)[:, None], total_y)
            dist = np.minimum(dist, total_y - dist).astype(np.float64)
            along_y = np.exp(-dist * dist / (2 * (total_y / fraction) ** 2))
            both = 0.125 * weight * along_z[:, None, :, None] * along_y[None, :, None, :]
            coarse[number, :6, :6, step, :6, :6] = both
    coarse = two_parts(coarse.reshape(128, sub_size * 128))
    return place, spread, ring, select, coarse


def halves(value):
    high = value.astype(BF16).astype(F32)
    return high, value - high


def thirds(value):
    high, rest = halves(value)
    middle, low = halves(rest)
    return high, middle, low


def dot(left, right):
    return lax.dot_general(left, right, (((1,), (0,)), ((), ())), preferred_element_type=F32)


def dot_rows(left, right):
    return lax.dot_general(left, right, (((1,), (1,)), ((), ())), preferred_element_type=F32)


def spline(shifted):
    size = jnp.abs(shifted)
    outer = jnp.maximum(2.0 - size, 0.0)
    inner = jnp.maximum(1.0 - size, 0.0)
    return outer * outer * outer * (1.0 / 6.0) - inner * inner * inner * (2.0 / 3.0)


def spline_slope(shifted):
    size = jnp.abs(shifted)
    outer = jnp.maximum(2.0 - size, 0.0)
    inner = jnp.maximum(1.0 - size, 0.0)
    slope = 2.0 * inner * inner - 0.5 * outer * outer
    return jnp.where(shifted < 0.0, -slope, slope)


def wrapped(shifted):
    return jnp.where(shifted > 6.0, shifted - 12.0, jnp.where(shifted < -6.0, shifted + 12.0, shifted))


def row_iota(rows, lanes=128):
    return lax.broadcasted_iota(jnp.int32, (rows, lanes), 0)


def kernel(
    spaces, subs,
    pos_ref, charge_ref, count_ref, place_hbm, wide_hi_hbm, wide_lo_hbm, ring_ref, select_hbm, far_hi_hbm, far_lo_hbm,
    out_ref,
    place_ref, wide_hi, wide_lo, select_ref, far_hi, far_lo,
    ext, lap_buf, plane_out, plane_buf, fine_out, fine_buf,
    fine_sum, by_ref, wz_ref, pair_hi, pair_lo, vx_ref, left_ref, right_ref, mom_ref, force_ref,
    const_sem, halo_send, halo_recv, lap_send, lap_recv, relay_send, relay_recv, fine_send, fine_recv, plane_send, plane_recv,
):
    laps = spaces // 4
    space = lax.axis_index("space")
    sub = lax.axis_index("sub")
    outer_x = space // (2 * laps)
    lap = (space // 2) % laps
    core = space % 2

    loads = [
        pltpu.make_async_copy(src, dst, const_sem.at[num])
        for num, (src, dst) in enumerate((
            (place_hbm, place_ref), (wide_hi_hbm, wide_hi), (wide_lo_hbm, wide_lo),
            (select_hbm, select_ref), (far_hi_hbm, far_hi), (far_lo_hbm, far_lo),
        ))
    ]
    for load in loads:
        load.start()

    def near_id(side):
        return {"space": (space + side[0] + spaces) % spaces, "sub": (sub + side[1] + subs) % subs}

    def lap_id(step):
        return {"space": outer_x * 2 * laps + ((lap + step + laps) % laps) * 2 + core, "sub": sub}

    def plane_id(member, step):
        return {
            "space": ((outer_x + member // 2) % 2) * 2 * laps + lap * 2 + (core + member % 2) % 2,
            "sub": (sub + step) % subs,
        }

    members = [(member, step) for member in range(4) for step in range(subs) if (member, step) != (0, 0)]
    barrier = pltpu.get_barrier_semaphore()
    for side in NEAR:
        pl.semaphore_signal(barrier, inc=1, device_id=near_id(side), device_id_type=MESH)
    for step in LAPS:
        pl.semaphore_signal(barrier, inc=1, device_id=lap_id(step), device_id_type=MESH)
    for member, step in members:
        pl.semaphore_signal(barrier, inc=1, device_id=plane_id(member, step), device_id_type=MESH)

    lane = lax.broadcasted_iota(jnp.int32, (1, 128), 1)
    for x in range(2):
        for y in range(2):
            for z in range(3):
                lanes = pl.ds(128 * z, 128)
                for k in range(3):
                    ext[1 + x, 1 + y, pl.ds(k, 1), lanes] = pos_ref[k, x, y, pl.ds(z, 1), :]
                live = lane < count_ref[x, y, z]
                ext[1 + x, 1 + y, pl.ds(3, 1), lanes] = jnp.where(live, charge_ref[x, y, pl.ds(z, 1), :], 0.0)
            ext[1 + x, 1 + y, pl.ds(4, 4), :] = jnp.zeros((4, 384), F32)

    def cell_rows(cell):
        x, y, z = cell // 6, (cell // 3) % 2, cell % 3
        block = ext[1 + x, 1 + y, :, pl.ds(pl.multiple_of(z * 128, 128), 128)]
        return x, y, z, block

    row8 = row_iota(8).astype(F32)
    row16 = row_iota(16).astype(F32)

    def coarse_step(cell, total):
        x, y, z, block = cell_rows(cell)
        at_x = 4.0 * block[0:1] + (4 * x + 2).astype(F32) - 2.0 * row8
        at_y = 4.0 * block[1:2] + (4 * y + 2).astype(F32) - 2.0 * row8
        at_z = 4.0 * block[2:3] + (4 * z).astype(F32) - 2.0 * row8
        charge = block[3:4]
        near_z, next_z = wrapped(at_z), wrapped(at_z - 1.0)
        some = row8 < 6.0
        vx = spline(at_x) + spline(at_x - 1.0)
        vy = spline(at_y) + spline(at_y - 1.0)
        vz = jnp.where(some, spline(near_z) + spline(next_z), 0.0)
        sx = spline_slope(at_x) + spline_slope(at_x - 1.0)
        sy = spline_slope(at_y) + spline_slope(at_y - 1.0)
        sz = jnp.where(some, spline_slope(near_z) + spline_slope(next_z), 0.0)
        vz_charge = vz * charge
        pad = jnp.zeros((16, 128), F32)
        product = jnp.concatenate([vz_charge[k : k + 1] * vy for k in range(6)], axis=0)
        high, low = halves(product)
        right = jnp.concatenate([high, pad, high, pad, low, pad, low, pad], axis=0).astype(BF16)
        left = jnp.concatenate(halves(vx), axis=0).astype(BF16)
        lanes = pl.ds(pl.multiple_of(cell * 384, 128), 384)
        tables = jnp.concatenate(
            [
                jnp.concatenate([one[k : k + 1] * other for k in range(6)], axis=0)
                for one, other in ((vz, vy), (vz, sy), (sz, vy))
            ],
            axis=1,
        )
        high, low = halves(tables)
        pair_hi[:, lanes] = high.astype(BF16)
        pair_lo[:, lanes] = low.astype(BF16)
        vx_ref[:, lanes] = jnp.concatenate([sx, vx, vx], axis=1)
        return total + dot_rows(left, right)

    total = lax.fori_loop(0, CELLS, coarse_step, jnp.zeros((16, 256), F32))
    total = total[0:8] + total[8:16]
    lap_buf[0] = total[:, 0:128] + total[:, 128:256]

    pl.semaphore_wait(barrier, len(NEAR) + len(LAPS) + len(members))

    lap_copies = []
    for num, step in enumerate(LAPS):
        copy = pltpu.make_async_remote_copy(
            src_ref=lap_buf.at[0], dst_ref=lap_buf.at[(-step) % laps], send_sem=lap_send.at[num], recv_sem=lap_recv.at[num],
            device_id=lap_id(step), device_id_type=MESH,
        )
        copy.start()
        lap_copies.append(copy)

    def piece(step, far):
        if step == 0:
            return pl.ds(1, 2)
        if far:
            return pl.ds(0 if step > 0 else 3, 1)
        return pl.ds(2 if step > 0 else 1, 1)

    halo_copies = []
    for num, side in enumerate(NEAR):
        copy = pltpu.make_async_remote_copy(
            src_ref=ext.at[piece(side[0], False), piece(side[1], False)],
            dst_ref=ext.at[piece(side[0], True), piece(side[1], True)],
            send_sem=halo_send.at[num], recv_sem=halo_recv.at[num], device_id=near_id(side), device_id_type=MESH,
        )
        copy.start()
        halo_copies.append(copy)

    fine_sum[...] = jnp.zeros_like(fine_sum)

    def fine_step(cell, carry):
        x, y, z, block = cell_rows(cell)
        at_x = 4.0 * block[0:1] - (row8 - 1.0)
        at_y = 4.0 * block[1:2] - (row8 - 1.0)
        at_z = wrapped(4.0 * block[2:3] + (4 * z).astype(F32) - row16)
        bx, by = spline(at_x), spline(at_y)
        bz = jnp.where(row16 < 12.0, spline(at_z), 0.0)
        sz = jnp.where(row16 < 12.0, spline_slope(at_z), 0.0)
        by_ref[cell] = jnp.concatenate([bx, spline_slope(at_x), by, spline_slope(at_y)], axis=0)
        bx_charge = bx * block[3:4]
        product = jnp.concatenate([bx_charge[e : e + 1] * by for e in range(7)] + [jnp.zeros((8, 128), F32)], axis=0)
        right = jnp.concatenate(halves(product), axis=0).astype(BF16)
        high, low = halves(jnp.concatenate([bz, sz], axis=1))
        left = jnp.concatenate([high[:, 0:128], low[:, 0:128]], axis=0).astype(BF16)
        wz_ref[cell] = jnp.concatenate([high, high, high, low, low, low], axis=0).astype(BF16)
        fine_sum[cell // 3] += dot_rows(left, right)
        return carry

    lax.fori_loop(0, CELLS, fine_step, 0)
    for load in loads:
        load.wait()
    boxes = jnp.concatenate([fine_sum[num, 0:16] + fine_sum[num, 16:32] for num in range(4)], axis=1)
    spots = dot(jnp.concatenate(thirds(boxes), axis=0).astype(BF16), place_ref[...])
    spots = spots[0:16] + spots[16:32] + spots[32:48]
    rings = lax.dot_general(
        ring_ref[...], spots, (((1,), (0,)), ((), ())), precision=HIGHEST, preferred_element_type=F32
    )
    rings = jnp.concatenate([rings[0:16], rings[16:32]], axis=1)
    parts = jnp.concatenate(halves(rings), axis=0).astype(BF16)
    fine_all = dot(parts, wide_hi[...])
    fine_all = fine_all[0:16] + fine_all[16:32] + dot(parts[0:16], wide_lo[...])
    for num in range(9):
        fine_out[num] = fine_all[:, 128 * num : 128 * (num + 1)]
    fine_copies = []
    for num, side in enumerate(NEAR):
        copy = pltpu.make_async_remote_copy(
            src_ref=fine_out.at[SIDES.index(side)], dst_ref=fine_buf.at[num],
            send_sem=fine_send.at[num], recv_sem=fine_recv.at[num], device_id=near_id(side), device_id_type=MESH,
        )
        copy.start()
        fine_copies.append(copy)

    for copy in lap_copies:
        copy.wait_recv()
    relays = []
    for num, (src, dst, step) in enumerate((
        (pl.ds(1, 4), pl.ds(5, 4), -4),
        (pl.ds(laps - 3, 3), pl.ds(laps - 7, 3), 4),
    )):
        copy = pltpu.make_async_remote_copy(
            src_ref=lap_buf.at[src], dst_ref=lap_buf.at[dst], send_sem=relay_send.at[num], recv_sem=relay_recv.at[num],
            device_id=lap_id(step), device_id_type=MESH,
        )
        copy.start()
        relays.append(copy)

    for copy in halo_copies:
        copy.wait_recv()

    row_w = row_iota(8, 640)
    slot_w = lax.broadcasted_iota(jnp.int32, (8, 640), 1) // 128

    def column_step(column, carry):
        x, y = column // 4, column % 4
        block = ext[x, y]
        block = jnp.concatenate([block[:, 256:384], block, block[:, 0:128]], axis=1)
        shift = jnp.where(
            row_w == 0, (x - 2).astype(F32), jnp.where(row_w == 1, (y - 2).astype(F32), slot_w.astype(F32) - 2.5)
        )
        coords = jnp.where(row_w < 3, SPLIT_RATE * (block + shift), 0.0)
        square = jnp.sum(coords * coords, axis=0, keepdims=True) + SPLIT_RATE * SPLIT_RATE * SOFT_SQUARE
        ones = jnp.where(row_w == 3, 1.0, 0.0)
        p1, p2, p3 = thirds(coords)
        s1, s2, s3 = thirds(square)

        def with_square(part, square_part):
            return jnp.where(row_w == 4, square_part, part + ones)

        right_ref[column] = jnp.concatenate(
            [with_square(p1, s1), with_square(p2, s2), with_square(p1, s3), p3, p2, p1], axis=0
        ).astype(BF16)
        moments = (coords + ones) * block[3:4]
        m1, m2, m3 = thirds(moments)
        mom_ref[column] = jnp.concatenate([m1, m2, m3, jnp.zeros_like(m1)], axis=0).astype(BF16)
        return carry

    lax.fori_loop(0, 16, column_step, 0)

    row_c = row_iota(8)

    def left_step(cell, carry):
        x, y, z, block = cell_rows(cell)
        shift = jnp.where(
            row_c == 0, (x - 1).astype(F32), jnp.where(row_c == 1, (y - 1).astype(F32), z.astype(F32) - 1.5)
        )
        coords = jnp.where(row_c < 3, SPLIT_RATE * (block + shift), 0.0)
        square = jnp.sum(coords * coords, axis=0, keepdims=True)
        ones = jnp.where(row_c == 4, 1.0, 0.0)
        p1, p2, p3 = thirds(-2.0 * coords)
        s1, s2, s3 = thirds(square)

        def with_square(part, square_part):
            return jnp.where(row_c == 3, square_part, part + ones)

        stacked = jnp.concatenate(
            [with_square(p1, s1), with_square(p1, s2), with_square(p2, s3), p1, p2, p3, jnp.zeros((80, 128), F32)], axis=0
        )
        left_ref[cell] = jnp.transpose(stacked).astype(BF16)
        return carry

    lax.fori_loop(0, CELLS, left_step, 0)

    def pair_step(cell, carry):
        x, y, z, block = cell_rows(cell)
        left = left_ref[cell][:, 0:48]

        def column_pairs(side, moments):
            column = (x + side // 3) * 4 + y + side % 3
            for slot in range(3):
                lanes = pl.ds(pl.multiple_of((z + slot) * 128, 128), 128)
                square = dot(left, right_ref[column, :, lanes])
                inverse = lax.rsqrt(square)
                far = 1.0 - lax.erf(square * inverse)
                bell = jnp.exp2(square * (-math.log2(math.e)))
                factor = (inverse * inverse) * (far * inverse + (2.0 / math.sqrt(math.pi)) * bell)
                high = factor.astype(BF16)
                low = (factor - high.astype(F32)).astype(BF16)
                other = mom_ref[column, :, lanes]
                moments = moments + dot_rows(
                    jnp.concatenate([high, low], axis=1), jnp.concatenate([other, other], axis=1)
                )
            return moments

        moments = lax.fori_loop(0, 9, column_pairs, jnp.zeros((128, 32), F32))
        moments = jnp.transpose(moments)
        moments = moments[0:8] + moments[8:16] + moments[16:24]
        shift = jnp.where(
            row_c == 0, (x - 1).astype(F32), jnp.where(row_c == 1, (y - 1).astype(F32), z.astype(F32) - 1.5)
        )
        coords = SPLIT_RATE * (block + shift)
        force_ref[cell] = (SPLIT_RATE * SPLIT_RATE) * block[3:4] * (coords * moments[3:4] - moments)
        return carry

    lax.fori_loop(0, 4, pair_step, 0)

    for copy in relays:
        copy.wait_recv()
    rows = lax.broadcasted_iota(jnp.int32, (64, 128), 0)
    cols = lax.broadcasted_iota(jnp.int32, (64, 128), 1)
    member = (rows // 8) % 4
    to_space = ((outer_x + member // 2) % 2) * 2 * laps + lap * 2 + (core + member % 2) % 2
    from_space = outer_x * 2 * laps + ((lap + cols // 8) % laps) * 2 + core
    total_x = 4 * spaces
    dist = (4 * (to_space - from_space) + rows % 8 - cols % 8 + 2 * total_x) % total_x
    dist = jnp.minimum(dist, total_x - dist).astype(F32)
    wide = [2.0 * (total_x / fraction) ** 2 for fraction in COARSE_FRACTIONS]
    bells = jnp.exp(-dist * dist * jnp.where(rows < 32, 1.0 / wide[0], 1.0 / wide[1]))
    gathered = jnp.concatenate([lap_buf[num] for num in range(laps)], axis=0)
    along_x = lax.dot_general(
        bells, gathered, (((1,), (0,)), ((), ())), precision=HIGHEST, preferred_element_type=F32
    )
    along_x = jnp.where(lax.broadcasted_iota(jnp.int32, (32, 128), 1) < 64, along_x[0:32], along_x[32:64])
    parts = jnp.concatenate(halves(along_x), axis=0).astype(BF16)
    shares = dot(parts, far_hi[...])
    shares = shares[0:32] + shares[32:64] + dot(parts[0:32], far_lo[...])
    for member_num in range(4):
        for step in range(subs):
            plane_out[member_num * subs + step] = shares[8 * member_num : 8 * member_num + 8, 128 * step : 128 * (step + 1)]
    plane_copies = []
    for member_num, step in members:
        num = member_num * subs + step
        copy = pltpu.make_async_remote_copy(
            src_ref=plane_out.at[num], dst_ref=plane_buf.at[num], send_sem=plane_send.at[num], recv_sem=plane_recv.at[num],
            device_id=plane_id(member_num, step), device_id_type=MESH,
        )
        copy.start()
        plane_copies.append(copy)

    lax.fori_loop(4, CELLS, pair_step, 0)

    for copy in fine_copies:
        copy.wait_recv()
    fine = fine_out[SIDES.index((0, 0))]
    for num in range(8):
        fine = fine + fine_buf[num]
    pieces = thirds(fine)
    points = dot_rows(select_ref[...], jnp.concatenate(pieces + pieces, axis=0).astype(BF16)).astype(BF16)
    fine_sum_rows = points

    def interpolate(cell, x, y):
        start = 96 * y + 32 * x
        spread = dot(fine_sum_rows[start : start + 64], wz_ref[cell])
        tables = by_ref[cell]
        u1 = jnp.zeros((8, 128), F32)
        u2 = jnp.zeros((8, 128), F32)
        u3 = jnp.zeros((8, 128), F32)
        for e in range(7):
            at = spread[8 * e : 8 * e + 8]
            u1 = u1 + tables[8 + e : 9 + e] * at[:, 0:128]
            u2 = u2 + tables[e : e + 1] * at[:, 0:128]
            u3 = u3 + tables[e : e + 1] * at[:, 128:256]
        by, sy = tables[16:24], tables[24:32]
        return [jnp.sum(one * other, axis=0, keepdims=True) for one, other in ((by, u1), (sy, u2), (by, u3))]

    fine_forces = [interpolate(cell, cell // 6, (cell // 3) % 2) for cell in range(CELLS)]

    for copy in plane_copies:
        copy.wait_recv()
    window = plane_out[0]
    for member_num, step in members:
        window = window + plane_buf[member_num * subs + step]
    parts = jnp.concatenate(halves(window), axis=0).astype(BF16)[:, 0:48]
    for cell in range(CELLS):
        x, y, z = cell // 6, (cell // 3) % 2, cell % 3
        lanes = pl.ds(384 * cell, 384)
        spread = dot(parts, pair_hi[:, lanes])
        spread = spread[0:8] + spread[8:16] + dot(parts, pair_lo[:, lanes])[0:8]
        spread = jnp.sum(spread * vx_ref[:, lanes], axis=0, keepdims=True)
        charge = ext[1 + x, 1 + y, pl.ds(3, 1), pl.ds(128 * z, 128)]
        for k in range(3):
            far = fine_forces[cell][k] + spread[:, 128 * k : 128 * (k + 1)]
            out_ref[k, x, y, pl.ds(z, 1), :] = force_ref[cell, pl.ds(k, 1), :] - 4.0 * charge * far

    for copy in lap_copies + halo_copies + fine_copies + relays + plane_copies:
        copy.wait_send()


def solution(mesh):
    spaces, subs = mesh.shape["space"], mesh.shape["sub"]
    laps = spaces // 4
    place, spread, ring, select, coarse = constants(subs)

    def body(positions, charges, counts):
        any_spec = pl.BlockSpec(memory_space=pl.ANY)
        vmem_spec = pl.BlockSpec(memory_space=pltpu.VMEM)
        planes = 4 * subs
        return pl.pallas_call(
            functools.partial(kernel, spaces, subs),
            out_shape=jax.ShapeDtypeStruct(positions.shape, F32),
            in_specs=[vmem_spec, vmem_spec, pl.BlockSpec(memory_space=pltpu.SMEM), any_spec, any_spec, any_spec, vmem_spec, any_spec, any_spec, any_spec],
            out_specs=vmem_spec,
            scratch_shapes=[
                pltpu.VMEM((512, 128), BF16),
                pltpu.VMEM((256, 1152), BF16),
                pltpu.VMEM((256, 1152), BF16),
                pltpu.VMEM((192, 128), BF16),
                pltpu.VMEM((128, 128 * subs), BF16),
                pltpu.VMEM((128, 128 * subs), BF16),
                pltpu.VMEM((4, 4, 8, 384), F32),
                pltpu.VMEM((laps, 8, 128), F32),
                pltpu.VMEM((planes, 8, 128), F32),
                pltpu.VMEM((planes, 8, 128), F32),
                pltpu.VMEM((9, 16, 128), F32),
                pltpu.VMEM((8, 16, 128), F32),
                pltpu.VMEM((4, 32, 128), F32),
                pltpu.VMEM((CELLS, 32, 128), F32),
                pltpu.VMEM((CELLS, 96, 256), BF16),
                pltpu.VMEM((48, CELLS * 384), BF16),
                pltpu.VMEM((48, CELLS * 384), BF16),
                pltpu.VMEM((8, CELLS * 384), F32),
                pltpu.VMEM((CELLS, 128, 128), BF16),
                pltpu.VMEM((16, 48, 640), BF16),
                pltpu.VMEM((16, 32, 640), BF16),
                pltpu.VMEM((CELLS, 8, 128), F32),
                pltpu.SemaphoreType.DMA((6,)),
                pltpu.SemaphoreType.DMA((8,)),
                pltpu.SemaphoreType.DMA((8,)),
                pltpu.SemaphoreType.DMA((8,)),
                pltpu.SemaphoreType.DMA((8,)),
                pltpu.SemaphoreType.DMA((2,)),
                pltpu.SemaphoreType.DMA((2,)),
                pltpu.SemaphoreType.DMA((8,)),
                pltpu.SemaphoreType.DMA((8,)),
                pltpu.SemaphoreType.DMA((planes,)),
                pltpu.SemaphoreType.DMA((planes,)),
            ],
            compiler_params=pltpu.CompilerParams(collective_id=0, has_side_effects=True),
        )(
            positions, charges, counts,
            jnp.asarray(place), jnp.asarray(spread[0]), jnp.asarray(spread[1]), jnp.asarray(ring), jnp.asarray(select),
            jnp.asarray(coarse[0]), jnp.asarray(coarse[1]),
        )

    in_specs = (
        P(None, "space", "sub", None, None),
        P("space", "sub", None, None),
        P("space", "sub", None),
    )
    out_specs = P(None, "space", "sub", None, None)
    return jax.shard_map(body, mesh=mesh, in_specs=in_specs, out_specs=out_specs, check_vma=False)
```

```python
import functools
import math

import jax
import jax.numpy as jnp
import numpy as np
from jax import lax
from jax.experimental import pallas as pl
from jax.experimental.pallas import tpu as pltpu
from jax.sharding import PartitionSpec as P

F32 = jnp.float32
BF16 = jnp.bfloat16
MESH = pl.DeviceIdType.MESH
HIGHEST = lax.Precision.HIGHEST
SPLIT_RATE = 0.8
SOFT_SQUARE = 0.0625
FINE_WIDTHS = (1.0, 2.0)
FINE_WEIGHTS = (2.0, 0.5)
COARSE_FRACTIONS = (8.0, 4.0)
COARSE_WEIGHTS = (4.0, 2.0)
REACH = 4
SIDES = [(dx, dy) for dx in (-1, 0, 1) for dy in (-1, 0, 1)]
NEAR = [side for side in SIDES if side != (0, 0)]
LAPS = (1, 2, 3, 4, -1, -2, -3, -4)
CELLS = 12


def two_parts(table):
    table = np.asarray(table, np.float32)
    high = table.astype(jnp.bfloat16)
    low = (table - high.astype(np.float32)).astype(jnp.bfloat16)
    return high, low


def constants(sub_size):
    place = np.zeros((4, 2, 64, 128), np.float32)
    for x in range(2):
        for y in range(2):
            for e in range(7):
                for f in range(7):
                    place[2 * x + y, :, 8 * e + f, 11 * (4 * x + e) + 4 * y + f] = 1.0
    place = place.reshape(512, 128).astype(jnp.bfloat16)
    tap = np.arange(11)
    spread = np.zeros((2, 128, 9, 128), np.float32)
    for number, (width, weight) in enumerate(zip(FINE_WIDTHS, FINE_WEIGHTS)):
        for place_num, (dx, dy) in enumerate(SIDES):
            per_axis = []
            for step in (dx, dy):
                dist = np.abs(tap[None, :] + 8 * step - tap[:, None]).astype(np.float64)
                per_axis.append(np.where(dist <= REACH, np.exp(-dist * dist / (2 * width * width)), 0.0))
            both = weight * np.kron(per_axis[0], per_axis[1])
            spread[number, :121, place_num, :121] = both
    spread = two_parts(spread.reshape(256, 9 * 128))
    ring = np.zeros((2, 16, 16), np.float32)
    for number, width in enumerate(FINE_WIDTHS):
        dist = np.abs(np.arange(12)[:, None] - np.arange(12)[None, :])
        dist = np.minimum(dist, 12 - dist).astype(np.float64)
        ring[number, :12, :12] = np.where(dist <= REACH, np.exp(-dist * dist / (2 * width * width)), 0.0)
    ring = ring.reshape(32, 16)
    select = np.zeros((2, 12, 8, 128), np.float32)
    for y in range(2):
        for x in range(11):
            for f in range(7):
                select[y, x, f, 11 * x + 4 * y + f] = 1.0
    select = select.reshape(192, 128).astype(jnp.bfloat16)
    total_y = 4 * sub_size
    coarse = np.zeros((2, 8, 8, sub_size, 16, 8), np.float32)
    for number, (fraction, weight) in enumerate(zip(COARSE_FRACTIONS, COARSE_WEIGHTS)):
        dist = np.abs(np.arange(6)[:, None] - np.arange(6)[None, :])
        dist = np.minimum(dist, 6 - dist).astype(np.float64)
        along_z = np.exp(-dist * dist / (2 * (6 / fraction) ** 2))
        for step in range(sub_size):
            dist = np.mod(4 * step + np.arange(6)[None, :] - np.arange(6)[:, None], total_y)
            dist = np.minimum(dist, total_y - dist).astype(np.float64)
            along_y = np.exp(-dist * dist / (2 * (total_y / fraction) ** 2))
            both = 0.125 * weight * along_z[:, None, :, None] * along_y[None, :, None, :]
            coarse[number, :6, :6, step, :6, :6] = both
    coarse = two_parts(coarse.reshape(128, sub_size * 128))
    return place, spread, ring, select, coarse


def halves(value):
    high = value.astype(BF16).astype(F32)
    return high, value - high


def thirds(value):
    high, rest = halves(value)
    middle, low = halves(rest)
    return high, middle, low


def dot(left, right):
    return lax.dot_general(left, right, (((1,), (0,)), ((), ())), preferred_element_type=F32)


def dot_rows(left, right):
    return lax.dot_general(left, right, (((1,), (1,)), ((), ())), preferred_element_type=F32)


def spline(shifted):
    size = jnp.abs(shifted)
    outer = jnp.maximum(2.0 - size, 0.0)
    inner = jnp.maximum(1.0 - size, 0.0)
    return outer * outer * outer * (1.0 / 6.0) - inner * inner * inner * (2.0 / 3.0)


def spline_slope(shifted):
    size = jnp.abs(shifted)
    outer = jnp.maximum(2.0 - size, 0.0)
    inner = jnp.maximum(1.0 - size, 0.0)
    slope = 2.0 * inner * inner - 0.5 * outer * outer
    return jnp.where(shifted < 0.0, -slope, slope)


def wrapped(shifted):
    return jnp.where(shifted > 6.0, shifted - 12.0, jnp.where(shifted < -6.0, shifted + 12.0, shifted))


def grouped(size, step, start, cells=CELLS):
    def group(number, carry):
        for num in range(size):
            carry = step(number * size + num, carry)
        return carry

    return lax.fori_loop(0, cells // size, group, start)


def row_iota(rows, lanes=128):
    return lax.broadcasted_iota(jnp.int32, (rows, lanes), 0)


def kernel(
    spaces, subs,
    pos_ref, charge_ref, count_ref, place_hbm, wide_hi_hbm, wide_lo_hbm, ring_ref, select_hbm, far_hi_hbm, far_lo_hbm,
    out_ref,
    place_ref, wide_hi, wide_lo, select_ref, far_hi, far_lo,
    ext, lap_buf, plane_out, plane_buf, fine_out, fine_buf,
    fine_sum, by_ref, wz_ref, pair_hi, pair_lo, vx_ref, left_ref, right_ref, mom_ref, force_ref,
    const_sem, halo_send, halo_recv, lap_send, lap_recv, relay_send, relay_recv, fine_send, fine_recv, plane_send, plane_recv,
):
    laps = spaces // 4
    space = lax.axis_index("space")
    sub = lax.axis_index("sub")
    outer_x = space // (2 * laps)
    lap = (space // 2) % laps
    core = space % 2

    loads = [
        pltpu.make_async_copy(src, dst, const_sem.at[num])
        for num, (src, dst) in enumerate((
            (place_hbm, place_ref), (wide_hi_hbm, wide_hi), (wide_lo_hbm, wide_lo),
            (select_hbm, select_ref), (far_hi_hbm, far_hi), (far_lo_hbm, far_lo),
        ))
    ]
    for load in loads:
        load.start()

    def near_id(side):
        return {"space": (space + side[0] + spaces) % spaces, "sub": (sub + side[1] + subs) % subs}

    def lap_id(step):
        return {"space": outer_x * 2 * laps + ((lap + step + laps) % laps) * 2 + core, "sub": sub}

    def plane_id(member, step):
        return {
            "space": ((outer_x + member // 2) % 2) * 2 * laps + lap * 2 + (core + member % 2) % 2,
            "sub": (sub + step) % subs,
        }

    members = [(member, step) for member in range(4) for step in range(subs) if (member, step) != (0, 0)]
    barrier = pltpu.get_barrier_semaphore()
    for side in NEAR:
        pl.semaphore_signal(barrier, inc=1, device_id=near_id(side), device_id_type=MESH)
    for step in LAPS:
        pl.semaphore_signal(barrier, inc=1, device_id=lap_id(step), device_id_type=MESH)
    for member, step in members:
        pl.semaphore_signal(barrier, inc=1, device_id=plane_id(member, step), device_id_type=MESH)

    lane = lax.broadcasted_iota(jnp.int32, (1, 128), 1)
    for x in range(2):
        for y in range(2):
            for z in range(3):
                lanes = pl.ds(128 * z, 128)
                for k in range(3):
                    ext[1 + x, 1 + y, pl.ds(k, 1), lanes] = pos_ref[k, x, z, pl.ds(y, 1), :]
                live = lane < count_ref[x, y, z]
                ext[1 + x, 1 + y, pl.ds(3, 1), lanes] = jnp.where(live, charge_ref[x, z, pl.ds(y, 1), :], 0.0)
            ext[1 + x, 1 + y, pl.ds(4, 4), :] = jnp.zeros((4, 384), F32)

    def cell_rows(cell):
        x, y, z = cell // 6, (cell // 3) % 2, cell % 3
        block = ext[1 + x, 1 + y, :, pl.ds(pl.multiple_of(z * 128, 128), 128)]
        return x, y, z, block

    row8 = row_iota(8).astype(F32)
    row16 = row_iota(16).astype(F32)

    def coarse_step(cell, total):
        x, y, z, block = cell_rows(cell)
        at_x = 4.0 * block[0:1] + (4 * x + 2).astype(F32) - 2.0 * row8
        at_y = 4.0 * block[1:2] + (4 * y + 2).astype(F32) - 2.0 * row8
        at_z = 4.0 * block[2:3] + (4 * z).astype(F32) - 2.0 * row8
        charge = block[3:4]
        near_z, next_z = wrapped(at_z), wrapped(at_z - 1.0)
        some = row8 < 6.0
        vx = spline(at_x) + spline(at_x - 1.0)
        vy = spline(at_y) + spline(at_y - 1.0)
        vz = jnp.where(some, spline(near_z) + spline(next_z), 0.0)
        sx = spline_slope(at_x) + spline_slope(at_x - 1.0)
        sy = spline_slope(at_y) + spline_slope(at_y - 1.0)
        sz = jnp.where(some, spline_slope(near_z) + spline_slope(next_z), 0.0)
        vz_charge = vz * charge
        pad = jnp.zeros((16, 128), F32)
        product = jnp.concatenate([vz_charge[k : k + 1] * vy for k in range(6)], axis=0)
        high, low = halves(product)
        right = jnp.concatenate([high, pad, high, pad, low, pad, low, pad], axis=0).astype(BF16)
        left = jnp.concatenate(halves(vx), axis=0).astype(BF16)
        lanes = pl.ds(pl.multiple_of(cell * 384, 128), 384)
        tables = jnp.concatenate(
            [
                jnp.concatenate([one[k : k + 1] * other for k in range(6)], axis=0)
                for one, other in ((vz, vy), (vz, sy), (sz, vy))
            ],
            axis=1,
        )
        high, low = halves(tables)
        pair_hi[:, lanes] = high.astype(BF16)
        pair_lo[:, lanes] = low.astype(BF16)
        vx_ref[:, lanes] = jnp.concatenate([sx, vx, vx], axis=1)
        return total + dot_rows(left, right)

    total = grouped(6, coarse_step, jnp.zeros((16, 256), F32))
    total = total[0:8] + total[8:16]
    lap_buf[0] = total[:, 0:128] + total[:, 128:256]

    pl.semaphore_wait(barrier, len(NEAR) + len(LAPS) + len(members))

    lap_copies = []
    for num, step in enumerate(LAPS):
        copy = pltpu.make_async_remote_copy(
            src_ref=lap_buf.at[0], dst_ref=lap_buf.at[(-step) % laps], send_sem=lap_send.at[num], recv_sem=lap_recv.at[num],
            device_id=lap_id(step), device_id_type=MESH,
        )
        copy.start()
        lap_copies.append(copy)

    def piece(step, far):
        if step == 0:
            return pl.ds(1, 2)
        if far:
            return pl.ds(0 if step > 0 else 3, 1)
        return pl.ds(2 if step > 0 else 1, 1)

    halo_copies = []
    for num, side in enumerate(NEAR):
        copy = pltpu.make_async_remote_copy(
            src_ref=ext.at[piece(side[0], False), piece(side[1], False)],
            dst_ref=ext.at[piece(side[0], True), piece(side[1], True)],
            send_sem=halo_send.at[num], recv_sem=halo_recv.at[num], device_id=near_id(side), device_id_type=MESH,
        )
        copy.start()
        halo_copies.append(copy)

    fine_sum[...] = jnp.zeros_like(fine_sum)

    def fine_step(cell, carry):
        x, y, z, block = cell_rows(cell)
        at_x = 4.0 * block[0:1] - (row8 - 1.0)
        at_y = 4.0 * block[1:2] - (row8 - 1.0)
        at_z = wrapped(4.0 * block[2:3] + (4 * z).astype(F32) - row16)
        bx, by = spline(at_x), spline(at_y)
        bz = jnp.where(row16 < 12.0, spline(at_z), 0.0)
        sz = jnp.where(row16 < 12.0, spline_slope(at_z), 0.0)
        by_ref[cell] = jnp.concatenate([bx, spline_slope(at_x), by, spline_slope(at_y)], axis=0)
        bx_charge = bx * block[3:4]
        product = jnp.concatenate([bx_charge[e : e + 1] * by for e in range(7)] + [jnp.zeros((8, 128), F32)], axis=0)
        right = jnp.concatenate(halves(product), axis=0).astype(BF16)
        high, low = halves(jnp.concatenate([bz, sz], axis=1))
        left = jnp.concatenate([high[:, 0:128], low[:, 0:128]], axis=0).astype(BF16)
        wz_ref[cell] = jnp.concatenate([high, high, high, low, low, low], axis=0).astype(BF16)
        fine_sum[cell // 3] += dot_rows(left, right)
        return carry

    grouped(6, fine_step, 0)
    for load in loads:
        load.wait()
    boxes = jnp.concatenate([fine_sum[num, 0:16] + fine_sum[num, 16:32] for num in range(4)], axis=1)
    spots = dot(jnp.concatenate(thirds(boxes), axis=0).astype(BF16), place_ref[...])
    spots = spots[0:16] + spots[16:32] + spots[32:48]
    rings = lax.dot_general(
        ring_ref[...], spots, (((1,), (0,)), ((), ())), precision=HIGHEST, preferred_element_type=F32
    )
    rings = jnp.concatenate([rings[0:16], rings[16:32]], axis=1)
    parts = jnp.concatenate(halves(rings), axis=0).astype(BF16)
    fine_all = dot(parts, wide_hi[...])
    fine_all = fine_all[0:16] + fine_all[16:32] + dot(parts[0:16], wide_lo[...])
    for num in range(9):
        fine_out[num] = fine_all[:, 128 * num : 128 * (num + 1)]
    fine_copies = []
    for num, side in enumerate(NEAR):
        copy = pltpu.make_async_remote_copy(
            src_ref=fine_out.at[SIDES.index(side)], dst_ref=fine_buf.at[num],
            send_sem=fine_send.at[num], recv_sem=fine_recv.at[num], device_id=near_id(side), device_id_type=MESH,
        )
        copy.start()
        fine_copies.append(copy)

    for copy in lap_copies:
        copy.wait_recv()
    relays = []
    for num, (src, dst, step) in enumerate((
        (pl.ds(1, 4), pl.ds(5, 4), -4),
        (pl.ds(laps - 3, 3), pl.ds(laps - 7, 3), 4),
    )):
        copy = pltpu.make_async_remote_copy(
            src_ref=lap_buf.at[src], dst_ref=lap_buf.at[dst], send_sem=relay_send.at[num], recv_sem=relay_recv.at[num],
            device_id=lap_id(step), device_id_type=MESH,
        )
        copy.start()
        relays.append(copy)

    for copy in halo_copies:
        copy.wait_recv()

    row_w = row_iota(8, 640)
    slot_w = lax.broadcasted_iota(jnp.int32, (8, 640), 1) // 128

    def column_step(column, carry):
        x, y = column // 4, column % 4
        block = ext[x, y]
        block = jnp.concatenate([block[:, 256:384], block, block[:, 0:128]], axis=1)
        shift = jnp.where(
            row_w == 0, (x - 2).astype(F32), jnp.where(row_w == 1, (y - 2).astype(F32), slot_w.astype(F32) - 2.5)
        )
        coords = jnp.where(row_w < 3, SPLIT_RATE * (block + shift), 0.0)
        square = jnp.sum(coords * coords, axis=0, keepdims=True) + SPLIT_RATE * SPLIT_RATE * SOFT_SQUARE
        ones = jnp.where(row_w == 3, 1.0, 0.0)
        p1, p2, p3 = thirds(coords)
        s1, s2, s3 = thirds(square)

        def with_square(part, square_part):
            return jnp.where(row_w == 4, square_part, part + ones)

        right_ref[column] = jnp.concatenate(
            [with_square(p1, s1), with_square(p2, s2), with_square(p1, s3), p3, p2, p1], axis=0
        ).astype(BF16)
        moments = (coords + ones) * block[3:4]
        m1, m2, m3 = thirds(moments)
        mom_ref[column] = jnp.concatenate([m1, m2, m3, jnp.zeros_like(m1)], axis=0).astype(BF16)
        return carry

    lax.fori_loop(0, 16, column_step, 0)

    row_c = row_iota(8)

    def left_step(cell, carry):
        x, y, z, block = cell_rows(cell)
        shift = jnp.where(
            row_c == 0, (x - 1).astype(F32), jnp.where(row_c == 1, (y - 1).astype(F32), z.astype(F32) - 1.5)
        )
        coords = jnp.where(row_c < 3, SPLIT_RATE * (block + shift), 0.0)
        square = jnp.sum(coords * coords, axis=0, keepdims=True)
        ones = jnp.where(row_c == 4, 1.0, 0.0)
        p1, p2, p3 = thirds(-2.0 * coords)
        s1, s2, s3 = thirds(square)

        def with_square(part, square_part):
            return jnp.where(row_c == 3, square_part, part + ones)

        stacked = jnp.concatenate(
            [with_square(p1, s1), with_square(p1, s2), with_square(p2, s3), p1, p2, p3, jnp.zeros((80, 128), F32)], axis=0
        )
        left_ref[cell] = jnp.transpose(stacked).astype(BF16)
        return carry

    grouped(6, left_step, 0)

    def pair_step(cell, carry):
        x, y, z, block = cell_rows(cell)
        left = left_ref[cell][:, 0:48]

        moments = jnp.zeros((128, 32), F32)
        lanes = pl.ds(pl.multiple_of(z * 128, 128), 384)
        for side in range(9):
            column = (x + side // 3) * 4 + y + side % 3
            square = dot(left, right_ref[column, :, lanes])
            inverse = lax.rsqrt(square)
            far = 1.0 - lax.erf(square * inverse)
            bell = jnp.exp2(square * (-math.log2(math.e)))
            factor = (inverse * inverse) * (far * inverse + (2.0 / math.sqrt(math.pi)) * bell)
            high = factor.astype(BF16)
            low = (factor - high.astype(F32)).astype(BF16)
            other = mom_ref[column, :, lanes]
            moments = moments + dot_rows(jnp.concatenate([high, low], axis=1), jnp.concatenate([other, other], axis=1))
        moments = jnp.transpose(moments)
        moments = moments[0:8] + moments[8:16] + moments[16:24]
        shift = jnp.where(
            row_c == 0, (x - 1).astype(F32), jnp.where(row_c == 1, (y - 1).astype(F32), z.astype(F32) - 1.5)
        )
        coords = SPLIT_RATE * (block + shift)
        force_ref[cell] = (SPLIT_RATE * SPLIT_RATE) * block[3:4] * (coords * moments[3:4] - moments)
        return carry

    lax.fori_loop(0, 4, pair_step, 0)

    for copy in relays:
        copy.wait_recv()
    rows = lax.broadcasted_iota(jnp.int32, (64, 128), 0)
    cols = lax.broadcasted_iota(jnp.int32, (64, 128), 1)
    member = (rows // 8) % 4
    to_space = ((outer_x + member // 2) % 2) * 2 * laps + lap * 2 + (core + member % 2) % 2
    from_space = outer_x * 2 * laps + ((lap + cols // 8) % laps) * 2 + core
    total_x = 4 * spaces
    dist = (4 * (to_space - from_space) + rows % 8 - cols % 8 + 2 * total_x) % total_x
    dist = jnp.minimum(dist, total_x - dist).astype(F32)
    wide = [2.0 * (total_x / fraction) ** 2 for fraction in COARSE_FRACTIONS]
    bells = jnp.exp(-dist * dist * jnp.where(rows < 32, 1.0 / wide[0], 1.0 / wide[1]))
    gathered = jnp.concatenate([lap_buf[num] for num in range(laps)], axis=0)
    along_x = lax.dot_general(
        bells, gathered, (((1,), (0,)), ((), ())), precision=HIGHEST, preferred_element_type=F32
    )
    along_x = jnp.where(lax.broadcasted_iota(jnp.int32, (32, 128), 1) < 64, along_x[0:32], along_x[32:64])
    parts = jnp.concatenate(halves(along_x), axis=0).astype(BF16)
    shares = dot(parts, far_hi[...])
    shares = shares[0:32] + shares[32:64] + dot(parts[0:32], far_lo[...])
    for member_num in range(4):
        for step in range(subs):
            plane_out[member_num * subs + step] = shares[8 * member_num : 8 * member_num + 8, 128 * step : 128 * (step + 1)]
    plane_copies = []
    for member_num, step in members:
        num = member_num * subs + step
        copy = pltpu.make_async_remote_copy(
            src_ref=plane_out.at[num], dst_ref=plane_buf.at[num], send_sem=plane_send.at[num], recv_sem=plane_recv.at[num],
            device_id=plane_id(member_num, step), device_id_type=MESH,
        )
        copy.start()
        plane_copies.append(copy)

    lax.fori_loop(4, CELLS, pair_step, 0)

    for copy in fine_copies:
        copy.wait_recv()
    fine = fine_out[SIDES.index((0, 0))]
    for num in range(8):
        fine = fine + fine_buf[num]
    pieces = thirds(fine)
    points = dot_rows(select_ref[...], jnp.concatenate(pieces + pieces, axis=0).astype(BF16)).astype(BF16)
    fine_sum_rows = points

    def interpolate(cell, x, y):
        start = 96 * y + 32 * x
        spread = dot(fine_sum_rows[start : start + 64], wz_ref[cell])
        tables = by_ref[cell]
        u1 = jnp.zeros((8, 128), F32)
        u2 = jnp.zeros((8, 128), F32)
        u3 = jnp.zeros((8, 128), F32)
        for e in range(7):
            at = spread[8 * e : 8 * e + 8]
            u1 = u1 + tables[8 + e : 9 + e] * at[:, 0:128]
            u2 = u2 + tables[e : e + 1] * at[:, 0:128]
            u3 = u3 + tables[e : e + 1] * at[:, 128:256]
        by, sy = tables[16:24], tables[24:32]
        return [jnp.sum(one * other, axis=0, keepdims=True) for one, other in ((by, u1), (sy, u2), (by, u3))]

    fine_forces = [interpolate(cell, cell // 6, (cell // 3) % 2) for cell in range(CELLS)]

    for copy in plane_copies:
        copy.wait_recv()
    window = plane_out[0]
    for member_num, step in members:
        window = window + plane_buf[member_num * subs + step]
    parts = jnp.concatenate(halves(window), axis=0).astype(BF16)[:, 0:48]
    for cell in range(CELLS):
        x, y, z = cell // 6, (cell // 3) % 2, cell % 3
        lanes = pl.ds(384 * cell, 384)
        spread = dot(parts, pair_hi[:, lanes])
        spread = spread[0:8] + spread[8:16] + dot(parts, pair_lo[:, lanes])[0:8]
        spread = jnp.sum(spread * vx_ref[:, lanes], axis=0, keepdims=True)
        charge = ext[1 + x, 1 + y, pl.ds(3, 1), pl.ds(128 * z, 128)]
        for k in range(3):
            far = fine_forces[cell][k] + spread[:, 128 * k : 128 * (k + 1)]
            out_ref[k, x, z, pl.ds(y, 1), :] = force_ref[cell, pl.ds(k, 1), :] - 4.0 * charge * far

    for copy in lap_copies + halo_copies + fine_copies + relays + plane_copies:
        copy.wait_send()


def solution(mesh):
    spaces, subs = mesh.shape["space"], mesh.shape["sub"]
    laps = spaces // 4
    place, spread, ring, select, coarse = constants(subs)

    def body(positions, charges, counts):
        any_spec = pl.BlockSpec(memory_space=pl.ANY)
        vmem_spec = pl.BlockSpec(memory_space=pltpu.VMEM)
        planes = 4 * subs
        positions = jnp.transpose(positions, (0, 1, 3, 2, 4))
        charges = jnp.transpose(charges, (0, 2, 1, 3))
        forces = pl.pallas_call(
            functools.partial(kernel, spaces, subs),
            out_shape=jax.ShapeDtypeStruct(positions.shape, F32),
            in_specs=[vmem_spec, vmem_spec, pl.BlockSpec(memory_space=pltpu.SMEM), any_spec, any_spec, any_spec, vmem_spec, any_spec, any_spec, any_spec],
            out_specs=vmem_spec,
            scratch_shapes=[
                pltpu.VMEM((512, 128), BF16),
                pltpu.VMEM((256, 1152), BF16),
                pltpu.VMEM((256, 1152), BF16),
                pltpu.VMEM((192, 128), BF16),
                pltpu.VMEM((128, 128 * subs), BF16),
                pltpu.VMEM((128, 128 * subs), BF16),
                pltpu.VMEM((4, 4, 8, 384), F32),
                pltpu.VMEM((laps, 8, 128), F32),
                pltpu.VMEM((planes, 8, 128), F32),
                pltpu.VMEM((planes, 8, 128), F32),
                pltpu.VMEM((9, 16, 128), F32),
                pltpu.VMEM((8, 16, 128), F32),
                pltpu.VMEM((4, 32, 128), F32),
                pltpu.VMEM((CELLS, 32, 128), F32),
                pltpu.VMEM((CELLS, 96, 256), BF16),
                pltpu.VMEM((48, CELLS * 384), BF16),
                pltpu.VMEM((48, CELLS * 384), BF16),
                pltpu.VMEM((8, CELLS * 384), F32),
                pltpu.VMEM((CELLS, 128, 128), BF16),
                pltpu.VMEM((16, 48, 640), BF16),
                pltpu.VMEM((16, 32, 640), BF16),
                pltpu.VMEM((CELLS, 8, 128), F32),
                pltpu.SemaphoreType.DMA((6,)),
                pltpu.SemaphoreType.DMA((8,)),
                pltpu.SemaphoreType.DMA((8,)),
                pltpu.SemaphoreType.DMA((8,)),
                pltpu.SemaphoreType.DMA((8,)),
                pltpu.SemaphoreType.DMA((2,)),
                pltpu.SemaphoreType.DMA((2,)),
                pltpu.SemaphoreType.DMA((8,)),
                pltpu.SemaphoreType.DMA((8,)),
                pltpu.SemaphoreType.DMA((planes,)),
                pltpu.SemaphoreType.DMA((planes,)),
            ],
            compiler_params=pltpu.CompilerParams(collective_id=0, has_side_effects=True),
        )(
            positions, charges, counts,
            jnp.asarray(place), jnp.asarray(spread[0]), jnp.asarray(spread[1]), jnp.asarray(ring), jnp.asarray(select),
            jnp.asarray(coarse[0]), jnp.asarray(coarse[1]),
        )
        return jnp.transpose(forces, (0, 1, 3, 2, 4))

    in_specs = (
        P(None, "space", "sub", None, None),
        P("space", "sub", None, None),
        P("space", "sub", None),
    )
    out_specs = P(None, "space", "sub", None, None)
    return jax.shard_map(body, mesh=mesh, in_specs=in_specs, out_specs=out_specs, check_vma=False)
```

```python
import functools
import math

import jax
import jax.numpy as jnp
import numpy as np
from jax import lax
from jax.experimental import pallas as pl
from jax.experimental.pallas import tpu as pltpu
from jax.sharding import PartitionSpec as P

F32 = jnp.float32
BF16 = jnp.bfloat16
MESH = pl.DeviceIdType.MESH
HIGHEST = lax.Precision.HIGHEST
SPLIT_RATE = 0.8
SOFT_SQUARE = 0.0625
FINE_WIDTHS = (1.0, 2.0)
FINE_WEIGHTS = (2.0, 0.5)
COARSE_FRACTIONS = (8.0, 4.0)
COARSE_WEIGHTS = (4.0, 2.0)
REACH = 4
SIDES = [(dx, dy) for dx in (-1, 0, 1) for dy in (-1, 0, 1)]
NEAR = [side for side in SIDES if side != (0, 0)]
LAPS = (1, 2, 3, 4, -1, -2, -3, -4)
CELLS = 12


def two_parts(table):
    table = np.asarray(table, np.float32)
    high = table.astype(jnp.bfloat16)
    low = (table - high.astype(np.float32)).astype(jnp.bfloat16)
    return high, low


def constants(sub_size):
    place = np.zeros((4, 2, 64, 128), np.float32)
    for x in range(2):
        for y in range(2):
            for e in range(7):
                for f in range(7):
                    place[2 * x + y, :, 8 * e + f, 11 * (4 * x + e) + 4 * y + f] = 1.0
    place = place.reshape(512, 128).astype(jnp.bfloat16)
    tap = np.arange(11)
    spread = np.zeros((2, 128, 9, 128), np.float32)
    for number, (width, weight) in enumerate(zip(FINE_WIDTHS, FINE_WEIGHTS)):
        for place_num, (dx, dy) in enumerate(SIDES):
            per_axis = []
            for step in (dx, dy):
                dist = np.abs(tap[None, :] + 8 * step - tap[:, None]).astype(np.float64)
                per_axis.append(np.where(dist <= REACH, np.exp(-dist * dist / (2 * width * width)), 0.0))
            both = weight * np.kron(per_axis[0], per_axis[1])
            spread[number, :121, place_num, :121] = both
    spread = two_parts(spread.reshape(256, 9 * 128))
    ring = np.zeros((2, 16, 16), np.float32)
    for number, width in enumerate(FINE_WIDTHS):
        dist = np.abs(np.arange(12)[:, None] - np.arange(12)[None, :])
        dist = np.minimum(dist, 12 - dist).astype(np.float64)
        ring[number, :12, :12] = np.where(dist <= REACH, np.exp(-dist * dist / (2 * width * width)), 0.0)
    ring = ring.reshape(32, 16)
    select = np.zeros((2, 12, 8, 128), np.float32)
    for y in range(2):
        for x in range(11):
            for f in range(7):
                select[y, x, f, 11 * x + 4 * y + f] = 1.0
    select = select.reshape(192, 128).astype(jnp.bfloat16)
    total_y = 4 * sub_size
    coarse = np.zeros((2, 8, 8, sub_size, 16, 8), np.float32)
    for number, (fraction, weight) in enumerate(zip(COARSE_FRACTIONS, COARSE_WEIGHTS)):
        dist = np.abs(np.arange(6)[:, None] - np.arange(6)[None, :])
        dist = np.minimum(dist, 6 - dist).astype(np.float64)
        along_z = np.exp(-dist * dist / (2 * (6 / fraction) ** 2))
        for step in range(sub_size):
            dist = np.mod(4 * step + np.arange(6)[None, :] - np.arange(6)[:, None], total_y)
            dist = np.minimum(dist, total_y - dist).astype(np.float64)
            along_y = np.exp(-dist * dist / (2 * (total_y / fraction) ** 2))
            both = 0.125 * weight * along_z[:, None, :, None] * along_y[None, :, None, :]
            coarse[number, :6, :6, step, :6, :6] = both
    coarse = two_parts(coarse.reshape(128, sub_size * 128))
    return place, spread, ring, select, coarse


def halves(value):
    high = value.astype(BF16).astype(F32)
    return high, value - high


def thirds(value):
    high, rest = halves(value)
    middle, low = halves(rest)
    return high, middle, low


def dot(left, right):
    return lax.dot_general(left, right, (((1,), (0,)), ((), ())), preferred_element_type=F32)


def dot_rows(left, right):
    return lax.dot_general(left, right, (((1,), (1,)), ((), ())), preferred_element_type=F32)


def spline(shifted):
    size = jnp.abs(shifted)
    outer = jnp.maximum(2.0 - size, 0.0)
    inner = jnp.maximum(1.0 - size, 0.0)
    return outer * outer * outer * (1.0 / 6.0) - inner * inner * inner * (2.0 / 3.0)


def spline_slope(shifted):
    size = jnp.abs(shifted)
    outer = jnp.maximum(2.0 - size, 0.0)
    inner = jnp.maximum(1.0 - size, 0.0)
    slope = 2.0 * inner * inner - 0.5 * outer * outer
    return jnp.where(shifted < 0.0, -slope, slope)


def wrapped(shifted):
    return jnp.where(shifted > 6.0, shifted - 12.0, jnp.where(shifted < -6.0, shifted + 12.0, shifted))


def grouped(size, step, start, cells=CELLS):
    def group(number, carry):
        for num in range(size):
            carry = step(number * size + num, carry)
        return carry

    return lax.fori_loop(0, cells // size, group, start)


def row_iota(rows, lanes=128):
    return lax.broadcasted_iota(jnp.int32, (rows, lanes), 0)


def kernel(
    spaces, subs,
    pos_hbm, charge_hbm, count_hbm, place_hbm, wide_hi_hbm, wide_lo_hbm, ring_hbm, select_hbm, far_hi_hbm, far_lo_hbm,
    out_ref,
    pos_ref, charge_ref, count_ref, ring_ref, place_ref, wide_hi, wide_lo, select_ref, far_hi, far_lo,
    ext, lap_buf, plane_out, plane_buf, fine_out, fine_buf,
    fine_sum, by_ref, wz_ref, pair_hi, pair_lo, vx_ref, left_ref, right_ref, mom_ref, square_ref, raw_ref, back_ref, force_ref,
    input_sem, const_sem, halo_send, halo_recv, lap_send, lap_recv, relay_send, relay_recv, fine_send, fine_recv, plane_send, plane_recv,
):
    laps = spaces // 4
    space = lax.axis_index("space")
    sub = lax.axis_index("sub")
    outer_x = space // (2 * laps)
    lap = (space // 2) % laps
    core = space % 2

    loads = [
        pltpu.make_async_copy(src, dst, const_sem.at[num])
        for num, (src, dst) in enumerate((
            (place_hbm, place_ref), (wide_hi_hbm, wide_hi), (wide_lo_hbm, wide_lo),
            (select_hbm, select_ref), (far_hi_hbm, far_hi), (far_lo_hbm, far_lo), (ring_hbm, ring_ref),
        ))
    ]
    inputs = [
        pltpu.make_async_copy(src, dst, input_sem.at[num])
        for num, (src, dst) in enumerate(((pos_hbm, pos_ref), (charge_hbm, charge_ref), (count_hbm, count_ref)))
    ]
    for load in inputs:
        load.start()

    def near_id(side):
        return {"space": (space + side[0] + spaces) % spaces, "sub": (sub + side[1] + subs) % subs}

    def lap_id(step):
        return {"space": outer_x * 2 * laps + ((lap + step + laps) % laps) * 2 + core, "sub": sub}

    def plane_id(member, step):
        return {
            "space": ((outer_x + member // 2) % 2) * 2 * laps + lap * 2 + (core + member % 2) % 2,
            "sub": (sub + step) % subs,
        }

    members = [(member, step) for member in range(4) for step in range(subs) if (member, step) != (0, 0)]
    barrier = pltpu.get_barrier_semaphore()
    for side in NEAR:
        pl.semaphore_signal(barrier, inc=1, device_id=near_id(side), device_id_type=MESH)
    for step in LAPS:
        pl.semaphore_signal(barrier, inc=1, device_id=lap_id(step), device_id_type=MESH)
    for member, step in members:
        pl.semaphore_signal(barrier, inc=1, device_id=plane_id(member, step), device_id_type=MESH)

    for load in loads:
        load.start()
    for load in inputs:
        load.wait()
    lane = lax.broadcasted_iota(jnp.int32, (1, 128), 1)
    for x in range(2):
        for y in range(2):
            for z in range(3):
                lanes = pl.ds(128 * z, 128)
                for k in range(3):
                    ext[1 + x, 1 + y, pl.ds(k, 1), lanes] = pos_ref[k, x, z, pl.ds(y, 1), :]
                live = lane < count_ref[x, y, z]
                ext[1 + x, 1 + y, pl.ds(3, 1), lanes] = jnp.where(live, charge_ref[x, z, pl.ds(y, 1), :], 0.0)
            ext[1 + x, 1 + y, pl.ds(4, 4), :] = jnp.zeros((4, 384), F32)

    def cell_rows(cell):
        x, y, z = cell // 6, (cell // 3) % 2, cell % 3
        block = ext[1 + x, 1 + y, :, pl.ds(pl.multiple_of(z * 128, 128), 128)]
        return x, y, z, block

    row8 = row_iota(8).astype(F32)
    row16 = row_iota(16).astype(F32)

    def coarse_step(cell, total):
        x, y, z, block = cell_rows(cell)
        at_x = 4.0 * block[0:1] + (4 * x + 2).astype(F32) - 2.0 * row8
        at_y = 4.0 * block[1:2] + (4 * y + 2).astype(F32) - 2.0 * row8
        at_z = 4.0 * block[2:3] + (4 * z).astype(F32) - 2.0 * row8
        charge = block[3:4]
        near_z, next_z = wrapped(at_z), wrapped(at_z - 1.0)
        some = row8 < 6.0
        vx = spline(at_x) + spline(at_x - 1.0)
        vy = spline(at_y) + spline(at_y - 1.0)
        vz = jnp.where(some, spline(near_z) + spline(next_z), 0.0)
        sx = spline_slope(at_x) + spline_slope(at_x - 1.0)
        sy = spline_slope(at_y) + spline_slope(at_y - 1.0)
        sz = jnp.where(some, spline_slope(near_z) + spline_slope(next_z), 0.0)
        vz_charge = vz * charge
        pad = jnp.zeros((16, 128), F32)
        product = jnp.concatenate([vz_charge[k : k + 1] * vy for k in range(6)], axis=0)
        high, low = halves(product)
        right = jnp.concatenate([high, pad, high, pad, low, pad, low, pad], axis=0).astype(BF16)
        left = jnp.concatenate(halves(vx), axis=0).astype(BF16)
        lanes = pl.ds(pl.multiple_of(cell * 384, 128), 384)
        tables = jnp.concatenate(
            [
                jnp.concatenate([one[k : k + 1] * other for k in range(6)], axis=0)
                for one, other in ((vz, vy), (vz, sy), (sz, vy))
            ],
            axis=1,
        )
        high, low = halves(tables)
        pair_hi[:, lanes] = high.astype(BF16)
        pair_lo[:, lanes] = low.astype(BF16)
        vx_ref[:, lanes] = jnp.concatenate([sx, vx, vx], axis=1)
        return total + dot_rows(left, right)

    total = grouped(6, coarse_step, jnp.zeros((16, 256), F32))
    total = total[0:8] + total[8:16]
    lap_buf[0] = total[:, 0:128] + total[:, 128:256]

    fine_sum[...] = jnp.zeros_like(fine_sum)

    def fine_step(cell, carry):
        x, y, z, block = cell_rows(cell)
        at_x = 4.0 * block[0:1] - (row8 - 1.0)
        at_y = 4.0 * block[1:2] - (row8 - 1.0)
        at_z = wrapped(4.0 * block[2:3] + (4 * z).astype(F32) - row16)
        bx, by = spline(at_x), spline(at_y)
        bz = jnp.where(row16 < 12.0, spline(at_z), 0.0)
        sz = jnp.where(row16 < 12.0, spline_slope(at_z), 0.0)
        by_ref[cell] = jnp.concatenate([bx, spline_slope(at_x), by, spline_slope(at_y)], axis=0)
        bx_charge = bx * block[3:4]
        product = jnp.concatenate([bx_charge[e : e + 1] * by for e in range(7)] + [jnp.zeros((8, 128), F32)], axis=0)
        right = jnp.concatenate(halves(product), axis=0).astype(BF16)
        high, low = halves(jnp.concatenate([bz, sz], axis=1))
        left = jnp.concatenate([high[:, 0:128], low[:, 0:128]], axis=0).astype(BF16)
        wz_ref[cell] = jnp.concatenate([high, high, high, low, low, low], axis=0).astype(BF16)
        fine_sum[cell // 3] += dot_rows(left, right)
        return carry

    grouped(6, fine_step, 0)
    for load in loads:
        load.wait()
    boxes = jnp.concatenate([fine_sum[num, 0:16] + fine_sum[num, 16:32] for num in range(4)], axis=1)
    spots = dot(jnp.concatenate(thirds(boxes), axis=0).astype(BF16), place_ref[...])
    spots = spots[0:16] + spots[16:32] + spots[32:48]
    rings = lax.dot_general(
        ring_ref[...], spots, (((1,), (0,)), ((), ())), precision=HIGHEST, preferred_element_type=F32
    )
    rings = jnp.concatenate([rings[0:16], rings[16:32]], axis=1)
    parts = jnp.concatenate(halves(rings), axis=0).astype(BF16)
    fine_all = dot(parts, wide_hi[...])
    fine_all = fine_all[0:16] + fine_all[16:32] + dot(parts[0:16], wide_lo[...])
    for num in range(9):
        fine_out[num] = fine_all[:, 128 * num : 128 * (num + 1)]
    row_w = row_iota(8, 640)
    slot_w = lax.broadcasted_iota(jnp.int32, (8, 640), 1) // 128

    def column_step(column, carry):
        x, y = column // 4, column % 4
        block = ext[x, y]
        block = jnp.concatenate([block[:, 256:384], block, block[:, 0:128]], axis=1)
        shift = jnp.where(
            row_w == 0, (x - 2).astype(F32), jnp.where(row_w == 1, (y - 2).astype(F32), slot_w.astype(F32) - 2.5)
        )
        coords = jnp.where(row_w < 3, SPLIT_RATE * (block + shift), 0.0)
        square = jnp.sum(coords * coords, axis=0, keepdims=True) + SPLIT_RATE * SPLIT_RATE * SOFT_SQUARE
        ones = jnp.where(row_w == 3, 1.0, 0.0)
        p1, p2, p3 = thirds(coords)
        s1, s2, s3 = thirds(square)

        def with_square(part, square_part):
            return jnp.where(row_w == 4, square_part, part + ones)

        right_ref[column] = jnp.concatenate(
            [with_square(p1, s1), with_square(p2, s2), with_square(p1, s3), p3, p2, p1], axis=0
        ).astype(BF16)
        moments = (coords + ones) * block[3:4]
        m1, m2, m3 = thirds(moments)
        mom_ref[column] = jnp.concatenate([m1, m2, m3, jnp.zeros_like(m1)], axis=0).astype(BF16)
        return carry

    for column in (5, 6, 9, 10):
        column_step(jnp.int32(column), 0)

    row_c = row_iota(8)

    def left_step(cell, carry):
        x, y, z, block = cell_rows(cell)
        shift = jnp.where(
            row_c == 0, (x - 1).astype(F32), jnp.where(row_c == 1, (y - 1).astype(F32), z.astype(F32) - 1.5)
        )
        coords = jnp.where(row_c < 3, SPLIT_RATE * (block + shift), 0.0)
        square = jnp.sum(coords * coords, axis=0, keepdims=True)
        ones = jnp.where(row_c == 4, 1.0, 0.0)
        p1, p2, p3 = thirds(-2.0 * coords)
        s1, s2, s3 = thirds(square)

        def with_square(part, square_part):
            return jnp.where(row_c == 3, square_part, part + ones)

        stacked = jnp.concatenate(
            [with_square(p1, s1), with_square(p1, s2), with_square(p2, s3), p1, p2, p3, jnp.zeros((80, 128), F32)], axis=0
        )
        left_ref[cell] = jnp.transpose(stacked).astype(BF16)
        return carry

    grouped(6, left_step, 0)

    pl.semaphore_wait(barrier, len(NEAR) + len(LAPS) + len(members))

    lap_copies = []
    for num, step in enumerate(LAPS):
        copy = pltpu.make_async_remote_copy(
            src_ref=lap_buf.at[0], dst_ref=lap_buf.at[(-step) % laps], send_sem=lap_send.at[num], recv_sem=lap_recv.at[num],
            device_id=lap_id(step), device_id_type=MESH,
        )
        copy.start()
        lap_copies.append(copy)

    def piece(step, far):
        if step == 0:
            return pl.ds(1, 2)
        if far:
            return pl.ds(0 if step > 0 else 3, 1)
        return pl.ds(2 if step > 0 else 1, 1)

    halo_copies = []
    for num, side in enumerate(NEAR):
        copy = pltpu.make_async_remote_copy(
            src_ref=ext.at[piece(side[0], False), piece(side[1], False)],
            dst_ref=ext.at[piece(side[0], True), piece(side[1], True)],
            send_sem=halo_send.at[num], recv_sem=halo_recv.at[num], device_id=near_id(side), device_id_type=MESH,
        )
        copy.start()
        halo_copies.append(copy)

    fine_copies = []
    for num, side in enumerate(NEAR):
        copy = pltpu.make_async_remote_copy(
            src_ref=fine_out.at[SIDES.index(side)], dst_ref=fine_buf.at[num],
            send_sem=fine_send.at[num], recv_sem=fine_recv.at[num], device_id=near_id(side), device_id_type=MESH,
        )
        copy.start()
        fine_copies.append(copy)


    def outer_columns(cell):
        x, y = cell // 6, (cell // 3) % 2
        return [12 * x + y + num for num in range(3)] + [3 * y + 4, 3 * y + 8]

    def slot_lanes(slot, count=1):
        return pl.ds(pl.multiple_of(slot * 128, 128), 128 * count)

    def pull(square):
        inverse = lax.rsqrt(square)
        far = 1.0 - lax.erf(square * inverse)
        bell = jnp.exp2(square * (-math.log2(math.e)))
        factor = (inverse * inverse) * (far * inverse + (2.0 / math.sqrt(math.pi)) * bell)
        high = factor.astype(BF16)
        return high, (factor - high.astype(F32)).astype(BF16)

    def gather_moments(moments, high, low, other):
        return moments + dot_rows(jnp.concatenate([high, low], axis=1), jnp.concatenate([other, other], axis=1))

    inner_ids = (5, 6, 9, 10)

    def inner_squares(z, half):
        at = 0
        for one in range(4):
            left = left_ref[3 * one + z][:, 0:48]
            own = inner_ids[one]
            square_ref[half, :, 128 * at : 128 * (at + 2)] = dot(left, right_ref[own, :, slot_lanes(z + 1, 2)])
            at += 2
            for other in range(one + 1, 4):
                column = inner_ids[other]
                square_ref[half, :, 128 * at : 128 * (at + 3)] = dot(left, right_ref[column, :, slot_lanes(z, 3)])
                at += 3

    def inner_pulls(z, half):
        at = 0
        for one in range(4):
            own = inner_ids[one]
            moments = jnp.zeros((128, 32), F32)
            units = [(one, 1), (one, 2)] + [(other, slot) for other in range(one + 1, 4) for slot in range(3)]
            for other, slot in units:
                high, low = pull(square_ref[half, :, 128 * at : 128 * (at + 1)])
                at += 1
                moments = gather_moments(moments, high, low, mom_ref[inner_ids[other], :, slot_lanes(z + slot)])
                if (other, slot) != (one, 1):
                    z_other = (z + slot + 2) % 3
                    back = mom_ref[own, :, slot_lanes(z_other + 2 - slot)]
                    cell = 3 * other + z_other
                    back_ref[cell] += dot(jnp.concatenate([back, back], axis=1), jnp.concatenate([high, low], axis=0))
            raw_ref[3 * one + z] = moments

    def inner_sweep(start, stop):
        inner_squares(jnp.int32(start), 0)
        for z in range(start, stop):
            if z + 1 < stop:
                inner_squares(jnp.int32(z + 1), (z + 1 - start) % 2)
            inner_pulls(jnp.int32(z), (z - start) % 2)

    def outer_squares(cell, half):
        left = left_ref[cell][:, 0:48]
        lanes = slot_lanes(cell % 3, 3)
        for num, column in enumerate(outer_columns(cell)):
            square_ref[half, :, 384 * num : 384 * (num + 1)] = dot(left, right_ref[column, :, lanes])

    def outer_pulls(cell, half):
        moments = raw_ref[cell]
        for num, column in enumerate(outer_columns(cell)):
            for slot in range(3):
                at = 384 * num + 128 * slot
                high, low = pull(square_ref[half, :, at : at + 128])
                moments = gather_moments(moments, high, low, mom_ref[column, :, slot_lanes(cell % 3 + slot)])
        raw_ref[cell] = moments

    def outer_sweep(start, stop):
        outer_squares(start, 0)

        def step(num, carry):
            for part in range(4):
                cell = start + 4 * num + part
                outer_squares(jnp.minimum(cell + 1, stop - 1), (part + 1) % 2)
                outer_pulls(cell, part % 2)
            return carry

        lax.fori_loop(0, (stop - start) // 4, step, 0)

    def finish_step(cell, carry):
        x, y, z, block = cell_rows(cell)
        moments = jnp.transpose(raw_ref[cell])
        moments = moments + back_ref[cell]
        moments = moments[0:8] + moments[8:16] + moments[16:24]
        shift = jnp.where(
            row_c == 0, (x - 1).astype(F32), jnp.where(row_c == 1, (y - 1).astype(F32), z.astype(F32) - 1.5)
        )
        coords = SPLIT_RATE * (block + shift)
        force_ref[cell] = (SPLIT_RATE * SPLIT_RATE) * block[3:4] * (coords * moments[3:4] - moments)
        return carry

    back_ref[...] = jnp.zeros_like(back_ref)
    inner_sweep(0, 3)

    for copy in lap_copies:
        copy.wait_recv()
    relays = []
    for num, (src, dst, step) in enumerate((
        (pl.ds(1, 4), pl.ds(5, 4), -4),
        (pl.ds(laps - 3, 3), pl.ds(laps - 7, 3), 4),
    )):
        copy = pltpu.make_async_remote_copy(
            src_ref=lap_buf.at[src], dst_ref=lap_buf.at[dst], send_sem=relay_send.at[num], recv_sem=relay_recv.at[num],
            device_id=lap_id(step), device_id_type=MESH,
        )
        copy.start()
        relays.append(copy)


    for copy in halo_copies:
        copy.wait_recv()

    def rim_step(num, carry):
        return column_step(num + jnp.where(num > 4, 2, 0) + jnp.where(num > 6, 2, 0), carry)

    lax.fori_loop(0, 12, rim_step, 0)
    outer_sweep(0, 4)

    for copy in relays:
        copy.wait_recv()
    rows = lax.broadcasted_iota(jnp.int32, (64, 128), 0)
    cols = lax.broadcasted_iota(jnp.int32, (64, 128), 1)
    member = (rows // 8) % 4
    to_space = ((outer_x + member // 2) % 2) * 2 * laps + lap * 2 + (core + member % 2) % 2
    from_space = outer_x * 2 * laps + ((lap + cols // 8) % laps) * 2 + core
    total_x = 4 * spaces
    dist = (4 * (to_space - from_space) + rows % 8 - cols % 8 + 2 * total_x) % total_x
    dist = jnp.minimum(dist, total_x - dist).astype(F32)
    wide = [2.0 * (total_x / fraction) ** 2 for fraction in COARSE_FRACTIONS]
    bells = jnp.exp(-dist * dist * jnp.where(rows < 32, 1.0 / wide[0], 1.0 / wide[1]))
    gathered = jnp.concatenate([lap_buf[num] for num in range(laps)], axis=0)
    along_x = lax.dot_general(
        bells, gathered, (((1,), (0,)), ((), ())), precision=HIGHEST, preferred_element_type=F32
    )
    along_x = jnp.where(lax.broadcasted_iota(jnp.int32, (32, 128), 1) < 64, along_x[0:32], along_x[32:64])
    parts = jnp.concatenate(halves(along_x), axis=0).astype(BF16)
    shares = dot(parts, far_hi[...])
    shares = shares[0:32] + shares[32:64] + dot(parts[0:32], far_lo[...])
    for member_num in range(4):
        for step in range(subs):
            plane_out[member_num * subs + step] = shares[8 * member_num : 8 * member_num + 8, 128 * step : 128 * (step + 1)]
    plane_copies = []
    for member_num, step in members:
        num = member_num * subs + step
        copy = pltpu.make_async_remote_copy(
            src_ref=plane_out.at[num], dst_ref=plane_buf.at[num], send_sem=plane_send.at[num], recv_sem=plane_recv.at[num],
            device_id=plane_id(member_num, step), device_id_type=MESH,
        )
        copy.start()
        plane_copies.append(copy)

    outer_sweep(4, CELLS)
    grouped(6, finish_step, 0)

    for copy in fine_copies:
        copy.wait_recv()
    fine = fine_out[SIDES.index((0, 0))]
    for num in range(8):
        fine = fine + fine_buf[num]
    pieces = thirds(fine)
    points = dot_rows(select_ref[...], jnp.concatenate(pieces + pieces, axis=0).astype(BF16)).astype(BF16)
    fine_sum_rows = points

    def interpolate(cell, x, y):
        start = 96 * y + 32 * x
        spread = dot(fine_sum_rows[start : start + 64], wz_ref[cell])
        tables = by_ref[cell]
        u1 = jnp.zeros((8, 128), F32)
        u2 = jnp.zeros((8, 128), F32)
        u3 = jnp.zeros((8, 128), F32)
        for e in range(7):
            at = spread[8 * e : 8 * e + 8]
            u1 = u1 + tables[8 + e : 9 + e] * at[:, 0:128]
            u2 = u2 + tables[e : e + 1] * at[:, 0:128]
            u3 = u3 + tables[e : e + 1] * at[:, 128:256]
        by, sy = tables[16:24], tables[24:32]
        return [jnp.sum(one * other, axis=0, keepdims=True) for one, other in ((by, u1), (sy, u2), (by, u3))]

    fine_forces = [interpolate(cell, cell // 6, (cell // 3) % 2) for cell in range(CELLS)]

    for copy in plane_copies:
        copy.wait_recv()
    window = plane_out[0]
    for member_num, step in members:
        window = window + plane_buf[member_num * subs + step]
    parts = jnp.concatenate(halves(window), axis=0).astype(BF16)[:, 0:48]
    for cell in range(CELLS):
        x, y, z = cell // 6, (cell // 3) % 2, cell % 3
        lanes = pl.ds(384 * cell, 384)
        spread = dot(parts, pair_hi[:, lanes])
        spread = spread[0:8] + spread[8:16] + dot(parts, pair_lo[:, lanes])[0:8]
        spread = jnp.sum(spread * vx_ref[:, lanes], axis=0, keepdims=True)
        charge = ext[1 + x, 1 + y, pl.ds(3, 1), pl.ds(128 * z, 128)]
        for k in range(3):
            far = fine_forces[cell][k] + spread[:, 128 * k : 128 * (k + 1)]
            out_ref[k, x, z, pl.ds(y, 1), :] = force_ref[cell, pl.ds(k, 1), :] - 4.0 * charge * far

    for copy in lap_copies + halo_copies + fine_copies + relays + plane_copies:
        copy.wait_send()


def solution(mesh):
    spaces, subs = mesh.shape["space"], mesh.shape["sub"]
    laps = spaces // 4
    place, spread, ring, select, coarse = constants(subs)

    def body(positions, charges, counts):
        any_spec = pl.BlockSpec(memory_space=pl.ANY)
        vmem_spec = pl.BlockSpec(memory_space=pltpu.VMEM)
        planes = 4 * subs
        positions = jnp.transpose(positions, (0, 1, 3, 2, 4))
        charges = jnp.transpose(charges, (0, 2, 1, 3))
        forces = pl.pallas_call(
            functools.partial(kernel, spaces, subs),
            out_shape=jax.ShapeDtypeStruct(positions.shape, F32),
            in_specs=[any_spec] * 10,
            out_specs=vmem_spec,
            scratch_shapes=[
                pltpu.VMEM((3, 2, 3, 2, 128), F32),
                pltpu.VMEM((2, 3, 2, 128), F32),
                pltpu.SMEM((2, 2, 3), jnp.int32),
                pltpu.VMEM((32, 16), F32),
                pltpu.VMEM((512, 128), BF16),
                pltpu.VMEM((256, 1152), BF16),
                pltpu.VMEM((256, 1152), BF16),
                pltpu.VMEM((192, 128), BF16),
                pltpu.VMEM((128, 128 * subs), BF16),
                pltpu.VMEM((128, 128 * subs), BF16),
                pltpu.VMEM((4, 4, 8, 384), F32),
                pltpu.VMEM((laps, 8, 128), F32),
                pltpu.VMEM((planes, 8, 128), F32),
                pltpu.VMEM((planes, 8, 128), F32),
                pltpu.VMEM((9, 16, 128), F32),
                pltpu.VMEM((8, 16, 128), F32),
                pltpu.VMEM((4, 32, 128), F32),
                pltpu.VMEM((CELLS, 32, 128), F32),
                pltpu.VMEM((CELLS, 96, 256), BF16),
                pltpu.VMEM((48, CELLS * 384), BF16),
                pltpu.VMEM((48, CELLS * 384), BF16),
                pltpu.VMEM((8, CELLS * 384), F32),
                pltpu.VMEM((CELLS, 128, 128), BF16),
                pltpu.VMEM((16, 48, 640), BF16),
                pltpu.VMEM((16, 32, 640), BF16),
                pltpu.VMEM((2, 128, 3328), F32),
                pltpu.VMEM((CELLS, 128, 32), F32),
                pltpu.VMEM((CELLS, 32, 128), F32),
                pltpu.VMEM((CELLS, 8, 128), F32),
                pltpu.SemaphoreType.DMA((3,)),
                pltpu.SemaphoreType.DMA((7,)),
                pltpu.SemaphoreType.DMA((8,)),
                pltpu.SemaphoreType.DMA((8,)),
                pltpu.SemaphoreType.DMA((8,)),
                pltpu.SemaphoreType.DMA((8,)),
                pltpu.SemaphoreType.DMA((2,)),
                pltpu.SemaphoreType.DMA((2,)),
                pltpu.SemaphoreType.DMA((8,)),
                pltpu.SemaphoreType.DMA((8,)),
                pltpu.SemaphoreType.DMA((planes,)),
                pltpu.SemaphoreType.DMA((planes,)),
            ],
            compiler_params=pltpu.CompilerParams(collective_id=0, has_side_effects=True),
        )(
            positions, charges, counts,
            jnp.asarray(place), jnp.asarray(spread[0]), jnp.asarray(spread[1]), jnp.asarray(ring), jnp.asarray(select),
            jnp.asarray(coarse[0]), jnp.asarray(coarse[1]),
        )
        return jnp.transpose(forces, (0, 1, 3, 2, 4))

    in_specs = (
        P(None, "space", "sub", None, None),
        P("space", "sub", None, None),
        P("space", "sub", None),
    )
    out_specs = P(None, "space", "sub", None, None)
    return jax.shard_map(body, mesh=mesh, in_specs=in_specs, out_specs=out_specs, check_vma=False)
```

```python
import functools
import math

import jax
import jax.numpy as jnp
import numpy as np
from jax import lax
from jax.experimental import pallas as pl
from jax.experimental.pallas import tpu as pltpu
from jax.sharding import PartitionSpec as P

F32 = jnp.float32
BF16 = jnp.bfloat16
MESH = pl.DeviceIdType.MESH
HIGHEST = lax.Precision.HIGHEST
SPLIT_RATE = 0.8
SOFT_SQUARE = 0.0625
FINE_WIDTHS = (1.0, 2.0)
FINE_WEIGHTS = (2.0, 0.5)
COARSE_FRACTIONS = (8.0, 4.0)
COARSE_WEIGHTS = (4.0, 2.0)
REACH = 4
SIDES = [(dx, dy) for dx in (-1, 0, 1) for dy in (-1, 0, 1)]
NEAR = [side for side in SIDES if side != (0, 0)]
LAPS = (1, 2, 3, 4, -1, -2, -3, -4)
CELLS = 12
INNER = (5, 6, 9, 10)
AHEAD = ((1, 0), (0, 1), (1, 1), (1, -1), (0, -1))
FROM = (((1, 1), (1, 2)), ((1, 1), (2, 1)), ((1, 1),), ((1, 2),), ((2, 2),))
INTO = (((3, 1), (3, 2)), ((1, 3), (2, 3)), ((3, 3),), ((3, 0),), ((2, 0),))
RIM = tuple(4 * x + y for group in INTO for x, y in group)
INNER_PLAN = [
    [(INNER[one], (1, 2))] + [(INNER[other], (0, 1, 2)) for other in range(one + 1, 4)] for one in range(4)
]
OUTER_PLAN = [
    [
        (4 * (1 + x + dx) + 1 + y + dy, (0, 1, 2))
        for dx, dy in ((1, -1), (1, 0), (1, 1), (0, 1))
        if x + dx > 1 or not 0 <= y + dy <= 1
    ]
    for x in range(2)
    for y in range(2)
]
LOG2E = math.log2(math.e)


def two_parts(table):
    table = np.asarray(table, np.float32)
    high = table.astype(jnp.bfloat16)
    low = (table - high.astype(np.float32)).astype(jnp.bfloat16)
    return high, low


def constants(sub_size):
    place = np.zeros((4, 2, 64, 128), np.float32)
    for x in range(2):
        for y in range(2):
            for e in range(7):
                for f in range(7):
                    place[2 * x + y, :, 8 * e + f, 11 * (4 * x + e) + 4 * y + f] = 1.0
    place = place.reshape(512, 128).astype(jnp.bfloat16)
    tap = np.arange(11)
    spread = np.zeros((2, 128, 9, 128), np.float32)
    for number, (width, weight) in enumerate(zip(FINE_WIDTHS, FINE_WEIGHTS)):
        for place_num, (dx, dy) in enumerate(SIDES):
            per_axis = []
            for step in (dx, dy):
                dist = np.abs(tap[None, :] + 8 * step - tap[:, None]).astype(np.float64)
                per_axis.append(np.where(dist <= REACH, np.exp(-dist * dist / (2 * width * width)), 0.0))
            both = weight * np.kron(per_axis[0], per_axis[1])
            spread[number, :121, place_num, :121] = both
    spread = two_parts(spread.reshape(256, 9 * 128))
    ring = np.zeros((2, 16, 16), np.float32)
    for number, width in enumerate(FINE_WIDTHS):
        dist = np.abs(np.arange(12)[:, None] - np.arange(12)[None, :])
        dist = np.minimum(dist, 12 - dist).astype(np.float64)
        ring[number, :12, :12] = np.where(dist <= REACH, np.exp(-dist * dist / (2 * width * width)), 0.0)
    ring = ring.reshape(32, 16)
    select = np.zeros((2, 12, 8, 128), np.float32)
    for y in range(2):
        for x in range(11):
            for f in range(7):
                select[y, x, f, 11 * x + 4 * y + f] = 1.0
    select = select.reshape(192, 128).astype(jnp.bfloat16)
    total_y = 4 * sub_size
    coarse = np.zeros((2, 2, 8, 8, sub_size, 2, 8, 8), np.float32)
    for number, (fraction, weight) in enumerate(zip(COARSE_FRACTIONS, COARSE_WEIGHTS)):
        dist = np.abs(np.arange(6)[:, None] - np.arange(6)[None, :])
        dist = np.minimum(dist, 6 - dist).astype(np.float64)
        along_z = np.exp(-dist * dist / (2 * (6 / fraction) ** 2))
        for step in range(sub_size):
            dist = np.mod(4 * step + np.arange(6)[None, :] - np.arange(6)[:, None], total_y)
            dist = np.minimum(dist, total_y - dist).astype(np.float64)
            along_y = np.exp(-dist * dist / (2 * (total_y / fraction) ** 2))
            both = 0.125 * weight * along_z[:, None, :, None] * along_y[None, :, None, :]
            for half in range(2):
                coarse[half, number, :6, :6, step, half, :6, :6] = both
    coarse = two_parts(coarse.reshape(256, sub_size * 128))
    return place, spread, ring, select, coarse


def halves(value):
    high = value.astype(BF16).astype(F32)
    return high, value - high


def thirds(value):
    high, rest = halves(value)
    middle, low = halves(rest)
    return high, middle, low


def dot(left, right):
    return lax.dot_general(left, right, (((1,), (0,)), ((), ())), preferred_element_type=F32)


def dot_rows(left, right):
    return lax.dot_general(left, right, (((1,), (1,)), ((), ())), preferred_element_type=F32)


def spline(shifted):
    size = jnp.abs(shifted)
    outer = jnp.maximum(2.0 - size, 0.0)
    inner = jnp.maximum(1.0 - size, 0.0)
    return outer * outer * outer * (1.0 / 6.0) - inner * inner * inner * (2.0 / 3.0)


def spline_slope(shifted):
    size = jnp.abs(shifted)
    outer = jnp.maximum(2.0 - size, 0.0)
    inner = jnp.maximum(1.0 - size, 0.0)
    slope = 2.0 * inner * inner - 0.5 * outer * outer
    return jnp.where(shifted < 0.0, -slope, slope)


def wrapped(shifted):
    return jnp.where(shifted > 6.0, shifted - 12.0, jnp.where(shifted < -6.0, shifted + 12.0, shifted))


def grouped(size, step, start, cells=CELLS):
    def group(number, carry):
        for num in range(size):
            carry = step(number * size + num, carry)
        return carry

    return lax.fori_loop(0, cells // size, group, start)


def row_iota(rows, lanes=128):
    return lax.broadcasted_iota(jnp.int32, (rows, lanes), 0)


def kernel(
    spaces, subs,
    pos_hbm, charge_hbm, count_hbm, place_hbm, wide_hi_hbm, wide_lo_hbm, ring_hbm, select_hbm, far_hi_hbm, far_lo_hbm,
    out_ref,
    pos_ref, charge_ref, count_ref, ring_ref, place_ref, wide_hi, wide_lo, select_ref, far_hi, far_lo,
    ext, lap_buf, plane_out, plane_buf, fine_out, fine_buf,
    fine_sum, by_ref, wz_ref, pair_hi, pair_lo, vx_ref, bells_ref, left_ref, right_ref, mom_ref, square_ref, bell_ref, raw_ref, back_ref, return_out, return_buf, force_ref,
    input_sem, const_sem, halo_send, halo_recv, lap_send, lap_recv, relay_send, relay_recv, return_send, return_recv, fine_send, fine_recv, plane_send, plane_recv,
):
    laps = spaces // 4
    space = lax.axis_index("space")
    sub = lax.axis_index("sub")
    outer_x = space // (2 * laps)
    lap = (space // 2) % laps
    core = space % 2

    loads = [
        pltpu.make_async_copy(src, dst, const_sem.at[num])
        for num, (src, dst) in enumerate((
            (place_hbm, place_ref), (wide_hi_hbm, wide_hi), (wide_lo_hbm, wide_lo),
            (select_hbm, select_ref), (far_hi_hbm, far_hi), (far_lo_hbm, far_lo), (ring_hbm, ring_ref),
        ))
    ]
    inputs = [
        pltpu.make_async_copy(src, dst, input_sem.at[num])
        for num, (src, dst) in enumerate(((pos_hbm, pos_ref), (charge_hbm, charge_ref), (count_hbm, count_ref)))
    ]
    for load in inputs:
        load.start()

    def near_id(side):
        return {"space": (space + side[0] + spaces) % spaces, "sub": (sub + side[1] + subs) % subs}

    def lap_id(step):
        return {"space": outer_x * 2 * laps + ((lap + step + laps) % laps) * 2 + core, "sub": sub}

    def plane_id(member, step):
        return {
            "space": ((outer_x + member // 2) % 2) * 2 * laps + lap * 2 + (core + member % 2) % 2,
            "sub": (sub + step) % subs,
        }

    members = [(member, step) for member in range(4) for step in range(subs) if (member, step) != (0, 0)]
    barrier = pltpu.get_barrier_semaphore()
    for side in NEAR:
        pl.semaphore_signal(barrier, inc=1, device_id=near_id(side), device_id_type=MESH)
    for step in LAPS:
        pl.semaphore_signal(barrier, inc=1, device_id=lap_id(step), device_id_type=MESH)
    for member, step in members:
        pl.semaphore_signal(barrier, inc=1, device_id=plane_id(member, step), device_id_type=MESH)

    for load in loads:
        load.start()
    for load in inputs:
        load.wait()
    lane = lax.broadcasted_iota(jnp.int32, (1, 128), 1)
    for x in range(2):
        for y in range(2):
            for z in range(3):
                lanes = pl.ds(128 * z, 128)
                for k in range(3):
                    ext[1 + x, 1 + y, pl.ds(k, 1), lanes] = pos_ref[k, x, z, pl.ds(y, 1), :]
                live = lane < count_ref[x, y, z]
                ext[1 + x, 1 + y, pl.ds(3, 1), lanes] = jnp.where(live, charge_ref[x, z, pl.ds(y, 1), :], 0.0)

    def cell_rows(cell):
        x, y, z = cell // 6, (cell // 3) % 2, cell % 3
        at = 128 * z if isinstance(z, int) else pl.multiple_of(z * 128, 128)
        return x, y, z, ext[1 + x, 1 + y, :, pl.ds(at, 128)]

    def real(value):
        return float(value) if isinstance(value, int) else value.astype(F32)

    def padded(block):
        return jnp.concatenate([block, jnp.zeros_like(block)], axis=0)

    row8 = row_iota(8).astype(F32)
    row16 = row_iota(16).astype(F32)

    row_map = jnp.where(row8 > 3.0, row8 - 1.0, row8)
    row_live = (row8 != 3.0) & (row8 != 7.0)

    def coarse_weights(cell, shape):
        x, y, z, block = cell_rows(cell)
        at_x = 4.0 * block[0:1] + real(4 * x + 2) - 2.0 * row_map
        at_y = 4.0 * block[1:2] + real(4 * y + 2) - 2.0 * row8
        at_z = 4.0 * block[2:3] + real(4 * z) - 2.0 * row8
        vx = jnp.where(row_live, shape(at_x) + shape(at_x - 1.0), 0.0)
        vy = shape(at_y) + shape(at_y - 1.0)
        vz = jnp.where(row8 < 6.0, shape(wrapped(at_z)) + shape(wrapped(at_z - 1.0)), 0.0)
        return vx, vy, vz, block[3:4]

    pad = jnp.zeros((16, 128), F32)
    total = jnp.zeros((16, 256), F32)
    for cell in range(CELLS):
        vx, vy, vz, charge = coarse_weights(cell, spline)
        vz = vz * charge
        high, low = halves(jnp.concatenate([vz[k : k + 1] * vy for k in range(6)], axis=0))
        right = jnp.concatenate([high, pad, high, pad, low, pad, low, pad], axis=0).astype(BF16)
        total = total + dot_rows(jnp.concatenate(halves(vx), axis=0).astype(BF16), right)
    total = total[0:8] + total[8:16]
    total = total[:, 0:128] + total[:, 128:256]
    lap_buf[0] = jnp.where(lane < 64, total[0:4], total[4:8])

    def tables_step(cell, carry):
        vx, vy, vz, charge = coarse_weights(cell, spline)
        sx, sy, sz, charge = coarse_weights(cell, spline_slope)
        lanes = pl.ds(pl.multiple_of(cell * 384, 128), 384)
        tables = jnp.concatenate(
            [
                jnp.concatenate([one[k : k + 1] * other for k in range(6)], axis=0)
                for one, other in ((vz, vy), (vz, sy), (sz, vy))
            ],
            axis=1,
        )
        high, low = halves(tables)
        pair_hi[:, lanes] = high.astype(BF16)
        pair_lo[:, lanes] = low.astype(BF16)
        vx_ref[:, lanes] = jnp.concatenate([sx, vx, vx], axis=1)
        return carry

    pl.semaphore_wait(barrier, len(NEAR) + len(LAPS) + len(members))

    lap_copies = []
    for num, step in enumerate(LAPS):
        copy = pltpu.make_async_remote_copy(
            src_ref=lap_buf.at[0], dst_ref=lap_buf.at[(-step) % laps], send_sem=lap_send.at[num], recv_sem=lap_recv.at[num],
            device_id=lap_id(step), device_id_type=MESH,
        )
        copy.start()
        lap_copies.append(copy)

    halo_copies = []
    for num, side in enumerate(AHEAD):
        (x, y), (to_x, to_y) = FROM[num][0], INTO[num][0]
        span_x, span_y = FROM[num][-1][0] - x + 1, FROM[num][-1][1] - y + 1
        copy = pltpu.make_async_remote_copy(
            src_ref=ext.at[pl.ds(x, span_x), pl.ds(y, span_y)], dst_ref=ext.at[pl.ds(to_x, span_x), pl.ds(to_y, span_y)],
            send_sem=halo_send.at[num], recv_sem=halo_recv.at[num],
            device_id=near_id((-side[0], -side[1])), device_id_type=MESH,
        )
        copy.start()
        halo_copies.append(copy)

    row_w = row_iota(8, 640)
    slot_w = lax.broadcasted_iota(jnp.int32, (8, 640), 1) // 128

    def column_step(column, carry):
        x, y = column // 4, column % 4
        block = ext[x, y]
        block = padded(jnp.concatenate([block[:, 256:384], block, block[:, 0:128]], axis=1))
        shift = jnp.where(
            row_w == 0, (x - 2).astype(F32), jnp.where(row_w == 1, (y - 2).astype(F32), slot_w.astype(F32) - 2.5)
        )
        coords = jnp.where(row_w < 3, SPLIT_RATE * (block + shift), 0.0)
        square = jnp.sum(coords * coords, axis=0, keepdims=True) + SPLIT_RATE * SPLIT_RATE * SOFT_SQUARE
        ones = jnp.where(row_w == 3, 1.0, 0.0)
        p1, p2, p3 = thirds(coords)
        squares_of = thirds(square)
        bells_of = thirds(-LOG2E * square)

        def with_square(part, num):
            return jnp.where(row_w == 4, squares_of[num], jnp.where(row_w == 5, bells_of[num], part + ones))

        right_ref[column] = jnp.concatenate(
            [with_square(p1, 0), with_square(p2, 1), with_square(p1, 2), p3, p2, p1], axis=0
        ).astype(BF16)
        moments = (coords + ones) * block[3:4]
        m1, m2, m3 = thirds(moments)
        mom_ref[column] = jnp.concatenate([m1, m2, m3, jnp.zeros_like(m1)], axis=0).astype(BF16)
        return carry

    for column in (5, 6, 9, 10):
        column_step(jnp.int32(column), 0)

    row_c = row_iota(8)

    def left_step(cell, carry):
        x, y, z, block = cell_rows(cell)
        block = padded(block)
        shift = jnp.where(
            row_c == 0, (x - 1).astype(F32), jnp.where(row_c == 1, (y - 1).astype(F32), z.astype(F32) - 1.5)
        )
        coords = jnp.where(row_c < 3, SPLIT_RATE * (block + shift), 0.0)
        square = jnp.sum(coords * coords, axis=0, keepdims=True)

        def features(cross, own, ones_row):
            ones = jnp.where(row_c == ones_row, 1.0, 0.0)
            p1, p2, p3 = thirds(cross)
            q1, q2, q3 = [jnp.where(row_c == 3, part, ones) for part in thirds(own)]
            return jnp.concatenate([p1 + q1, p1 + q2, p2 + q3, p1, p2, p3, jnp.zeros((80, 128), F32)], axis=0)

        left_ref[cell, 0:128, :] = jnp.transpose(features(-2.0 * coords, square, 4)).astype(BF16)
        bell_own = math.log2(2.0 / math.sqrt(math.pi)) - LOG2E * square
        left_ref[cell, 128:256, :] = jnp.transpose(features((2.0 * LOG2E) * coords, bell_own, 5)).astype(BF16)
        return carry

    grouped(6, left_step, 0)

    def slot_lanes(slot, count=1):
        return pl.ds(pl.multiple_of(slot * 128, 128), 128 * count)

    def squares(plan, z, half):
        at = 0
        for one in range(4):
            left = left_ref[3 * one + z][:, 0:48]
            for column, slots in plan[one]:
                both = dot(left, right_ref[column, :, slot_lanes(z + slots[0], len(slots))])
                lanes = slice(128 * at, 128 * (at + len(slots)))
                square_ref[half, :, lanes] = both[0:128]
                bell_ref[half, :, lanes] = both[128:256]
                at += len(slots)

    def pulls(plan, z, half, first):
        at = 0
        for one in range(4):
            own = INNER[one]
            moments = jnp.zeros((128, 32), F32) if first else raw_ref[3 * one + z]
            for column, slot in [(column, slot) for column, slots in plan[one] for slot in slots]:
                square = square_ref[half, :, 128 * at : 128 * (at + 1)]
                inverse = lax.rsqrt(square)
                far = 1.0 - lax.erf(square * inverse)
                factor = (inverse * inverse) * (far * inverse + jnp.exp2(bell_ref[half, :, 128 * at : 128 * (at + 1)]))
                high = factor.astype(BF16)
                low = (factor - high.astype(F32)).astype(BF16)
                other = mom_ref[column, :, slot_lanes(z + slot)]
                moments = moments + dot_rows(jnp.concatenate([high, low], axis=1), jnp.concatenate([other, other], axis=1))
                if (column, slot) != (own, 1):
                    z_other = (z + slot + 2) % 3
                    back = mom_ref[own, :, slot_lanes(z_other + 2 - slot)]
                    back_ref[3 * column + z_other] += dot(
                        jnp.concatenate([back, back], axis=1), jnp.concatenate([high, low], axis=0)
                    )
                at += 1
            raw_ref[3 * one + z] = moments

    def sweep(plan, start, stop, first):
        squares(plan, start, 0)
        for z in range(start, stop):
            if z + 1 < stop:
                squares(plan, z + 1, (z + 1 - start) % 2)
            pulls(plan, z, (z - start) % 2, first)

    def summed(rows):
        return rows[0:8] + rows[8:16] + rows[16:24]

    def finish(cell):
        x, y, z = cell // 6, (cell // 3) % 2, cell % 3
        block = padded(ext[1 + x, 1 + y, :, 128 * z : 128 * (z + 1)])
        moments = summed(jnp.transpose(raw_ref[cell]) + back_ref[3 * INNER[2 * x + y] + z])
        for num, group in enumerate(FROM):
            for place, column in enumerate(group):
                if column == (1 + x, 1 + y):
                    moments = moments + padded(return_buf[num, place, :, 128 * z : 128 * (z + 1)])
        shift = jnp.where(row_c == 0, x - 1.0, jnp.where(row_c == 1, y - 1.0, z - 1.5))
        coords = SPLIT_RATE * (block + shift)
        force_ref[cell] = (SPLIT_RATE * SPLIT_RATE) * block[3:4] * (coords * moments[3:4] - moments)

    back_ref[...] = jnp.zeros_like(back_ref)
    for one in range(4):
        raw_ref[3 * one + 2] = jnp.zeros((128, 32), F32)
    sweep(INNER_PLAN, 0, 2, True)

    fine_sum[...] = jnp.zeros_like(fine_sum)

    def fine_step(cell, carry):
        x, y, z, block = cell_rows(cell)
        at_x = 4.0 * block[0:1] - (row8 - 1.0)
        at_y = 4.0 * block[1:2] - (row8 - 1.0)
        at_z = wrapped(4.0 * block[2:3] + (4 * z).astype(F32) - row16)
        bx, by = spline(at_x), spline(at_y)
        bz = jnp.where(row16 < 12.0, spline(at_z), 0.0)
        sz = jnp.where(row16 < 12.0, spline_slope(at_z), 0.0)
        by_ref[cell] = jnp.concatenate([bx, spline_slope(at_x), by, spline_slope(at_y)], axis=0)
        bx_charge = bx * block[3:4]
        product = jnp.concatenate([bx_charge[e : e + 1] * by for e in range(7)] + [jnp.zeros((8, 128), F32)], axis=0)
        right = jnp.concatenate(halves(product), axis=0).astype(BF16)
        high, low = halves(jnp.concatenate([bz, sz], axis=1))
        left = jnp.concatenate([high[:, 0:128], low[:, 0:128]], axis=0).astype(BF16)
        wz_ref[cell] = jnp.concatenate([high, high, high, low, low, low], axis=0).astype(BF16)
        fine_sum[cell // 3] += dot_rows(left, right)
        return carry

    grouped(6, fine_step, 0)
    for load in loads:
        load.wait()
    boxes = jnp.concatenate([fine_sum[num, 0:16] + fine_sum[num, 16:32] for num in range(4)], axis=1)
    spots = dot(jnp.concatenate(thirds(boxes), axis=0).astype(BF16), place_ref[...])
    spots = spots[0:16] + spots[16:32] + spots[32:48]
    rings = lax.dot_general(
        ring_ref[...], spots, (((1,), (0,)), ((), ())), precision=HIGHEST, preferred_element_type=F32
    )
    rings = jnp.concatenate([rings[0:16], rings[16:32]], axis=1)
    parts = jnp.concatenate(halves(rings), axis=0).astype(BF16)
    fine_all = dot(parts, wide_hi[...])
    fine_all = fine_all[0:16] + fine_all[16:32] + dot(parts[0:16], wide_lo[...])
    for num in range(9):
        fine_out[num] = fine_all[:, 128 * num : 128 * (num + 1)]
    fine_copies = []
    for num, side in enumerate(NEAR):
        copy = pltpu.make_async_remote_copy(
            src_ref=fine_out.at[SIDES.index(side)], dst_ref=fine_buf.at[num],
            send_sem=fine_send.at[num], recv_sem=fine_recv.at[num], device_id=near_id(side), device_id_type=MESH,
        )
        copy.start()
        fine_copies.append(copy)


    rows = lax.broadcasted_iota(jnp.int32, (128, 64), 0)
    cols = lax.broadcasted_iota(jnp.int32, (128, 64), 1)
    member = (rows // 4) % 4
    to_space = ((outer_x + member // 2) % 2) * 2 * laps + lap * 2 + (core + member % 2) % 2
    from_space = outer_x * 2 * laps + ((lap + cols // 4) % laps) * 2 + core
    total_x = 4 * spaces
    to_row = 3 * ((rows // 16) % 2) + rows % 4
    from_row = 3 * (rows // 64) + cols % 4
    dist = (4 * (to_space - from_space) + to_row - from_row + 2 * total_x) % total_x
    dist = jnp.minimum(dist, total_x - dist).astype(F32)
    wide = [2.0 * (total_x / fraction) ** 2 for fraction in COARSE_FRACTIONS]
    bells = jnp.exp(-dist * dist * jnp.where((rows // 32) % 2 == 0, 1.0 / wide[0], 1.0 / wide[1]))
    bells_ref[...] = jnp.concatenate(halves(bells), axis=0).astype(BF16)

    for copy in lap_copies:
        copy.wait_recv()
    relays = []
    for num, (src, dst, step) in enumerate((
        (pl.ds(1, 4), pl.ds(5, 4), -4),
        (pl.ds(laps - 3, 3), pl.ds(laps - 7, 3), 4),
    )):
        copy = pltpu.make_async_remote_copy(
            src_ref=lap_buf.at[src], dst_ref=lap_buf.at[dst], send_sem=relay_send.at[num], recv_sem=relay_recv.at[num],
            device_id=lap_id(step), device_id_type=MESH,
        )
        copy.start()
        relays.append(copy)

    for copy in halo_copies:
        copy.wait_recv()
    for column in RIM:
        column_step(jnp.int32(column), 0)
    sweep(OUTER_PLAN, 0, 3, False)

    return_copies = []
    for num, side in enumerate(AHEAD):
        shift = jnp.where(row_c == 0, 2.0 * SPLIT_RATE * side[0], jnp.where(row_c == 1, 2.0 * SPLIT_RATE * side[1], 0.0))
        for place, (x, y) in enumerate(INTO[num]):
            for z in range(3):
                moments = summed(back_ref[3 * (4 * x + y) + z])
                return_out[num, place, :, 128 * z : 128 * (z + 1)] = (moments - shift * moments[3:4])[0:4]
        count = len(INTO[num])
        copy = pltpu.make_async_remote_copy(
            src_ref=return_out.at[num, pl.ds(0, count)], dst_ref=return_buf.at[num, pl.ds(0, count)],
            send_sem=return_send.at[num], recv_sem=return_recv.at[num], device_id=near_id(side), device_id_type=MESH,
        )
        copy.start()
        return_copies.append(copy)

    for copy in relays:
        copy.wait_recv()
    gathered = jnp.concatenate([lap_buf[num] for num in range(laps)], axis=0)
    along_x = dot(bells_ref[...], jnp.concatenate(halves(gathered), axis=1).astype(BF16))
    along_x = along_x[0:128, 0:128] + along_x[0:128, 128:256] + along_x[128:256, 0:128]
    turned = pltpu.roll(along_x, 64, 1)
    along_x = jnp.where(lane < 64, along_x[0:32] + turned[64:96], turned[32:64] + along_x[96:128])
    parts = jnp.concatenate(halves(jnp.concatenate([along_x[0:16], along_x[16:32]], axis=1)), axis=0).astype(BF16)
    shares = dot(parts, far_hi[...])
    shares = shares[0:16] + shares[16:32] + dot(parts[0:16], far_lo[...])
    for member_num in range(4):
        for step in range(subs):
            plane_out[member_num * subs + step] = shares[4 * member_num : 4 * member_num + 4, 128 * step : 128 * (step + 1)]
    plane_copies = []
    for member_num, step in members:
        num = member_num * subs + step
        copy = pltpu.make_async_remote_copy(
            src_ref=plane_out.at[num], dst_ref=plane_buf.at[num], send_sem=plane_send.at[num], recv_sem=plane_recv.at[num],
            device_id=plane_id(member_num, step), device_id_type=MESH,
        )
        copy.start()
        plane_copies.append(copy)

    sweep(INNER_PLAN, 2, 3, False)
    grouped(6, tables_step, 0)

    for copy in fine_copies:
        copy.wait_recv()
    fine = fine_out[SIDES.index((0, 0))]
    for num in range(8):
        fine = fine + fine_buf[num]
    pieces = thirds(fine)
    points = dot_rows(select_ref[...], jnp.concatenate(pieces + pieces, axis=0).astype(BF16)).astype(BF16)
    fine_sum_rows = points

    def interpolate(cell, x, y):
        start = 96 * y + 32 * x
        spread = dot(fine_sum_rows[start : start + 64], wz_ref[cell])
        tables = by_ref[cell]
        u1 = jnp.zeros((8, 128), F32)
        u2 = jnp.zeros((8, 128), F32)
        u3 = jnp.zeros((8, 128), F32)
        for e in range(7):
            at = spread[8 * e : 8 * e + 8]
            u1 = u1 + tables[8 + e : 9 + e] * at[:, 0:128]
            u2 = u2 + tables[e : e + 1] * at[:, 0:128]
            u3 = u3 + tables[e : e + 1] * at[:, 128:256]
        by, sy = tables[16:24], tables[24:32]
        return [jnp.sum(one * other, axis=0, keepdims=True) for one, other in ((by, u1), (sy, u2), (by, u3))]

    fine_forces = [interpolate(cell, cell // 6, (cell // 3) % 2) for cell in range(CELLS)]

    for copy in return_copies:
        copy.wait_recv()
    for cell in range(CELLS):
        finish(cell)

    for copy in plane_copies:
        copy.wait_recv()
    window = plane_out[0]
    for member_num, step in members:
        window = window + plane_buf[member_num * subs + step]
    window = jnp.concatenate([window, pltpu.roll(window, 64, 1)], axis=0)
    parts = jnp.concatenate(halves(window), axis=0).astype(BF16)[:, 0:48]
    for cell in range(CELLS):
        x, y, z = cell // 6, (cell // 3) % 2, cell % 3
        lanes = pl.ds(384 * cell, 384)
        spread = dot(parts, pair_hi[:, lanes])
        spread = spread[0:8] + spread[8:16] + dot(parts, pair_lo[:, lanes])[0:8]
        spread = jnp.sum(spread * vx_ref[:, lanes], axis=0, keepdims=True)
        charge = ext[1 + x, 1 + y, pl.ds(3, 1), pl.ds(128 * z, 128)]
        for k in range(3):
            far = fine_forces[cell][k] + spread[:, 128 * k : 128 * (k + 1)]
            out_ref[k, x, z, pl.ds(y, 1), :] = force_ref[cell, pl.ds(k, 1), :] - 4.0 * charge * far

    for copy in lap_copies + halo_copies + fine_copies + relays + return_copies + plane_copies:
        copy.wait_send()


def solution(mesh):
    spaces, subs = mesh.shape["space"], mesh.shape["sub"]
    laps = spaces // 4
    place, spread, ring, select, coarse = constants(subs)

    def body(positions, charges, counts):
        any_spec = pl.BlockSpec(memory_space=pl.ANY)
        vmem_spec = pl.BlockSpec(memory_space=pltpu.VMEM)
        planes = 4 * subs
        positions = jnp.transpose(positions, (0, 1, 3, 2, 4))
        charges = jnp.transpose(charges, (0, 2, 1, 3))
        forces = pl.pallas_call(
            functools.partial(kernel, spaces, subs),
            out_shape=pltpu.VMEM(positions.shape, F32),
            in_specs=[any_spec] * 10,
            out_specs=vmem_spec,
            scratch_shapes=[
                pltpu.VMEM((3, 2, 3, 2, 128), F32),
                pltpu.VMEM((2, 3, 2, 128), F32),
                pltpu.SMEM((2, 2, 3), jnp.int32),
                pltpu.VMEM((32, 16), F32),
                pltpu.VMEM((512, 128), BF16),
                pltpu.VMEM((256, 1152), BF16),
                pltpu.VMEM((256, 1152), BF16),
                pltpu.VMEM((192, 128), BF16),
                pltpu.VMEM((256, 128 * subs), BF16),
                pltpu.VMEM((256, 128 * subs), BF16),
                pltpu.VMEM((4, 4, 4, 384), F32),
                pltpu.VMEM((laps, 4, 128), F32),
                pltpu.VMEM((planes, 4, 128), F32),
                pltpu.VMEM((planes, 4, 128), F32),
                pltpu.VMEM((9, 16, 128), F32),
                pltpu.VMEM((8, 16, 128), F32),
                pltpu.VMEM((4, 32, 128), F32),
                pltpu.VMEM((CELLS, 32, 128), F32),
                pltpu.VMEM((CELLS, 96, 256), BF16),
                pltpu.VMEM((48, CELLS * 384), BF16),
                pltpu.VMEM((48, CELLS * 384), BF16),
                pltpu.VMEM((8, CELLS * 384), F32),
                pltpu.VMEM((256, 64), BF16),
                pltpu.VMEM((CELLS, 256, 128), BF16),
                pltpu.VMEM((16, 48, 640), BF16),
                pltpu.VMEM((16, 32, 640), BF16),
                pltpu.VMEM((2, 128, 3840), F32),
                pltpu.VMEM((2, 128, 3840), F32),
                pltpu.VMEM((CELLS, 128, 32), F32),
                pltpu.VMEM((48, 32, 128), F32),
                pltpu.VMEM((5, 2, 4, 384), F32),
                pltpu.VMEM((5, 2, 4, 384), F32),
                pltpu.VMEM((CELLS, 8, 128), F32),
                pltpu.SemaphoreType.DMA((3,)),
                pltpu.SemaphoreType.DMA((7,)),
                pltpu.SemaphoreType.DMA((5,)),
                pltpu.SemaphoreType.DMA((5,)),
                pltpu.SemaphoreType.DMA((8,)),
                pltpu.SemaphoreType.DMA((8,)),
                pltpu.SemaphoreType.DMA((2,)),
                pltpu.SemaphoreType.DMA((2,)),
                pltpu.SemaphoreType.DMA((5,)),
                pltpu.SemaphoreType.DMA((5,)),
                pltpu.SemaphoreType.DMA((8,)),
                pltpu.SemaphoreType.DMA((8,)),
                pltpu.SemaphoreType.DMA((planes,)),
                pltpu.SemaphoreType.DMA((planes,)),
            ],
            compiler_params=pltpu.CompilerParams(collective_id=0, has_side_effects=True),
        )(
            positions, charges, counts,
            jnp.asarray(place), jnp.asarray(spread[0]), jnp.asarray(spread[1]), jnp.asarray(ring), jnp.asarray(select),
            jnp.asarray(coarse[0]), jnp.asarray(coarse[1]),
        )
        return jnp.transpose(forces, (0, 1, 3, 2, 4))

    in_specs = (
        P(None, "space", "sub", None, None),
        P("space", "sub", None, None),
        P("space", "sub", None),
    )
    out_specs = P(None, "space", "sub", None, None)
    return jax.shard_map(body, mesh=mesh, in_specs=in_specs, out_specs=out_specs, check_vma=False)
```

```python
import functools
import math

import jax
import jax.numpy as jnp
import numpy as np
from jax import lax
from jax.experimental import pallas as pl
from jax.experimental.pallas import tpu as pltpu
from jax.sharding import PartitionSpec as P

F32 = jnp.float32
BF16 = jnp.bfloat16
MESH = pl.DeviceIdType.MESH
HIGHEST = lax.Precision.HIGHEST
SPLIT_RATE = 0.8
SOFT_SQUARE = 0.0625
FINE_WIDTHS = (1.0, 2.0)
FINE_WEIGHTS = (2.0, 0.5)
COARSE_FRACTIONS = (8.0, 4.0)
COARSE_WEIGHTS = (4.0, 2.0)
REACH = 4
SIDES = [(dx, dy) for dx in (-1, 0, 1) for dy in (-1, 0, 1)]
NEAR = [side for side in SIDES if side != (0, 0)]
LAPS = (1, 2, 3, 4, -1, -2, -3, -4)
CELLS = 12
INNER = (5, 6, 9, 10)
AHEAD = ((1, 0), (0, 1), (1, 1), (1, -1), (0, -1))
FROM = (((1, 1), (1, 2)), ((1, 1), (2, 1)), ((1, 1),), ((1, 2),), ((2, 2),))
INTO = (((3, 1), (3, 2)), ((1, 3), (2, 3)), ((3, 3),), ((3, 0),), ((2, 0),))
RIM = tuple(4 * x + y for group in INTO for x, y in group)
INNER_PLAN = [
    [(INNER[one], (1, 2))] + [(INNER[other], (0, 1, 2)) for other in range(one + 1, 4)] for one in range(4)
]
OUTER_PLAN = [
    [
        (4 * (1 + x + dx) + 1 + y + dy, (0, 1, 2))
        for dx, dy in ((1, -1), (1, 0), (1, 1), (0, 1))
        if x + dx > 1 or not 0 <= y + dy <= 1
    ]
    for x in range(2)
    for y in range(2)
]
LOG2E = math.log2(math.e)


def two_parts(table):
    table = np.asarray(table, np.float32)
    high = table.astype(jnp.bfloat16)
    low = (table - high.astype(np.float32)).astype(jnp.bfloat16)
    return high, low


def constants(sub_size):
    place = np.zeros((4, 2, 64, 128), np.float32)
    for x in range(2):
        for y in range(2):
            for e in range(7):
                for f in range(7):
                    place[2 * x + y, :, 8 * e + f, 11 * (4 * x + e) + 4 * y + f] = 1.0
    place = place.reshape(512, 128).astype(jnp.bfloat16)
    tap = np.arange(11)
    spread = np.zeros((2, 128, 9, 128), np.float32)
    for number, (width, weight) in enumerate(zip(FINE_WIDTHS, FINE_WEIGHTS)):
        for place_num, (dx, dy) in enumerate(SIDES):
            per_axis = []
            for step in (dx, dy):
                dist = np.abs(tap[None, :] + 8 * step - tap[:, None]).astype(np.float64)
                per_axis.append(np.where(dist <= REACH, np.exp(-dist * dist / (2 * width * width)), 0.0))
            both = weight * np.kron(per_axis[0], per_axis[1])
            spread[number, :121, place_num, :121] = both
    spread = two_parts(spread.reshape(256, 9 * 128))
    ring = np.zeros((2, 16, 16), np.float32)
    for number, width in enumerate(FINE_WIDTHS):
        dist = np.abs(np.arange(12)[:, None] - np.arange(12)[None, :])
        dist = np.minimum(dist, 12 - dist).astype(np.float64)
        ring[number, :12, :12] = np.where(dist <= REACH, np.exp(-dist * dist / (2 * width * width)), 0.0)
    ring = ring.reshape(32, 16)
    select = np.zeros((2, 12, 8, 128), np.float32)
    for y in range(2):
        for x in range(11):
            for f in range(7):
                select[y, x, f, 11 * x + 4 * y + f] = 1.0
    select = select.reshape(192, 128).astype(jnp.bfloat16)
    total_y = 4 * sub_size
    coarse = np.zeros((2, 2, 8, 8, sub_size, 2, 8, 8), np.float32)
    for number, (fraction, weight) in enumerate(zip(COARSE_FRACTIONS, COARSE_WEIGHTS)):
        dist = np.abs(np.arange(6)[:, None] - np.arange(6)[None, :])
        dist = np.minimum(dist, 6 - dist).astype(np.float64)
        along_z = np.exp(-dist * dist / (2 * (6 / fraction) ** 2))
        for step in range(sub_size):
            dist = np.mod(4 * step + np.arange(6)[None, :] - np.arange(6)[:, None], total_y)
            dist = np.minimum(dist, total_y - dist).astype(np.float64)
            along_y = np.exp(-dist * dist / (2 * (total_y / fraction) ** 2))
            both = 0.125 * weight * along_z[:, None, :, None] * along_y[None, :, None, :]
            for half in range(2):
                coarse[half, number, :6, :6, step, half, :6, :6] = both
    coarse = two_parts(coarse.reshape(256, sub_size * 128))
    return place, spread, ring, select, coarse


def halves(value):
    high = value.astype(BF16).astype(F32)
    return high, value - high


def thirds(value):
    high, rest = halves(value)
    middle, low = halves(rest)
    return high, middle, low


def dot(left, right):
    return lax.dot_general(left, right, (((1,), (0,)), ((), ())), preferred_element_type=F32)


def dot_rows(left, right):
    return lax.dot_general(left, right, (((1,), (1,)), ((), ())), preferred_element_type=F32)


def spline(shifted):
    size = jnp.abs(shifted)
    outer = jnp.maximum(2.0 - size, 0.0)
    inner = jnp.maximum(1.0 - size, 0.0)
    return outer * outer * outer * (1.0 / 6.0) - inner * inner * inner * (2.0 / 3.0)


def spline_slope(shifted):
    size = jnp.abs(shifted)
    outer = jnp.maximum(2.0 - size, 0.0)
    inner = jnp.maximum(1.0 - size, 0.0)
    slope = 2.0 * inner * inner - 0.5 * outer * outer
    return jnp.where(shifted < 0.0, -slope, slope)


def wrapped(shifted):
    return jnp.where(shifted > 6.0, shifted - 12.0, jnp.where(shifted < -6.0, shifted + 12.0, shifted))


def grouped(size, step, start, cells=CELLS):
    def group(number, carry):
        for num in range(size):
            carry = step(number * size + num, carry)
        return carry

    return lax.fori_loop(0, cells // size, group, start)


def row_iota(rows, lanes=128):
    return lax.broadcasted_iota(jnp.int32, (rows, lanes), 0)


def kernel(
    spaces, subs,
    pos_hbm, charge_hbm, count_hbm, place_hbm, wide_hi_hbm, wide_lo_hbm, ring_hbm, select_hbm, far_hi_hbm, far_lo_hbm,
    out_ref,
    pos_ref, charge_ref, count_ref, ring_ref, place_ref, wide_hi, wide_lo, select_ref, far_hi, far_lo,
    ext, lap_buf, plane_out, plane_buf, fine_out, fine_buf,
    fine_sum, by_ref, wz_ref, pair_hi, pair_lo, vx_ref, bells_ref, left_ref, right_ref, mom_ref, square_ref, raw_ref, back_ref, return_out, return_buf, force_ref,
    input_sem, const_sem, halo_send, halo_recv, lap_send, lap_recv, relay_send, relay_recv, return_send, return_recv, fine_send, fine_recv, plane_send, plane_recv,
):
    laps = spaces // 4
    space = lax.axis_index("space")
    sub = lax.axis_index("sub")
    outer_x = space // (2 * laps)
    lap = (space // 2) % laps
    core = space % 2

    loads = [
        pltpu.make_async_copy(src, dst, const_sem.at[num])
        for num, (src, dst) in enumerate((
            (place_hbm, place_ref), (wide_hi_hbm, wide_hi), (wide_lo_hbm, wide_lo),
            (select_hbm, select_ref), (far_hi_hbm, far_hi), (far_lo_hbm, far_lo), (ring_hbm, ring_ref),
        ))
    ]
    inputs = [
        pltpu.make_async_copy(src, dst, input_sem.at[num])
        for num, (src, dst) in enumerate(((pos_hbm, pos_ref), (charge_hbm, charge_ref), (count_hbm, count_ref)))
    ]
    for load in inputs:
        load.start()

    def near_id(side):
        return {"space": (space + side[0] + spaces) % spaces, "sub": (sub + side[1] + subs) % subs}

    def lap_id(step):
        return {"space": outer_x * 2 * laps + ((lap + step + laps) % laps) * 2 + core, "sub": sub}

    def plane_id(member, step):
        return {
            "space": ((outer_x + member // 2) % 2) * 2 * laps + lap * 2 + (core + member % 2) % 2,
            "sub": (sub + step) % subs,
        }

    members = [(member, step) for member in range(4) for step in range(subs) if (member, step) != (0, 0)]
    barrier = pltpu.get_barrier_semaphore()
    for step in sorted(LAPS, key=abs, reverse=True):
        pl.semaphore_signal(barrier, inc=1, device_id=lap_id(step), device_id_type=MESH)
    for member, step in sorted(members, key=lambda one: min(one[1], subs - one[1]), reverse=True):
        pl.semaphore_signal(barrier, inc=1, device_id=plane_id(member, step), device_id_type=MESH)
    for side in NEAR:
        pl.semaphore_signal(barrier, inc=1, device_id=near_id(side), device_id_type=MESH)

    for load in loads:
        load.start()
    for load in inputs:
        load.wait()
    lane = lax.broadcasted_iota(jnp.int32, (1, 128), 1)
    for x in range(2):
        for y in range(2):
            for z in range(3):
                lanes = pl.ds(128 * z, 128)
                for k in range(3):
                    ext[1 + x, 1 + y, pl.ds(k, 1), lanes] = pos_ref[k, x, z, pl.ds(y, 1), :]
                live = lane < count_ref[x, y, z]
                ext[1 + x, 1 + y, pl.ds(3, 1), lanes] = jnp.where(live, charge_ref[x, z, pl.ds(y, 1), :], 0.0)

    def cell_rows(cell):
        x, y, z = cell // 6, (cell // 3) % 2, cell % 3
        at = 128 * z if isinstance(z, int) else pl.multiple_of(z * 128, 128)
        return x, y, z, ext[1 + x, 1 + y, :, pl.ds(at, 128)]

    def real(value):
        return float(value) if isinstance(value, int) else value.astype(F32)

    def padded(block):
        return jnp.concatenate([block, jnp.zeros_like(block)], axis=0)

    row8 = row_iota(8).astype(F32)
    row16 = row_iota(16).astype(F32)

    row_map = jnp.where(row8 > 3.0, row8 - 1.0, row8)
    row_live = (row8 != 3.0) & (row8 != 7.0)

    def coarse_weights(cell, shape):
        x, y, z, block = cell_rows(cell)
        at_x = 4.0 * block[0:1] + real(4 * x + 2) - 2.0 * row_map
        at_y = 4.0 * block[1:2] + real(4 * y + 2) - 2.0 * row8
        at_z = 4.0 * block[2:3] + real(4 * z) - 2.0 * row8
        vx = jnp.where(row_live, shape(at_x) + shape(at_x - 1.0), 0.0)
        vy = shape(at_y) + shape(at_y - 1.0)
        vz = jnp.where(row8 < 6.0, shape(wrapped(at_z)) + shape(wrapped(at_z - 1.0)), 0.0)
        return vx, vy, vz, block[3:4]

    pad = jnp.zeros((16, 128), F32)
    total = jnp.zeros((16, 128), F32)
    for cell in range(CELLS):
        vx, vy, vz, charge = coarse_weights(cell, spline)
        vz = vz * charge
        high, low = halves(jnp.concatenate([vz[k : k + 1] * vy for k in range(6)], axis=0))
        right = jnp.concatenate([high, pad, low, pad], axis=0).astype(BF16)
        total = total + dot_rows(jnp.concatenate(halves(vx), axis=0).astype(BF16), right)
    total = total[0:8] + total[8:16]
    total = total + pltpu.roll(total, 64, 1)
    lap_buf[0] = jnp.where(lane < 64, total[0:4], total[4:8])

    def tables_step(cell, carry):
        vx, vy, vz, charge = coarse_weights(cell, spline)
        sx, sy, sz, charge = coarse_weights(cell, spline_slope)
        lanes = pl.ds(pl.multiple_of(cell * 384, 128), 384)
        tables = jnp.concatenate(
            [
                jnp.concatenate([one[k : k + 1] * other for k in range(6)], axis=0)
                for one, other in ((vz, vy), (vz, sy), (sz, vy))
            ],
            axis=1,
        )
        high, low = halves(tables)
        pair_hi[:, lanes] = high.astype(BF16)
        pair_lo[:, lanes] = low.astype(BF16)
        vx_ref[:, lanes] = jnp.concatenate([sx, vx, vx], axis=1)
        return carry

    row_w = row_iota(8, 640)
    slot_w = lax.broadcasted_iota(jnp.int32, (8, 640), 1) // 128

    def column_step(column, carry):
        x, y = column // 4, column % 4
        block = ext[x, y]
        block = padded(jnp.concatenate([block[:, 256:384], block, block[:, 0:128]], axis=1))
        shift = jnp.where(
            row_w == 0, (x - 2).astype(F32), jnp.where(row_w == 1, (y - 2).astype(F32), slot_w.astype(F32) - 2.5)
        )
        coords = jnp.where(row_w < 3, SPLIT_RATE * (block + shift), 0.0)
        square = jnp.sum(coords * coords, axis=0, keepdims=True) + SPLIT_RATE * SPLIT_RATE * SOFT_SQUARE
        ones = jnp.where(row_w == 3, 1.0, 0.0)
        p1, p2, p3 = thirds(coords)
        squares_of = thirds(square)

        def with_square(part, num):
            return jnp.where(row_w == 4, squares_of[num], part + ones)

        right_ref[column] = jnp.concatenate(
            [with_square(p1, 0), with_square(p2, 1), with_square(p1, 2), p3, p2, p1], axis=0
        ).astype(BF16)
        moments = (coords + ones) * block[3:4]
        m1, m2, m3 = thirds(moments)
        mom_ref[column] = jnp.concatenate([m1, m2, m3, jnp.zeros_like(m1)], axis=0).astype(BF16)
        return carry

    for column in (5, 6, 9, 10):
        column_step(jnp.int32(column), 0)

    row_c = row_iota(8)

    def left_step(cell, carry):
        x, y, z, block = cell_rows(cell)
        block = padded(block)
        shift = jnp.where(
            row_c == 0, real(x - 1), jnp.where(row_c == 1, real(y - 1), real(z) - 1.5)
        )
        coords = jnp.where(row_c < 3, SPLIT_RATE * (block + shift), 0.0)
        square = jnp.sum(coords * coords, axis=0, keepdims=True)

        ones = jnp.where(row_c == 4, 1.0, 0.0)
        p1, p2, p3 = thirds(-2.0 * coords)
        q1, q2, q3 = [jnp.where(row_c == 3, part, ones) for part in thirds(square)]
        stacked = jnp.concatenate([p1 + q1, p1 + q2, p2 + q3, p1, p2, p3, jnp.zeros((80, 128), F32)], axis=0)
        left_ref[cell] = jnp.transpose(stacked).astype(BF16)
        return carry

    for cell in range(CELLS):
        left_step(cell, 0)

    def slot_lanes(slot, count=1):
        return pl.ds(pl.multiple_of(slot * 128, 128), 128 * count)

    def squares(plan, z, half):
        at = 0
        for one in range(4):
            left = left_ref[3 * one + z][:, 0:48]
            for column, slots in plan[one]:
                square_ref[half, :, 128 * at : 128 * (at + len(slots))] = dot(
                    left, right_ref[column, :, slot_lanes(z + slots[0], len(slots))]
                )
                at += len(slots)

    def pulls(plan, z, half, first):
        at = 0
        for one in range(4):
            own = INNER[one]
            moments = jnp.zeros((128, 32), F32) if first else raw_ref[3 * one + z]
            for column, slot in [(column, slot) for column, slots in plan[one] for slot in slots]:
                square = square_ref[half, :, 128 * at : 128 * (at + 1)]
                inverse = lax.rsqrt(square)
                far = 1.0 - lax.erf(square * inverse)
                bell = (2.0 / math.sqrt(math.pi)) * jnp.exp2(square * -LOG2E)
                factor = (inverse * inverse) * (far * inverse + bell)
                high = factor.astype(BF16)
                low = (factor - high.astype(F32)).astype(BF16)
                other = mom_ref[column, :, slot_lanes(z + slot)]
                moments = moments + dot_rows(jnp.concatenate([high, low], axis=1), jnp.concatenate([other, other], axis=1))
                if (column, slot) != (own, 1):
                    z_other = (z + slot + 2) % 3
                    back = mom_ref[own, :, slot_lanes(z_other + 2 - slot)]
                    back_ref[3 * column + z_other] += dot(
                        jnp.concatenate([back, back], axis=1), jnp.concatenate([high, low], axis=0)
                    )
                at += 1
            raw_ref[3 * one + z] = moments

    def sweep(plan, start, stop, first):
        squares(plan, start, 0)
        for z in range(start, stop):
            if z + 1 < stop:
                squares(plan, z + 1, (z + 1 - start) % 2)
            pulls(plan, z, (z - start) % 2, first)

    def summed(rows):
        return rows[0:8] + rows[8:16] + rows[16:24]

    def finish(cell):
        x, y, z = cell // 6, (cell // 3) % 2, cell % 3
        block = padded(ext[1 + x, 1 + y, :, 128 * z : 128 * (z + 1)])
        moments = summed(jnp.transpose(raw_ref[cell]) + back_ref[3 * INNER[2 * x + y] + z])
        for num, group in enumerate(FROM):
            for place, column in enumerate(group):
                if column == (1 + x, 1 + y):
                    moments = moments + padded(return_buf[num, place, :, 128 * z : 128 * (z + 1)])
        shift = jnp.where(row_c == 0, x - 1.0, jnp.where(row_c == 1, y - 1.0, z - 1.5))
        coords = SPLIT_RATE * (block + shift)
        force_ref[cell] = (SPLIT_RATE * SPLIT_RATE) * block[3:4] * (coords * moments[3:4] - moments)

    fine_sum[...] = jnp.zeros_like(fine_sum)

    def fine_step(cell, carry):
        x, y, z, block = cell_rows(cell)
        at_x = 4.0 * block[0:1] - (row8 - 1.0)
        at_y = 4.0 * block[1:2] - (row8 - 1.0)
        at_z = wrapped(4.0 * block[2:3] + real(4 * z) - row16)
        bx, by = spline(at_x), spline(at_y)
        bz = jnp.where(row16 < 12.0, spline(at_z), 0.0)
        sz = jnp.where(row16 < 12.0, spline_slope(at_z), 0.0)
        by_ref[cell] = jnp.concatenate([bx, spline_slope(at_x), by, spline_slope(at_y)], axis=0)
        bx_charge = bx * block[3:4]
        product = jnp.concatenate([bx_charge[e : e + 1] * by for e in range(7)] + [jnp.zeros((8, 128), F32)], axis=0)
        right = jnp.concatenate(halves(product), axis=0).astype(BF16)
        high, low = halves(jnp.concatenate([bz, sz], axis=1))
        left = jnp.concatenate([high[:, 0:128], low[:, 0:128]], axis=0).astype(BF16)
        wz_ref[cell] = jnp.concatenate([high, high, high, low, low, low], axis=0).astype(BF16)
        fine_sum[cell // 3] += dot_rows(left, right)
        return carry

    for cell in range(CELLS):
        fine_step(cell, 0)
    for load in loads:
        load.wait()
    boxes = jnp.concatenate([fine_sum[num, 0:16] + fine_sum[num, 16:32] for num in range(4)], axis=1)
    spots = dot(jnp.concatenate(thirds(boxes), axis=0).astype(BF16), place_ref[...])
    spots = spots[0:16] + spots[16:32] + spots[32:48]
    rings = lax.dot_general(
        ring_ref[...], spots, (((1,), (0,)), ((), ())), precision=HIGHEST, preferred_element_type=F32
    )
    rings = jnp.concatenate([rings[0:16], rings[16:32]], axis=1)
    parts = jnp.concatenate(halves(rings), axis=0).astype(BF16)
    fine_all = dot(parts, wide_hi[...])
    fine_all = fine_all[0:16] + fine_all[16:32] + dot(parts[0:16], wide_lo[...])
    for num in range(9):
        fine_out[num] = fine_all[:, 128 * num : 128 * (num + 1)]
    rows = lax.broadcasted_iota(jnp.int32, (128, 64), 0)
    cols = lax.broadcasted_iota(jnp.int32, (128, 64), 1)
    member = (rows // 4) % 4
    to_space = ((outer_x + member // 2) % 2) * 2 * laps + lap * 2 + (core + member % 2) % 2
    from_space = outer_x * 2 * laps + ((lap + cols // 4) % laps) * 2 + core
    total_x = 4 * spaces
    to_row = 3 * ((rows // 16) % 2) + rows % 4
    from_row = 3 * (rows // 64) + cols % 4
    dist = (4 * (to_space - from_space) + to_row - from_row + 2 * total_x) % total_x
    dist = jnp.minimum(dist, total_x - dist).astype(F32)
    wide = [2.0 * (total_x / fraction) ** 2 for fraction in COARSE_FRACTIONS]
    bells = jnp.exp(-dist * dist * jnp.where((rows // 32) % 2 == 0, 1.0 / wide[0], 1.0 / wide[1]))
    bells_ref[...] = jnp.concatenate(halves(bells), axis=0).astype(BF16)

    back_ref[...] = jnp.zeros_like(back_ref)
    for one in range(4):
        raw_ref[3 * one + 2] = jnp.zeros((128, 32), F32)

    pl.semaphore_wait(barrier, len(NEAR) + len(LAPS) + len(members))

    for num, step in enumerate(LAPS):
        copy = pltpu.make_async_remote_copy(
            src_ref=lap_buf.at[0], dst_ref=lap_buf.at[(-step) % laps], send_sem=lap_send.at[0], recv_sem=lap_recv.at[num // 4],
            device_id=lap_id(step), device_id_type=MESH,
        )
        copy.start()

    halo_copies = []
    for num, side in enumerate(AHEAD):
        (x, y), (to_x, to_y) = FROM[num][0], INTO[num][0]
        span_x, span_y = FROM[num][-1][0] - x + 1, FROM[num][-1][1] - y + 1
        copy = pltpu.make_async_remote_copy(
            src_ref=ext.at[pl.ds(x, span_x), pl.ds(y, span_y)], dst_ref=ext.at[pl.ds(to_x, span_x), pl.ds(to_y, span_y)],
            send_sem=halo_send.at[num], recv_sem=halo_recv.at[num],
            device_id=near_id((-side[0], -side[1])), device_id_type=MESH,
        )
        copy.start()
        halo_copies.append(copy)

    for num, side in enumerate(NEAR):
        copy = pltpu.make_async_remote_copy(
            src_ref=fine_out.at[SIDES.index(side)], dst_ref=fine_buf.at[num],
            send_sem=fine_send.at[0], recv_sem=fine_recv.at[0], device_id=near_id(side), device_id_type=MESH,
        )
        copy.start()


    sweep(INNER_PLAN, 0, 2, True)

    for num, start in enumerate((laps - 4, 1)):
        pltpu.make_async_remote_copy(
            src_ref=lap_buf.at[pl.ds(start, 4)], dst_ref=lap_buf.at[pl.ds(start, 4)], send_sem=lap_send.at[0], recv_sem=lap_recv.at[num],
            device_id=lap_id(1), device_id_type=MESH,
        ).wait_recv()
    relays = []
    for num, (src, dst, step) in enumerate((
        (pl.ds(1, 4), pl.ds(5, 4), -4),
        (pl.ds(laps - 3, 3), pl.ds(laps - 7, 3), 4),
    )):
        copy = pltpu.make_async_remote_copy(
            src_ref=lap_buf.at[src], dst_ref=lap_buf.at[dst], send_sem=relay_send.at[num], recv_sem=relay_recv.at[num],
            device_id=lap_id(step), device_id_type=MESH,
        )
        copy.start()
        relays.append(copy)

    for copy in halo_copies:
        copy.wait_recv()
    for column in RIM:
        column_step(jnp.int32(column), 0)
    sweep(OUTER_PLAN, 0, 3, False)

    return_copies = []
    for num, side in enumerate(AHEAD):
        shift = jnp.where(row_c == 0, 2.0 * SPLIT_RATE * side[0], jnp.where(row_c == 1, 2.0 * SPLIT_RATE * side[1], 0.0))
        for place, (x, y) in enumerate(INTO[num]):
            for z in range(3):
                moments = summed(back_ref[3 * (4 * x + y) + z])
                return_out[num, place, :, 128 * z : 128 * (z + 1)] = (moments - shift * moments[3:4])[0:4]
        count = len(INTO[num])
        copy = pltpu.make_async_remote_copy(
            src_ref=return_out.at[num, pl.ds(0, count)], dst_ref=return_buf.at[num, pl.ds(0, count)],
            send_sem=return_send.at[num], recv_sem=return_recv.at[num], device_id=near_id(side), device_id_type=MESH,
        )
        copy.start()
        return_copies.append(copy)

    for copy in relays:
        copy.wait_recv()
    gathered = jnp.concatenate([lap_buf[num] for num in range(laps)], axis=0)
    along_x = dot(bells_ref[...], jnp.concatenate(halves(gathered), axis=1).astype(BF16))
    along_x = along_x[0:128, 0:128] + along_x[0:128, 128:256] + along_x[128:256, 0:128]
    turned = pltpu.roll(along_x, 64, 1)
    along_x = jnp.where(lane < 64, along_x[0:32] + turned[64:96], turned[32:64] + along_x[96:128])
    parts = jnp.concatenate(halves(jnp.concatenate([along_x[0:16], along_x[16:32]], axis=1)), axis=0).astype(BF16)
    shares = dot(parts, far_hi[...])
    shares = shares[0:16] + shares[16:32] + dot(parts[0:16], far_lo[...])
    for member_num in range(4):
        for step in range(subs):
            plane_out[member_num * subs + step] = shares[4 * member_num : 4 * member_num + 4, 128 * step : 128 * (step + 1)]
    for member_num, step in members:
        num = member_num * subs + step
        copy = pltpu.make_async_remote_copy(
            src_ref=plane_out.at[num], dst_ref=plane_buf.at[num], send_sem=plane_send.at[0], recv_sem=plane_recv.at[0],
            device_id=plane_id(member_num, step), device_id_type=MESH,
        )
        copy.start()


    sweep(INNER_PLAN, 2, 3, False)
    grouped(6, tables_step, 0)

    fine_all_in = pltpu.make_async_remote_copy(
        src_ref=fine_buf, dst_ref=fine_buf, send_sem=fine_send.at[0], recv_sem=fine_recv.at[0], device_id=near_id((0, 1)), device_id_type=MESH,
    )
    fine_all_in.wait_recv()
    fine = fine_out[SIDES.index((0, 0))]
    for num in range(8):
        fine = fine + fine_buf[num]
    pieces = thirds(fine)
    points = dot_rows(select_ref[...], jnp.concatenate(pieces + pieces, axis=0).astype(BF16)).astype(BF16)
    fine_sum_rows = points

    def interpolate(cell, x, y):
        start = 96 * y + 32 * x
        spread = dot(fine_sum_rows[start : start + 64], wz_ref[cell])
        tables = by_ref[cell]
        u1 = jnp.zeros((8, 128), F32)
        u2 = jnp.zeros((8, 128), F32)
        u3 = jnp.zeros((8, 128), F32)
        for e in range(7):
            at = spread[8 * e : 8 * e + 8]
            u1 = u1 + tables[8 + e : 9 + e] * at[:, 0:128]
            u2 = u2 + tables[e : e + 1] * at[:, 0:128]
            u3 = u3 + tables[e : e + 1] * at[:, 128:256]
        by, sy = tables[16:24], tables[24:32]
        return [jnp.sum(one * other, axis=0, keepdims=True) for one, other in ((by, u1), (sy, u2), (by, u3))]

    fine_forces = [interpolate(cell, cell // 6, (cell // 3) % 2) for cell in range(CELLS)]

    for copy in return_copies:
        copy.wait_recv()
    for cell in range(CELLS):
        finish(cell)

    plane_all_in = pltpu.make_async_remote_copy(
        src_ref=plane_out.at[pl.ds(1, 4 * subs - 1)], dst_ref=plane_buf.at[pl.ds(1, 4 * subs - 1)], send_sem=plane_send.at[0], recv_sem=plane_recv.at[0], device_id=plane_id(0, 1), device_id_type=MESH,
    )
    plane_all_in.wait_recv()
    window = plane_out[0]
    for member_num, step in members:
        window = window + plane_buf[member_num * subs + step]
    window = jnp.concatenate([window, pltpu.roll(window, 64, 1)], axis=0)
    parts = jnp.concatenate(halves(window), axis=0).astype(BF16)[:, 0:48]
    for cell in range(CELLS):
        x, y, z = cell // 6, (cell // 3) % 2, cell % 3
        lanes = pl.ds(384 * cell, 384)
        spread = dot(parts, pair_hi[:, lanes])
        spread = spread[0:8] + spread[8:16] + dot(parts, pair_lo[:, lanes])[0:8]
        spread = jnp.sum(spread * vx_ref[:, lanes], axis=0, keepdims=True)
        charge = ext[1 + x, 1 + y, pl.ds(3, 1), pl.ds(128 * z, 128)]
        for k in range(3):
            far = fine_forces[cell][k] + spread[:, 128 * k : 128 * (k + 1)]
            out_ref[k, x, z, pl.ds(y, 1), :] = force_ref[cell, pl.ds(k, 1), :] - 4.0 * charge * far

    lap_all_out = pltpu.make_async_remote_copy(
        src_ref=lap_buf.at[pl.ds(0, 8)], dst_ref=lap_buf.at[pl.ds(0, 8)], send_sem=lap_send.at[0], recv_sem=lap_recv.at[0], device_id=lap_id(1), device_id_type=MESH,
    )
    lap_all_out.wait_send()
    fine_all_in.wait_send()
    plane_all_in.wait_send()
    for copy in halo_copies + relays + return_copies:
        copy.wait_send()


def solution(mesh):
    spaces, subs = mesh.shape["space"], mesh.shape["sub"]
    laps = spaces // 4
    place, spread, ring, select, coarse = constants(subs)

    def body(positions, charges, counts):
        any_spec = pl.BlockSpec(memory_space=pl.ANY)
        vmem_spec = pl.BlockSpec(memory_space=pltpu.VMEM)
        planes = 4 * subs
        positions = jnp.transpose(positions, (0, 1, 3, 2, 4))
        charges = jnp.transpose(charges, (0, 2, 1, 3))
        forces = pl.pallas_call(
            functools.partial(kernel, spaces, subs),
            out_shape=pltpu.VMEM(positions.shape, F32),
            in_specs=[any_spec] * 10,
            out_specs=vmem_spec,
            scratch_shapes=[
                pltpu.VMEM((3, 2, 3, 2, 128), F32),
                pltpu.VMEM((2, 3, 2, 128), F32),
                pltpu.SMEM((2, 2, 3), jnp.int32),
                pltpu.VMEM((32, 16), F32),
                pltpu.VMEM((512, 128), BF16),
                pltpu.VMEM((256, 1152), BF16),
                pltpu.VMEM((256, 1152), BF16),
                pltpu.VMEM((192, 128), BF16),
                pltpu.VMEM((256, 128 * subs), BF16),
                pltpu.VMEM((256, 128 * subs), BF16),
                pltpu.VMEM((4, 4, 4, 384), F32),
                pltpu.VMEM((laps, 4, 128), F32),
                pltpu.VMEM((planes, 4, 128), F32),
                pltpu.VMEM((planes, 4, 128), F32),
                pltpu.VMEM((9, 16, 128), F32),
                pltpu.VMEM((8, 16, 128), F32),
                pltpu.VMEM((4, 32, 128), F32),
                pltpu.VMEM((CELLS, 32, 128), F32),
                pltpu.VMEM((CELLS, 96, 256), BF16),
                pltpu.VMEM((48, CELLS * 384), BF16),
                pltpu.VMEM((48, CELLS * 384), BF16),
                pltpu.VMEM((8, CELLS * 384), F32),
                pltpu.VMEM((256, 64), BF16),
                pltpu.VMEM((CELLS, 128, 128), BF16),
                pltpu.VMEM((16, 48, 640), BF16),
                pltpu.VMEM((16, 32, 640), BF16),
                pltpu.VMEM((2, 128, 3840), F32),
                pltpu.VMEM((CELLS, 128, 32), F32),
                pltpu.VMEM((48, 32, 128), F32),
                pltpu.VMEM((5, 2, 4, 384), F32),
                pltpu.VMEM((5, 2, 4, 384), F32),
                pltpu.VMEM((CELLS, 8, 128), F32),
                pltpu.SemaphoreType.DMA((3,)),
                pltpu.SemaphoreType.DMA((7,)),
                pltpu.SemaphoreType.DMA((5,)),
                pltpu.SemaphoreType.DMA((5,)),
                pltpu.SemaphoreType.DMA((1,)),
                pltpu.SemaphoreType.DMA((2,)),
                pltpu.SemaphoreType.DMA((2,)),
                pltpu.SemaphoreType.DMA((2,)),
                pltpu.SemaphoreType.DMA((5,)),
                pltpu.SemaphoreType.DMA((5,)),
                pltpu.SemaphoreType.DMA((1,)),
                pltpu.SemaphoreType.DMA((1,)),
                pltpu.SemaphoreType.DMA((1,)),
                pltpu.SemaphoreType.DMA((1,)),
            ],
            compiler_params=pltpu.CompilerParams(collective_id=0, has_side_effects=True),
        )(
            positions, charges, counts,
            jnp.asarray(place), jnp.asarray(spread[0]), jnp.asarray(spread[1]), jnp.asarray(ring), jnp.asarray(select),
            jnp.asarray(coarse[0]), jnp.asarray(coarse[1]),
        )
        return jnp.transpose(forces, (0, 1, 3, 2, 4))

    in_specs = (
        P(None, "space", "sub", None, None),
        P("space", "sub", None, None),
        P("space", "sub", None),
    )
    out_specs = P(None, "space", "sub", None, None)
    return jax.shard_map(body, mesh=mesh, in_specs=in_specs, out_specs=out_specs, check_vma=False)
```

```python
import functools
import math

import jax
import jax.numpy as jnp
import numpy as np
from jax import lax
from jax.experimental import pallas as pl
from jax.experimental.pallas import tpu as pltpu
from jax.sharding import PartitionSpec as P

F32 = jnp.float32
BF16 = jnp.bfloat16
MESH = pl.DeviceIdType.MESH
HIGHEST = lax.Precision.HIGHEST
SPLIT_RATE = 0.8
SOFT_SQUARE = 0.0625
FINE_WIDTHS = (1.0, 2.0)
FINE_WEIGHTS = (2.0, 0.5)
COARSE_FRACTIONS = (8.0, 4.0)
COARSE_WEIGHTS = (4.0, 2.0)
REACH = 4
SIDES = [(dx, dy) for dx in (-1, 0, 1) for dy in (-1, 0, 1)]
NEAR = [side for side in SIDES if side != (0, 0)]
LAPS = (1, 2, 3, 4, -1, -2, -3, -4)
CELLS = 12
INNER = (5, 6, 9, 10)
AHEAD = ((1, 0), (0, 1), (1, 1), (1, -1), (0, -1))
FROM = (((1, 1), (1, 2)), ((1, 1), (2, 1)), ((1, 1),), ((1, 2),), ((2, 2),))
INTO = (((3, 1), (3, 2)), ((1, 3), (2, 3)), ((3, 3),), ((3, 0),), ((2, 0),))
RIM = tuple(4 * x + y for group in INTO for x, y in group)
INNER_PLAN = [
    [(INNER[one], (1, 2))] + [(INNER[other], (0, 1, 2)) for other in range(one + 1, 4)] for one in range(4)
]
OUTER_PLAN = [
    [
        (4 * (1 + x + dx) + 1 + y + dy, (0, 1, 2))
        for dx, dy in ((1, -1), (1, 0), (1, 1), (0, 1))
        if x + dx > 1 or not 0 <= y + dy <= 1
    ]
    for x in range(2)
    for y in range(2)
]
LOG2E = math.log2(math.e)


def two_parts(table):
    table = np.asarray(table, np.float32)
    high = table.astype(jnp.bfloat16)
    low = (table - high.astype(np.float32)).astype(jnp.bfloat16)
    return high, low


def constants(sub_size):
    place = np.zeros((4, 2, 64, 128), np.float32)
    for x in range(2):
        for y in range(2):
            for e in range(7):
                for f in range(7):
                    place[2 * x + y, :, 8 * e + f, 11 * (4 * x + e) + 4 * y + f] = 1.0
    place = place.reshape(512, 128).astype(jnp.bfloat16)
    tap = np.arange(11)
    spread = np.zeros((2, 128, 9, 128), np.float32)
    for number, (width, weight) in enumerate(zip(FINE_WIDTHS, FINE_WEIGHTS)):
        for place_num, (dx, dy) in enumerate(SIDES):
            per_axis = []
            for step in (dx, dy):
                dist = np.abs(tap[None, :] + 8 * step - tap[:, None]).astype(np.float64)
                per_axis.append(np.where(dist <= REACH, np.exp(-dist * dist / (2 * width * width)), 0.0))
            both = weight * np.kron(per_axis[0], per_axis[1])
            spread[number, :121, place_num, :121] = both
    spread = two_parts(spread.reshape(256, 9 * 128))
    ring = np.zeros((2, 16, 16), np.float32)
    for number, width in enumerate(FINE_WIDTHS):
        dist = np.abs(np.arange(12)[:, None] - np.arange(12)[None, :])
        dist = np.minimum(dist, 12 - dist).astype(np.float64)
        ring[number, :12, :12] = np.where(dist <= REACH, np.exp(-dist * dist / (2 * width * width)), 0.0)
    ring = ring.reshape(32, 16)
    select = np.zeros((2, 12, 8, 128), np.float32)
    for y in range(2):
        for x in range(11):
            for f in range(7):
                select[y, x, f, 11 * x + 4 * y + f] = 1.0
    select = select.reshape(192, 128).astype(jnp.bfloat16)
    total_y = 4 * sub_size
    coarse = np.zeros((2, 2, 8, 8, sub_size, 2, 8, 8), np.float32)
    for number, (fraction, weight) in enumerate(zip(COARSE_FRACTIONS, COARSE_WEIGHTS)):
        dist = np.abs(np.arange(6)[:, None] - np.arange(6)[None, :])
        dist = np.minimum(dist, 6 - dist).astype(np.float64)
        along_z = np.exp(-dist * dist / (2 * (6 / fraction) ** 2))
        for step in range(sub_size):
            dist = np.mod(4 * step + np.arange(6)[None, :] - np.arange(6)[:, None], total_y)
            dist = np.minimum(dist, total_y - dist).astype(np.float64)
            along_y = np.exp(-dist * dist / (2 * (total_y / fraction) ** 2))
            both = 0.125 * weight * along_z[:, None, :, None] * along_y[None, :, None, :]
            for half in range(2):
                coarse[half, number, :6, :6, step, half, :6, :6] = both
    coarse = two_parts(coarse.reshape(256, sub_size * 128))
    return place, spread, ring, select, coarse


def halves(value):
    high = value.astype(BF16).astype(F32)
    return high, value - high


def thirds(value):
    high, rest = halves(value)
    middle, low = halves(rest)
    return high, middle, low


def dot(left, right):
    return lax.dot_general(left, right, (((1,), (0,)), ((), ())), preferred_element_type=F32)


def dot_rows(left, right):
    return lax.dot_general(left, right, (((1,), (1,)), ((), ())), preferred_element_type=F32)


def spline(shifted):
    size = jnp.abs(shifted)
    outer = jnp.maximum(2.0 - size, 0.0)
    inner = jnp.maximum(1.0 - size, 0.0)
    return outer * outer * outer * (1.0 / 6.0) - inner * inner * inner * (2.0 / 3.0)


def spline_slope(shifted):
    size = jnp.abs(shifted)
    outer = jnp.maximum(2.0 - size, 0.0)
    inner = jnp.maximum(1.0 - size, 0.0)
    slope = 2.0 * inner * inner - 0.5 * outer * outer
    return jnp.where(shifted < 0.0, -slope, slope)


def wrapped(shifted):
    return jnp.where(shifted > 6.0, shifted - 12.0, jnp.where(shifted < -6.0, shifted + 12.0, shifted))


def grouped(size, step, start, cells=CELLS):
    def group(number, carry):
        for num in range(size):
            carry = step(number * size + num, carry)
        return carry

    return lax.fori_loop(0, cells // size, group, start)


def row_iota(rows, lanes=128):
    return lax.broadcasted_iota(jnp.int32, (rows, lanes), 0)


def kernel(
    spaces, subs,
    pos_hbm, charge_hbm, count_hbm, place_hbm, wide_hi_hbm, wide_lo_hbm, ring_hbm, select_hbm, far_hi_hbm, far_lo_hbm,
    out_ref,
    pos_ref, charge_ref, count_ref, ring_ref, place_ref, wide_hi, wide_lo, select_ref, far_hi, far_lo,
    ext, lap_buf, plane_out, plane_buf, fine_out, fine_buf,
    fine_sum, by_ref, wz_ref, pair_hi, pair_lo, vx_ref, bells_ref, left_ref, right_ref, mom_ref, square_ref, raw_ref, back_ref, return_out, return_buf, seven_ref, force_ref,
    input_sem, const_sem, halo_send, halo_recv, lap_send, lap_recv, relay_send, relay_recv, return_send, return_recv, fine_send, fine_recv, plane_send, plane_recv,
):
    laps = spaces // 4
    space = lax.axis_index("space")
    sub = lax.axis_index("sub")
    outer_x = space // (2 * laps)
    lap = (space // 2) % laps
    core = space % 2

    loads = [
        pltpu.make_async_copy(src, dst, const_sem.at[num])
        for num, (src, dst) in enumerate((
            (place_hbm, place_ref), (wide_hi_hbm, wide_hi), (wide_lo_hbm, wide_lo),
            (select_hbm, select_ref), (far_hi_hbm, far_hi), (far_lo_hbm, far_lo), (ring_hbm, ring_ref),
        ))
    ]
    inputs = [
        pltpu.make_async_copy(src, dst, input_sem.at[num])
        for num, (src, dst) in enumerate(((pos_hbm, pos_ref), (charge_hbm, charge_ref), (count_hbm, count_ref)))
    ]
    for load in inputs:
        load.start()

    def near_id(side):
        return {"space": (space + side[0] + spaces) % spaces, "sub": (sub + side[1] + subs) % subs}

    def lap_id(step):
        return {"space": outer_x * 2 * laps + ((lap + step + laps) % laps) * 2 + core, "sub": sub}

    def plane_id(member, step):
        return {
            "space": ((outer_x + member // 2) % 2) * 2 * laps + lap * 2 + (core + member % 2) % 2,
            "sub": (sub + step) % subs,
        }

    members = [(member, step) for member in range(4) for step in range(subs) if (member, step) != (0, 0)]
    barrier = pltpu.get_barrier_semaphore()
    for step in sorted(LAPS, key=abs, reverse=True):
        pl.semaphore_signal(barrier, inc=1, device_id=lap_id(step), device_id_type=MESH)
    for member, step in sorted(members, key=lambda one: min(one[1], subs - one[1]), reverse=True):
        pl.semaphore_signal(barrier, inc=1, device_id=plane_id(member, step), device_id_type=MESH)
    for side in NEAR:
        pl.semaphore_signal(barrier, inc=1, device_id=near_id(side), device_id_type=MESH)

    for load in loads:
        load.start()
    for load in inputs:
        load.wait()
    lane = lax.broadcasted_iota(jnp.int32, (1, 128), 1)
    for x in range(2):
        for y in range(2):
            for z in range(3):
                lanes = pl.ds(128 * z, 128)
                for k in range(3):
                    ext[1 + x, 1 + y, pl.ds(k, 1), lanes] = pos_ref[k, x, z, pl.ds(y, 1), :]
                live = lane < count_ref[x, y, z]
                ext[1 + x, 1 + y, pl.ds(3, 1), lanes] = jnp.where(live, charge_ref[x, z, pl.ds(y, 1), :], 0.0)

    def cell_rows(cell):
        x, y, z = cell // 6, (cell // 3) % 2, cell % 3
        at = 128 * z if isinstance(z, int) else pl.multiple_of(z * 128, 128)
        return x, y, z, ext[1 + x, 1 + y, :, pl.ds(at, 128)]

    def real(value):
        return float(value) if isinstance(value, int) else value.astype(F32)

    def padded(block):
        return jnp.concatenate([block, jnp.zeros_like(block)], axis=0)

    row8 = row_iota(8).astype(F32)
    row16 = row_iota(16).astype(F32)

    row_map = jnp.where(row8 > 3.0, row8 - 1.0, row8)
    row_live = (row8 != 3.0) & (row8 != 7.0)

    def coarse_weights(cell, shape):
        x, y, z, block = cell_rows(cell)
        at_x = 4.0 * block[0:1] + real(4 * x + 2) - 2.0 * row_map
        at_y = 4.0 * block[1:2] + real(4 * y + 2) - 2.0 * row8
        at_z = 4.0 * block[2:3] + real(4 * z) - 2.0 * row8
        vx = jnp.where(row_live, shape(at_x) + shape(at_x - 1.0), 0.0)
        vy = shape(at_y) + shape(at_y - 1.0)
        vz = jnp.where(row8 < 6.0, shape(wrapped(at_z)) + shape(wrapped(at_z - 1.0)), 0.0)
        return vx, vy, vz, block[3:4]

    pad = jnp.zeros((16, 128), F32)
    total = jnp.zeros((16, 128), F32)
    for cell in range(CELLS):
        vx, vy, vz, charge = coarse_weights(cell, spline)
        vz = vz * charge
        high, low = halves(jnp.concatenate([vz[k : k + 1] * vy for k in range(6)], axis=0))
        right = jnp.concatenate([high, pad, low, pad], axis=0).astype(BF16)
        total = total + dot_rows(jnp.concatenate(halves(vx), axis=0).astype(BF16), right)
    total = total[0:8] + total[8:16]
    total = total + pltpu.roll(total, 64, 1)
    lap_buf[0] = jnp.where(lane < 64, total[0:4], total[4:8])

    def tables_step(cell, carry):
        vx, vy, vz, charge = coarse_weights(cell, spline)
        sx, sy, sz, charge = coarse_weights(cell, spline_slope)
        lanes = pl.ds(pl.multiple_of(cell * 384, 128), 384)
        tables = jnp.concatenate(
            [
                jnp.concatenate([one[k : k + 1] * other for k in range(6)], axis=0)
                for one, other in ((vz, vy), (vz, sy), (sz, vy))
            ],
            axis=1,
        )
        high, low = halves(tables)
        pair_hi[:, lanes] = high.astype(BF16)
        pair_lo[:, lanes] = low.astype(BF16)
        vx_ref[:, lanes] = jnp.concatenate([sx, vx, vx], axis=1)
        return carry

    row_w = row_iota(8, 640)
    slot_w = lax.broadcasted_iota(jnp.int32, (8, 640), 1) // 128

    def column_step(column, carry):
        x, y = column // 4, column % 4
        block = ext[x, y]
        block = padded(jnp.concatenate([block[:, 256:384], block, block[:, 0:128]], axis=1))
        shift = jnp.where(
            row_w == 0, (x - 2).astype(F32), jnp.where(row_w == 1, (y - 2).astype(F32), slot_w.astype(F32) - 2.5)
        )
        coords = jnp.where(row_w < 3, SPLIT_RATE * (block + shift), 0.0)
        square = jnp.sum(coords * coords, axis=0, keepdims=True) + SPLIT_RATE * SPLIT_RATE * SOFT_SQUARE
        ones = jnp.where(row_w == 3, 1.0, 0.0)
        p1, p2, p3 = thirds(coords)
        squares_of = thirds(square)

        def with_square(part, num):
            return jnp.where(row_w == 4, squares_of[num], part + ones)

        right_ref[column] = jnp.concatenate(
            [with_square(p1, 0), with_square(p2, 1), with_square(p1, 2), p3, p2, p1], axis=0
        ).astype(BF16)
        moments = (coords + ones) * block[3:4]
        m1, m2, m3 = thirds(moments)
        mom_ref[column] = jnp.concatenate([m1, m2, m3, jnp.zeros_like(m1)], axis=0).astype(BF16)
        return carry

    for column in (5, 6, 9, 10):
        column_step(jnp.int32(column), 0)

    row_c = row_iota(8)

    def left_step(cell, carry):
        x, y, z, block = cell_rows(cell)
        block = padded(block)
        shift = jnp.where(
            row_c == 0, real(x - 1), jnp.where(row_c == 1, real(y - 1), real(z) - 1.5)
        )
        coords = jnp.where(row_c < 3, SPLIT_RATE * (block + shift), 0.0)
        square = jnp.sum(coords * coords, axis=0, keepdims=True)

        ones = jnp.where(row_c == 4, 1.0, 0.0)
        p1, p2, p3 = thirds(-2.0 * coords)
        q1, q2, q3 = [jnp.where(row_c == 3, part, ones) for part in thirds(square)]
        stacked = jnp.concatenate([p1 + q1, p1 + q2, p2 + q3, p1, p2, p3, jnp.zeros((80, 128), F32)], axis=0)
        left_ref[cell] = jnp.transpose(stacked).astype(BF16)
        return carry

    for cell in range(CELLS):
        left_step(cell, 0)

    def slot_lanes(slot, count=1):
        return pl.ds(pl.multiple_of(slot * 128, 128), 128 * count)

    def squares(plan, z, half):
        at = 0
        for one in range(4):
            left = left_ref[3 * one + z][:, 0:48]
            for column, slots in plan[one]:
                square_ref[half, :, 128 * at : 128 * (at + len(slots))] = dot(
                    left, right_ref[column, :, slot_lanes(z + slots[0], len(slots))]
                )
                at += len(slots)

    def pulls(plan, z, half, first):
        at = 0
        for one in range(4):
            own = INNER[one]
            moments = jnp.zeros((128, 32), F32) if first else raw_ref[3 * one + z]
            for column, slot in [(column, slot) for column, slots in plan[one] for slot in slots]:
                square = square_ref[half, :, 128 * at : 128 * (at + 1)]
                inverse = lax.rsqrt(square)
                far = 1.0 - lax.erf(square * inverse)
                bell = (2.0 / math.sqrt(math.pi)) * jnp.exp2(square * -LOG2E)
                factor = (inverse * inverse) * (far * inverse + bell)
                high = factor.astype(BF16)
                low = (factor - high.astype(F32)).astype(BF16)
                other = mom_ref[column, :, slot_lanes(z + slot)]
                moments = moments + dot_rows(jnp.concatenate([high, low], axis=1), jnp.concatenate([other, other], axis=1))
                if (column, slot) != (own, 1):
                    z_other = (z + slot + 2) % 3
                    back = mom_ref[own, :, slot_lanes(z_other + 2 - slot)]
                    back_ref[3 * column + z_other] += dot(
                        jnp.concatenate([back, back], axis=1), jnp.concatenate([high, low], axis=0)
                    )
                at += 1
            raw_ref[3 * one + z] = moments

    def sweep(plan, start, stop, first):
        squares(plan, start, 0)
        for z in range(start, stop):
            if z + 1 < stop:
                squares(plan, z + 1, (z + 1 - start) % 2)
            pulls(plan, z, (z - start) % 2, first)

    def summed(rows):
        return rows[0:8] + rows[8:16] + rows[16:24]

    def finish(cell):
        x, y, z = cell // 6, (cell // 3) % 2, cell % 3
        block = padded(ext[1 + x, 1 + y, :, 128 * z : 128 * (z + 1)])
        moments = summed(jnp.transpose(raw_ref[cell]) + back_ref[3 * INNER[2 * x + y] + z])
        for num, group in enumerate(FROM):
            for place, column in enumerate(group):
                if column == (1 + x, 1 + y):
                    moments = moments + padded(return_buf[num, place, :, 128 * z : 128 * (z + 1)])
        shift = jnp.where(row_c == 0, x - 1.0, jnp.where(row_c == 1, y - 1.0, z - 1.5))
        coords = SPLIT_RATE * (block + shift)
        force_ref[cell] = (SPLIT_RATE * SPLIT_RATE) * block[3:4] * (coords * moments[3:4] - moments)

    rows = lax.broadcasted_iota(jnp.int32, (128, 64), 0)
    cols = lax.broadcasted_iota(jnp.int32, (128, 64), 1)
    member = (rows // 4) % 4
    to_space = ((outer_x + member // 2) % 2) * 2 * laps + lap * 2 + (core + member % 2) % 2
    from_space = outer_x * 2 * laps + ((lap + cols // 4) % laps) * 2 + core
    total_x = 4 * spaces
    to_row = 3 * ((rows // 16) % 2) + rows % 4
    from_row = 3 * (rows // 64) + cols % 4
    dist = (4 * (to_space - from_space) + to_row - from_row + 2 * total_x) % total_x
    dist = jnp.minimum(dist, total_x - dist).astype(F32)
    wide = [2.0 * (total_x / fraction) ** 2 for fraction in COARSE_FRACTIONS]
    bells = jnp.exp(-dist * dist * jnp.where((rows // 32) % 2 == 0, 1.0 / wide[0], 1.0 / wide[1]))
    bells_ref[...] = jnp.concatenate(halves(bells), axis=0).astype(BF16)

    back_ref[...] = jnp.zeros_like(back_ref)
    for one in range(4):
        raw_ref[3 * one + 2] = jnp.zeros((128, 32), F32)

    pl.semaphore_wait(barrier, len(NEAR) + len(LAPS) + len(members))

    for num, step in sorted(enumerate(LAPS), key=lambda one: -abs(one[1])):
        copy = pltpu.make_async_remote_copy(
            src_ref=lap_buf.at[0], dst_ref=lap_buf.at[(-step) % laps], send_sem=lap_send.at[0], recv_sem=lap_recv.at[num // 4],
            device_id=lap_id(step), device_id_type=MESH,
        )
        copy.start()

    for num, side in enumerate(AHEAD):
        (x, y), (to_x, to_y) = FROM[num][0], INTO[num][0]
        span_x, span_y = FROM[num][-1][0] - x + 1, FROM[num][-1][1] - y + 1
        copy = pltpu.make_async_remote_copy(
            src_ref=ext.at[pl.ds(x, span_x), pl.ds(y, span_y)], dst_ref=ext.at[pl.ds(to_x, span_x), pl.ds(to_y, span_y)],
            send_sem=halo_send.at[0], recv_sem=halo_recv.at[0],
            device_id=near_id((-side[0], -side[1])), device_id_type=MESH,
        )
        copy.start()

    fine_sum[...] = jnp.zeros_like(fine_sum)

    def fine_step(cell, carry):
        x, y, z, block = cell_rows(cell)
        at_x = 4.0 * block[0:1] - (row8 - 1.0)
        at_y = 4.0 * block[1:2] - (row8 - 1.0)
        at_z = wrapped(4.0 * block[2:3] + real(4 * z) - row16)
        bx, by = spline(at_x), spline(at_y)
        bz = jnp.where(row16 < 12.0, spline(at_z), 0.0)
        sz = jnp.where(row16 < 12.0, spline_slope(at_z), 0.0)
        by_ref[cell] = jnp.concatenate([bx, spline_slope(at_x), by, spline_slope(at_y)], axis=0)
        bx_charge = bx * block[3:4]
        product = jnp.concatenate([bx_charge[e : e + 1] * by for e in range(7)] + [jnp.zeros((8, 128), F32)], axis=0)
        right = jnp.concatenate(halves(product), axis=0).astype(BF16)
        high, low = halves(jnp.concatenate([bz, sz], axis=1))
        left = jnp.concatenate([high[:, 0:128], low[:, 0:128]], axis=0).astype(BF16)
        wz_ref[cell] = jnp.concatenate([high, high, high, low, low, low], axis=0).astype(BF16)
        fine_sum[cell // 3] += dot_rows(left, right)
        return carry

    for cell in range(CELLS):
        fine_step(cell, 0)
    for load in loads:
        load.wait()
    boxes = jnp.concatenate([fine_sum[num, 0:16] + fine_sum[num, 16:32] for num in range(4)], axis=1)
    spots = dot(jnp.concatenate(thirds(boxes), axis=0).astype(BF16), place_ref[...])
    spots = spots[0:16] + spots[16:32] + spots[32:48]
    rings = lax.dot_general(
        ring_ref[...], spots, (((1,), (0,)), ((), ())), precision=HIGHEST, preferred_element_type=F32
    )
    rings = jnp.concatenate([rings[0:16], rings[16:32]], axis=1)
    parts = jnp.concatenate(halves(rings), axis=0).astype(BF16)
    fine_all = dot(parts, wide_hi[...])
    fine_all = fine_all[0:16] + fine_all[16:32] + dot(parts[0:16], wide_lo[...])
    for num in range(9):
        fine_out[num] = fine_all[:, 128 * num : 128 * (num + 1)]
    for num, side in enumerate(NEAR):
        copy = pltpu.make_async_remote_copy(
            src_ref=fine_out.at[SIDES.index(side)], dst_ref=fine_buf.at[num],
            send_sem=fine_send.at[0], recv_sem=fine_recv.at[0], device_id=near_id(side), device_id_type=MESH,
        )
        copy.start()


    sweep(INNER_PLAN, 0, 2, True)

    for num, start in enumerate((laps - 4, 1)):
        pltpu.make_async_remote_copy(
            src_ref=lap_buf.at[pl.ds(start, 4)], dst_ref=lap_buf.at[pl.ds(start, 4)], send_sem=lap_send.at[0], recv_sem=lap_recv.at[num],
            device_id=lap_id(1), device_id_type=MESH,
        ).wait_recv()
    relays = []
    for num, (src, dst, step) in enumerate((
        (pl.ds(1, 4), pl.ds(5, 4), -4),
        (pl.ds(laps - 3, 3), pl.ds(laps - 7, 3), 4),
    )):
        copy = pltpu.make_async_remote_copy(
            src_ref=lap_buf.at[src], dst_ref=lap_buf.at[dst], send_sem=relay_send.at[num], recv_sem=relay_recv.at[num],
            device_id=lap_id(step), device_id_type=MESH,
        )
        copy.start()
        relays.append(copy)

    halo_all = pltpu.make_async_remote_copy(
        src_ref=seven_ref, dst_ref=seven_ref, send_sem=halo_send.at[0], recv_sem=halo_recv.at[0],
        device_id=near_id((0, 1)), device_id_type=MESH,
    )
    halo_all.wait_recv()
    for column in RIM:
        column_step(jnp.int32(column), 0)
    sweep(OUTER_PLAN, 0, 3, False)

    for num, side in enumerate(AHEAD):
        shift = jnp.where(row_c == 0, 2.0 * SPLIT_RATE * side[0], jnp.where(row_c == 1, 2.0 * SPLIT_RATE * side[1], 0.0))
        for place, (x, y) in enumerate(INTO[num]):
            for z in range(3):
                moments = summed(back_ref[3 * (4 * x + y) + z])
                return_out[num, place, :, 128 * z : 128 * (z + 1)] = (moments - shift * moments[3:4])[0:4]
        count = len(INTO[num])
        copy = pltpu.make_async_remote_copy(
            src_ref=return_out.at[num, pl.ds(0, count)], dst_ref=return_buf.at[num, pl.ds(0, count)],
            send_sem=return_send.at[0], recv_sem=return_recv.at[0], device_id=near_id(side), device_id_type=MESH,
        )
        copy.start()

    for copy in relays:
        copy.wait_recv()
    gathered = jnp.concatenate([lap_buf[num] for num in range(laps)], axis=0)
    along_x = dot(bells_ref[...], jnp.concatenate(halves(gathered), axis=1).astype(BF16))
    along_x = along_x[0:128, 0:128] + along_x[0:128, 128:256] + along_x[128:256, 0:128]
    turned = pltpu.roll(along_x, 64, 1)
    along_x = jnp.where(lane < 64, along_x[0:32] + turned[64:96], turned[32:64] + along_x[96:128])
    parts = jnp.concatenate(halves(jnp.concatenate([along_x[0:16], along_x[16:32]], axis=1)), axis=0).astype(BF16)
    shares = dot(parts, far_hi[...])
    shares = shares[0:16] + shares[16:32] + dot(parts[0:16], far_lo[...])
    for member_num in range(4):
        for step in range(subs):
            plane_out[member_num * subs + step] = shares[4 * member_num : 4 * member_num + 4, 128 * step : 128 * (step + 1)]
    for member_num, step in sorted(members, key=lambda one: -min(one[1], subs - one[1])):
        num = member_num * subs + step
        copy = pltpu.make_async_remote_copy(
            src_ref=plane_out.at[num], dst_ref=plane_buf.at[num], send_sem=plane_send.at[0], recv_sem=plane_recv.at[0],
            device_id=plane_id(member_num, step), device_id_type=MESH,
        )
        copy.start()


    sweep(INNER_PLAN, 2, 3, False)
    grouped(6, tables_step, 0)

    fine_all_in = pltpu.make_async_remote_copy(
        src_ref=fine_buf, dst_ref=fine_buf, send_sem=fine_send.at[0], recv_sem=fine_recv.at[0], device_id=near_id((0, 1)), device_id_type=MESH,
    )
    fine_all_in.wait_recv()
    fine = fine_out[SIDES.index((0, 0))]
    for num in range(8):
        fine = fine + fine_buf[num]
    pieces = thirds(fine)
    points = dot_rows(select_ref[...], jnp.concatenate(pieces + pieces, axis=0).astype(BF16)).astype(BF16)
    fine_sum_rows = points

    def interpolate(cell, x, y):
        start = 96 * y + 32 * x
        spread = dot(fine_sum_rows[start : start + 64], wz_ref[cell])
        tables = by_ref[cell]
        u1 = jnp.zeros((8, 128), F32)
        u2 = jnp.zeros((8, 128), F32)
        u3 = jnp.zeros((8, 128), F32)
        for e in range(7):
            at = spread[8 * e : 8 * e + 8]
            u1 = u1 + tables[8 + e : 9 + e] * at[:, 0:128]
            u2 = u2 + tables[e : e + 1] * at[:, 0:128]
            u3 = u3 + tables[e : e + 1] * at[:, 128:256]
        by, sy = tables[16:24], tables[24:32]
        return [jnp.sum(one * other, axis=0, keepdims=True) for one, other in ((by, u1), (sy, u2), (by, u3))]

    fine_forces = [interpolate(cell, cell // 6, (cell // 3) % 2) for cell in range(CELLS)]

    return_all = pltpu.make_async_remote_copy(
        src_ref=seven_ref, dst_ref=seven_ref, send_sem=return_send.at[0], recv_sem=return_recv.at[0],
        device_id=near_id((0, 1)), device_id_type=MESH,
    )
    return_all.wait_recv()
    for cell in range(CELLS):
        finish(cell)

    plane_all_in = pltpu.make_async_remote_copy(
        src_ref=plane_out.at[pl.ds(1, 4 * subs - 1)], dst_ref=plane_buf.at[pl.ds(1, 4 * subs - 1)], send_sem=plane_send.at[0], recv_sem=plane_recv.at[0], device_id=plane_id(0, 1), device_id_type=MESH,
    )
    plane_all_in.wait_recv()
    pieces = [plane_out[0]] + [plane_buf[member_num * subs + step] for member_num, step in members]
    while len(pieces) > 1:
        pieces = [sum(pieces[num : num + 2][1:], pieces[num]) for num in range(0, len(pieces), 2)]
    window = pieces[0]
    window = jnp.concatenate([window, pltpu.roll(window, 64, 1)], axis=0)
    parts = jnp.concatenate(halves(window), axis=0).astype(BF16)[:, 0:48]
    for cell in range(CELLS):
        x, y, z = cell // 6, (cell // 3) % 2, cell % 3
        lanes = pl.ds(384 * cell, 384)
        spread = dot(parts, pair_hi[:, lanes])
        spread = spread[0:8] + spread[8:16] + dot(parts, pair_lo[:, lanes])[0:8]
        spread = jnp.sum(spread * vx_ref[:, lanes], axis=0, keepdims=True)
        charge = ext[1 + x, 1 + y, pl.ds(3, 1), pl.ds(128 * z, 128)]
        for k in range(3):
            far = fine_forces[cell][k] + spread[:, 128 * k : 128 * (k + 1)]
            out_ref[k, x, z, pl.ds(y, 1), :] = force_ref[cell, pl.ds(k, 1), :] - 4.0 * charge * far

    lap_all_out = pltpu.make_async_remote_copy(
        src_ref=lap_buf.at[pl.ds(0, 8)], dst_ref=lap_buf.at[pl.ds(0, 8)], send_sem=lap_send.at[0], recv_sem=lap_recv.at[0], device_id=lap_id(1), device_id_type=MESH,
    )
    lap_all_out.wait_send()
    fine_all_in.wait_send()
    plane_all_in.wait_send()
    halo_all.wait_send()
    return_all.wait_send()
    for copy in relays:
        copy.wait_send()


def solution(mesh):
    spaces, subs = mesh.shape["space"], mesh.shape["sub"]
    laps = spaces // 4
    place, spread, ring, select, coarse = constants(subs)

    def body(positions, charges, counts):
        any_spec = pl.BlockSpec(memory_space=pl.ANY)
        vmem_spec = pl.BlockSpec(memory_space=pltpu.VMEM)
        planes = 4 * subs
        positions = jnp.transpose(positions, (0, 1, 3, 2, 4))
        charges = jnp.transpose(charges, (0, 2, 1, 3))
        forces = pl.pallas_call(
            functools.partial(kernel, spaces, subs),
            out_shape=pltpu.VMEM(positions.shape, F32),
            in_specs=[any_spec] * 10,
            out_specs=vmem_spec,
            scratch_shapes=[
                pltpu.VMEM((3, 2, 3, 2, 128), F32),
                pltpu.VMEM((2, 3, 2, 128), F32),
                pltpu.SMEM((2, 2, 3), jnp.int32),
                pltpu.VMEM((32, 16), F32),
                pltpu.VMEM((512, 128), BF16),
                pltpu.VMEM((256, 1152), BF16),
                pltpu.VMEM((256, 1152), BF16),
                pltpu.VMEM((192, 128), BF16),
                pltpu.VMEM((256, 128 * subs), BF16),
                pltpu.VMEM((256, 128 * subs), BF16),
                pltpu.VMEM((4, 4, 4, 384), F32),
                pltpu.VMEM((laps, 4, 128), F32),
                pltpu.VMEM((planes, 4, 128), F32),
                pltpu.VMEM((planes, 4, 128), F32),
                pltpu.VMEM((9, 16, 128), F32),
                pltpu.VMEM((8, 16, 128), F32),
                pltpu.VMEM((4, 32, 128), F32),
                pltpu.VMEM((CELLS, 32, 128), F32),
                pltpu.VMEM((CELLS, 96, 256), BF16),
                pltpu.VMEM((48, CELLS * 384), BF16),
                pltpu.VMEM((48, CELLS * 384), BF16),
                pltpu.VMEM((8, CELLS * 384), F32),
                pltpu.VMEM((256, 64), BF16),
                pltpu.VMEM((CELLS, 128, 128), BF16),
                pltpu.VMEM((16, 48, 640), BF16),
                pltpu.VMEM((16, 32, 640), BF16),
                pltpu.VMEM((2, 128, 3840), F32),
                pltpu.VMEM((CELLS, 128, 32), F32),
                pltpu.VMEM((48, 32, 128), F32),
                pltpu.VMEM((5, 2, 4, 384), F32),
                pltpu.VMEM((5, 2, 4, 384), F32),
                pltpu.VMEM((7, 4, 384), F32),
                pltpu.VMEM((CELLS, 8, 128), F32),
                pltpu.SemaphoreType.DMA((3,)),
                pltpu.SemaphoreType.DMA((7,)),
                pltpu.SemaphoreType.DMA((1,)),
                pltpu.SemaphoreType.DMA((1,)),
                pltpu.SemaphoreType.DMA((1,)),
                pltpu.SemaphoreType.DMA((2,)),
                pltpu.SemaphoreType.DMA((2,)),
                pltpu.SemaphoreType.DMA((2,)),
                pltpu.SemaphoreType.DMA((1,)),
                pltpu.SemaphoreType.DMA((1,)),
                pltpu.SemaphoreType.DMA((1,)),
                pltpu.SemaphoreType.DMA((1,)),
                pltpu.SemaphoreType.DMA((1,)),
                pltpu.SemaphoreType.DMA((1,)),
            ],
            compiler_params=pltpu.CompilerParams(collective_id=0, has_side_effects=True),
        )(
            positions, charges, counts,
            jnp.asarray(place), jnp.asarray(spread[0]), jnp.asarray(spread[1]), jnp.asarray(ring), jnp.asarray(select),
            jnp.asarray(coarse[0]), jnp.asarray(coarse[1]),
        )
        return jnp.transpose(forces, (0, 1, 3, 2, 4))

    in_specs = (
        P(None, "space", "sub", None, None),
        P("space", "sub", None, None),
        P("space", "sub", None),
    )
    out_specs = P(None, "space", "sub", None, None)
    return jax.shard_map(body, mesh=mesh, in_specs=in_specs, out_specs=out_specs, check_vma=False)
```

```python
import functools
import math

import jax
import jax.numpy as jnp
import numpy as np
from jax import lax
from jax.experimental import pallas as pl
from jax.experimental.pallas import tpu as pltpu
from jax.sharding import PartitionSpec as P

F32 = jnp.float32
BF16 = jnp.bfloat16
MESH = pl.DeviceIdType.MESH
HIGHEST = lax.Precision.HIGHEST
SPLIT_RATE = 0.8
SOFT_SQUARE = 0.0625
FINE_WIDTHS = (1.0, 2.0)
FINE_WEIGHTS = (2.0, 0.5)
COARSE_FRACTIONS = (8.0, 4.0)
COARSE_WEIGHTS = (4.0, 2.0)
REACH = 4
SIDES = [(dx, dy) for dx in (-1, 0, 1) for dy in (-1, 0, 1)]
NEAR = [side for side in SIDES if side != (0, 0)]
LAPS = (1, 2, 3, 4, -1, -2, -3, -4)
CELLS = 12
INNER = (5, 6, 9, 10)
AHEAD = ((1, 0), (0, 1), (1, 1), (1, -1), (0, -1))
FROM = (((1, 1), (1, 2)), ((1, 1), (2, 1)), ((1, 1),), ((1, 2),), ((2, 2),))
INTO = (((3, 1), (3, 2)), ((1, 3), (2, 3)), ((3, 3),), ((3, 0),), ((2, 0),))
RIM = tuple(4 * x + y for group in INTO for x, y in group)
INNER_PLAN = [
    [(INNER[one], (1, 2))] + [(INNER[other], (0, 1, 2)) for other in range(one + 1, 4)] for one in range(4)
]
OUTER_PLAN = [
    [
        (4 * (1 + x + dx) + 1 + y + dy, (0, 1, 2))
        for dx, dy in ((1, -1), (1, 0), (1, 1), (0, 1))
        if x + dx > 1 or not 0 <= y + dy <= 1
    ]
    for x in range(2)
    for y in range(2)
]
LOG2E = math.log2(math.e)


def two_parts(table):
    table = np.asarray(table, np.float32)
    high = table.astype(jnp.bfloat16)
    low = (table - high.astype(np.float32)).astype(jnp.bfloat16)
    return high, low


def constants(sub_size):
    place = np.zeros((4, 2, 64, 128), np.float32)
    for x in range(2):
        for y in range(2):
            for e in range(7):
                for f in range(7):
                    place[2 * x + y, :, 8 * e + f, 11 * (4 * x + e) + 4 * y + f] = 1.0
    place = place.reshape(512, 128).astype(jnp.bfloat16)
    tap = np.arange(11)
    spread = np.zeros((2, 128, 9, 128), np.float32)
    for number, (width, weight) in enumerate(zip(FINE_WIDTHS, FINE_WEIGHTS)):
        for place_num, (dx, dy) in enumerate(SIDES):
            per_axis = []
            for step in (dx, dy):
                dist = np.abs(tap[None, :] + 8 * step - tap[:, None]).astype(np.float64)
                per_axis.append(np.where(dist <= REACH, np.exp(-dist * dist / (2 * width * width)), 0.0))
            both = weight * np.kron(per_axis[0], per_axis[1])
            spread[number, :121, place_num, :121] = both
    spread = two_parts(spread.reshape(256, 9 * 128))
    ring = np.zeros((2, 16, 16), np.float32)
    for number, width in enumerate(FINE_WIDTHS):
        dist = np.abs(np.arange(12)[:, None] - np.arange(12)[None, :])
        dist = np.minimum(dist, 12 - dist).astype(np.float64)
        ring[number, :12, :12] = np.where(dist <= REACH, np.exp(-dist * dist / (2 * width * width)), 0.0)
    ring = ring.reshape(32, 16)
    select = np.zeros((2, 12, 8, 128), np.float32)
    for y in range(2):
        for x in range(11):
            for f in range(7):
                select[y, x, f, 11 * x + 4 * y + f] = 1.0
    select = select.reshape(192, 128).astype(jnp.bfloat16)
    total_y = 4 * sub_size
    coarse = np.zeros((2, 2, 8, 8, sub_size, 2, 8, 8), np.float32)
    for number, (fraction, weight) in enumerate(zip(COARSE_FRACTIONS, COARSE_WEIGHTS)):
        dist = np.abs(np.arange(6)[:, None] - np.arange(6)[None, :])
        dist = np.minimum(dist, 6 - dist).astype(np.float64)
        along_z = np.exp(-dist * dist / (2 * (6 / fraction) ** 2))
        for step in range(sub_size):
            dist = np.mod(4 * step + np.arange(6)[None, :] - np.arange(6)[:, None], total_y)
            dist = np.minimum(dist, total_y - dist).astype(np.float64)
            along_y = np.exp(-dist * dist / (2 * (total_y / fraction) ** 2))
            both = 0.125 * weight * along_z[:, None, :, None] * along_y[None, :, None, :]
            for half in range(2):
                coarse[half, number, :6, :6, step, half, :6, :6] = both
    coarse = two_parts(coarse.reshape(256, sub_size * 128))
    return place, spread, ring, select, coarse


def halves(value):
    high = value.astype(BF16).astype(F32)
    return high, value - high


def thirds(value):
    high, rest = halves(value)
    middle, low = halves(rest)
    return high, middle, low


def dot(left, right):
    return lax.dot_general(left, right, (((1,), (0,)), ((), ())), preferred_element_type=F32)


def dot_rows(left, right):
    return lax.dot_general(left, right, (((1,), (1,)), ((), ())), preferred_element_type=F32)


def spline(shifted):
    size = jnp.abs(shifted)
    outer = jnp.maximum(2.0 - size, 0.0)
    inner = jnp.maximum(1.0 - size, 0.0)
    return outer * outer * outer * (1.0 / 6.0) - inner * inner * inner * (2.0 / 3.0)


def spline_slope(shifted):
    size = jnp.abs(shifted)
    outer = jnp.maximum(2.0 - size, 0.0)
    inner = jnp.maximum(1.0 - size, 0.0)
    slope = 2.0 * inner * inner - 0.5 * outer * outer
    return jnp.where(shifted < 0.0, -slope, slope)


def wrapped(shifted):
    return jnp.where(shifted > 6.0, shifted - 12.0, jnp.where(shifted < -6.0, shifted + 12.0, shifted))


def grouped(size, step, start, cells=CELLS):
    def group(number, carry):
        for num in range(size):
            carry = step(number * size + num, carry)
        return carry

    return lax.fori_loop(0, cells // size, group, start)


def row_iota(rows, lanes=128):
    return lax.broadcasted_iota(jnp.int32, (rows, lanes), 0)


def kernel(
    spaces, subs,
    pos_hbm, charge_hbm, count_hbm, place_hbm, wide_hi_hbm, wide_lo_hbm, ring_hbm, select_hbm, far_hi_hbm, far_lo_hbm,
    out_ref,
    pos_ref, charge_ref, count_ref, ring_ref, place_ref, wide_hi, wide_lo, select_ref, far_hi, far_lo,
    ext, lap_buf, plane_out, plane_buf, fine_out, fine_buf,
    fine_sum, by_ref, wz_ref, pair_hi, pair_lo, vx_ref, bells_ref, left_ref, right_ref, mom_ref, square_ref, raw_ref, back_ref, return_out, return_buf, seven_ref, force_ref,
    input_sem, const_sem, halo_send, halo_recv, lap_send, lap_recv, relay_send, relay_recv, return_send, return_recv, fine_send, fine_recv, plane_send, plane_recv,
):
    laps = spaces // 4
    space = lax.axis_index("space")
    sub = lax.axis_index("sub")
    outer_x = space // (2 * laps)
    lap = (space // 2) % laps
    core = space % 2

    loads = [
        pltpu.make_async_copy(src, dst, const_sem.at[num])
        for num, (src, dst) in enumerate((
            (place_hbm, place_ref), (wide_hi_hbm, wide_hi), (wide_lo_hbm, wide_lo),
            (select_hbm, select_ref), (far_hi_hbm, far_hi), (far_lo_hbm, far_lo), (ring_hbm, ring_ref),
        ))
    ]
    inputs = [
        pltpu.make_async_copy(src, dst, input_sem.at[num])
        for num, (src, dst) in enumerate(((pos_hbm, pos_ref), (charge_hbm, charge_ref), (count_hbm, count_ref)))
    ]
    for load in inputs:
        load.start()

    def near_id(side):
        return {"space": (space + side[0] + spaces) % spaces, "sub": (sub + side[1] + subs) % subs}

    def lap_id(step):
        return {"space": outer_x * 2 * laps + ((lap + step + laps) % laps) * 2 + core, "sub": sub}

    def plane_id(member, step):
        return {
            "space": ((outer_x + member // 2) % 2) * 2 * laps + lap * 2 + (core + member % 2) % 2,
            "sub": (sub + step) % subs,
        }

    members = [(member, step) for member in range(4) for step in range(subs) if (member, step) != (0, 0)]
    barrier = pltpu.get_barrier_semaphore()
    for step in sorted(LAPS, key=abs, reverse=True):
        pl.semaphore_signal(barrier, inc=1, device_id=lap_id(step), device_id_type=MESH)
    for member, step in sorted(members, key=lambda one: min(one[1], subs - one[1]), reverse=True):
        pl.semaphore_signal(barrier, inc=1, device_id=plane_id(member, step), device_id_type=MESH)
    for side in NEAR:
        pl.semaphore_signal(barrier, inc=1, device_id=near_id(side), device_id_type=MESH)

    for load in loads:
        load.start()
    for load in inputs:
        load.wait()
    lane = lax.broadcasted_iota(jnp.int32, (1, 128), 1)
    for x in range(2):
        for y in range(2):
            for z in range(3):
                lanes = pl.ds(128 * z, 128)
                for k in range(3):
                    ext[1 + x, 1 + y, pl.ds(k, 1), lanes] = pos_ref[k, x, z, pl.ds(y, 1), :]
                live = lane < count_ref[x, y, z]
                ext[1 + x, 1 + y, pl.ds(3, 1), lanes] = jnp.where(live, charge_ref[x, z, pl.ds(y, 1), :], 0.0)

    def cell_rows(cell):
        x, y, z = cell // 6, (cell // 3) % 2, cell % 3
        at = 128 * z if isinstance(z, int) else pl.multiple_of(z * 128, 128)
        return x, y, z, ext[1 + x, 1 + y, :, pl.ds(at, 128)]

    def real(value):
        return float(value) if isinstance(value, int) else value.astype(F32)

    def padded(block):
        return jnp.concatenate([block, jnp.zeros_like(block)], axis=0)

    row8 = row_iota(8).astype(F32)
    row16 = row_iota(16).astype(F32)

    row_map = jnp.where(row8 > 3.0, row8 - 1.0, row8)
    row_live = (row8 != 3.0) & (row8 != 7.0)

    def coarse_weights(cell, shape):
        x, y, z, block = cell_rows(cell)
        at_x = 4.0 * block[0:1] + real(4 * x + 2) - 2.0 * row_map
        at_y = 4.0 * block[1:2] + real(4 * y + 2) - 2.0 * row8
        at_z = 4.0 * block[2:3] + real(4 * z) - 2.0 * row8
        vx = jnp.where(row_live, shape(at_x) + shape(at_x - 1.0), 0.0)
        vy = shape(at_y) + shape(at_y - 1.0)
        vz = jnp.where(row8 < 6.0, shape(wrapped(at_z)) + shape(wrapped(at_z - 1.0)), 0.0)
        return vx, vy, vz, block[3:4]

    pad = jnp.zeros((16, 128), F32)
    total = jnp.zeros((16, 128), F32)
    for cell in range(CELLS):
        vx, vy, vz, charge = coarse_weights(cell, spline)
        vz = vz * charge
        high, low = halves(jnp.concatenate([vz[k : k + 1] * vy for k in range(6)], axis=0))
        right = jnp.concatenate([high, pad, low, pad], axis=0).astype(BF16)
        total = total + dot_rows(jnp.concatenate(halves(vx), axis=0).astype(BF16), right)
    total = total[0:8] + total[8:16]
    total = total + pltpu.roll(total, 64, 1)
    lap_buf[0] = jnp.where(lane < 64, total[0:4], total[4:8])

    def tables_step(cell, carry):
        vx, vy, vz, charge = coarse_weights(cell, spline)
        sx, sy, sz, charge = coarse_weights(cell, spline_slope)
        lanes = pl.ds(pl.multiple_of(cell * 384, 128), 384)
        tables = jnp.concatenate(
            [
                jnp.concatenate([one[k : k + 1] * other for k in range(6)], axis=0)
                for one, other in ((vz, vy), (vz, sy), (sz, vy))
            ],
            axis=1,
        )
        high, low = halves(tables)
        pair_hi[:, lanes] = high.astype(BF16)
        pair_lo[:, lanes] = low.astype(BF16)
        pull = -4.0 * charge
        vx_ref[:, lanes] = jnp.concatenate([sx * pull, vx * pull, vx * pull], axis=1)
        return carry

    row_w = row_iota(8, 640)
    slot_w = lax.broadcasted_iota(jnp.int32, (8, 640), 1) // 128

    def column_step(column, carry):
        x, y = column // 4, column % 4
        block = ext[x, y]
        block = padded(jnp.concatenate([block[:, 256:384], block, block[:, 0:128]], axis=1))
        shift = jnp.where(
            row_w == 0, (x - 2).astype(F32), jnp.where(row_w == 1, (y - 2).astype(F32), slot_w.astype(F32) - 2.5)
        )
        coords = jnp.where(row_w < 3, SPLIT_RATE * (block + shift), 0.0)
        square = jnp.sum(coords * coords, axis=0, keepdims=True) + SPLIT_RATE * SPLIT_RATE * SOFT_SQUARE
        ones = jnp.where(row_w == 3, 1.0, 0.0)
        p1, p2, p3 = thirds(coords)
        squares_of = thirds(square)

        def with_square(part, num):
            return jnp.where(row_w == 4, squares_of[num], part + ones)

        right_ref[column] = jnp.concatenate(
            [with_square(p1, 0), with_square(p2, 1), with_square(p1, 2), p3, p2, p1], axis=0
        ).astype(BF16)
        moments = (coords + ones) * block[3:4]
        m1, m2, m3 = thirds(moments)
        mom_ref[column] = jnp.concatenate([m1, m2, m3, jnp.zeros_like(m1)], axis=0).astype(BF16)
        return carry

    for column in (5, 6, 9, 10):
        column_step(jnp.int32(column), 0)

    row_c = row_iota(8)

    def left_step(cell, carry):
        x, y, z, block = cell_rows(cell)
        block = padded(block)
        shift = jnp.where(
            row_c == 0, real(x - 1), jnp.where(row_c == 1, real(y - 1), real(z) - 1.5)
        )
        coords = jnp.where(row_c < 3, SPLIT_RATE * (block + shift), 0.0)
        square = jnp.sum(coords * coords, axis=0, keepdims=True)

        ones = jnp.where(row_c == 4, 1.0, 0.0)
        p1, p2, p3 = thirds(-2.0 * coords)
        q1, q2, q3 = [jnp.where(row_c == 3, part, ones) for part in thirds(square)]
        stacked = jnp.concatenate([p1 + q1, p1 + q2, p2 + q3, p1, p2, p3, jnp.zeros((80, 128), F32)], axis=0)
        left_ref[cell] = jnp.transpose(stacked).astype(BF16)
        return carry

    for cell in range(CELLS):
        left_step(cell, 0)

    def slot_lanes(slot, count=1):
        return pl.ds(pl.multiple_of(slot * 128, 128), 128 * count)

    def squares(plan, z, half):
        at = 0
        for one in range(4):
            left = left_ref[3 * one + z][:, 0:48]
            for column, slots in plan[one]:
                square_ref[half, :, 128 * at : 128 * (at + len(slots))] = dot(
                    left, right_ref[column, :, slot_lanes(z + slots[0], len(slots))]
                )
                at += len(slots)

    def pulls(plan, z, half, first):
        at = 0
        for one in range(4):
            own = INNER[one]
            moments = jnp.zeros((128, 32), F32) if first else raw_ref[3 * one + z]
            for column, slot in [(column, slot) for column, slots in plan[one] for slot in slots]:
                square = square_ref[half, :, 128 * at : 128 * (at + 1)]
                inverse = lax.rsqrt(square)
                far = 1.0 - lax.erf(square * inverse)
                bell = (2.0 / math.sqrt(math.pi)) * jnp.exp2(square * -LOG2E)
                factor = (inverse * inverse) * (far * inverse + bell)
                high = factor.astype(BF16)
                low = (factor - high.astype(F32)).astype(BF16)
                other = mom_ref[column, :, slot_lanes(z + slot)]
                moments = moments + dot_rows(jnp.concatenate([high, low], axis=1), jnp.concatenate([other, other], axis=1))
                if (column, slot) != (own, 1):
                    z_other = (z + slot + 2) % 3
                    back = mom_ref[own, :, slot_lanes(z_other + 2 - slot)]
                    back_ref[3 * column + z_other] += dot(
                        jnp.concatenate([back, back], axis=1), jnp.concatenate([high, low], axis=0)
                    )
                at += 1
            raw_ref[3 * one + z] = moments

    def sweep(plan, start, stop, first):
        squares(plan, start, 0)
        for z in range(start, stop):
            if z + 1 < stop:
                squares(plan, z + 1, (z + 1 - start) % 2)
            pulls(plan, z, (z - start) % 2, first)

    def summed(rows):
        return rows[0:8] + rows[8:16] + rows[16:24]

    def finish(cell):
        x, y, z = cell // 6, (cell // 3) % 2, cell % 3
        block = padded(ext[1 + x, 1 + y, :, 128 * z : 128 * (z + 1)])
        moments = summed(jnp.transpose(raw_ref[cell]) + back_ref[3 * INNER[2 * x + y] + z])
        for num, group in enumerate(FROM):
            for place, column in enumerate(group):
                if column == (1 + x, 1 + y):
                    moments = moments + padded(return_buf[num, place, :, 128 * z : 128 * (z + 1)])
        shift = jnp.where(row_c == 0, x - 1.0, jnp.where(row_c == 1, y - 1.0, z - 1.5))
        coords = SPLIT_RATE * (block + shift)
        force_ref[cell] = (SPLIT_RATE * SPLIT_RATE) * block[3:4] * (coords * moments[3:4] - moments)

    rows = lax.broadcasted_iota(jnp.int32, (128, 64), 0)
    cols = lax.broadcasted_iota(jnp.int32, (128, 64), 1)
    member = (rows // 4) % 4
    to_space = ((outer_x + member // 2) % 2) * 2 * laps + lap * 2 + (core + member % 2) % 2
    from_space = outer_x * 2 * laps + ((lap + cols // 4) % laps) * 2 + core
    total_x = 4 * spaces
    to_row = 3 * ((rows // 16) % 2) + rows % 4
    from_row = 3 * (rows // 64) + cols % 4
    dist = (4 * (to_space - from_space) + to_row - from_row + 2 * total_x) % total_x
    dist = jnp.minimum(dist, total_x - dist).astype(F32)
    wide = [2.0 * (total_x / fraction) ** 2 for fraction in COARSE_FRACTIONS]
    bells = jnp.exp(-dist * dist * jnp.where((rows // 32) % 2 == 0, 1.0 / wide[0], 1.0 / wide[1]))
    bells_ref[...] = jnp.concatenate(halves(bells), axis=0).astype(BF16)

    back_ref[...] = jnp.zeros_like(back_ref)
    for one in range(4):
        raw_ref[3 * one + 2] = jnp.zeros((128, 32), F32)

    pl.semaphore_wait(barrier, len(NEAR) + len(LAPS) + len(members))

    for num, step in sorted(enumerate(LAPS), key=lambda one: -abs(one[1])):
        copy = pltpu.make_async_remote_copy(
            src_ref=lap_buf.at[0], dst_ref=lap_buf.at[(-step) % laps], send_sem=lap_send.at[0], recv_sem=lap_recv.at[num // 4],
            device_id=lap_id(step), device_id_type=MESH,
        )
        copy.start()

    for num, side in enumerate(AHEAD):
        (x, y), (to_x, to_y) = FROM[num][0], INTO[num][0]
        span_x, span_y = FROM[num][-1][0] - x + 1, FROM[num][-1][1] - y + 1
        copy = pltpu.make_async_remote_copy(
            src_ref=ext.at[pl.ds(x, span_x), pl.ds(y, span_y)], dst_ref=ext.at[pl.ds(to_x, span_x), pl.ds(to_y, span_y)],
            send_sem=halo_send.at[0], recv_sem=halo_recv.at[0],
            device_id=near_id((-side[0], -side[1])), device_id_type=MESH,
        )
        copy.start()

    fine_sum[...] = jnp.zeros_like(fine_sum)

    def fine_step(cell, carry):
        x, y, z, block = cell_rows(cell)
        at_x = 4.0 * block[0:1] - (row8 - 1.0)
        at_y = 4.0 * block[1:2] - (row8 - 1.0)
        at_z = wrapped(4.0 * block[2:3] + real(4 * z) - row16)
        bx, by = spline(at_x), spline(at_y)
        bz = jnp.where(row16 < 12.0, spline(at_z), 0.0)
        sz = jnp.where(row16 < 12.0, spline_slope(at_z), 0.0)
        by_ref[cell] = jnp.concatenate([bx, spline_slope(at_x), by, spline_slope(at_y)], axis=0)
        bx_charge = bx * block[3:4]
        product = jnp.concatenate([bx_charge[e : e + 1] * by for e in range(7)] + [jnp.zeros((8, 128), F32)], axis=0)
        right = jnp.concatenate(halves(product), axis=0).astype(BF16)
        high, low = halves(jnp.concatenate([bz, sz], axis=1))
        left = jnp.concatenate([high[:, 0:128], low[:, 0:128]], axis=0).astype(BF16)
        wz_ref[cell] = jnp.concatenate([high, high, high, low, low, low], axis=0).astype(BF16)
        fine_sum[cell // 3] += dot_rows(left, right)
        return carry

    for cell in range(CELLS):
        fine_step(cell, 0)
    for load in loads:
        load.wait()
    boxes = jnp.concatenate([fine_sum[num, 0:16] + fine_sum[num, 16:32] for num in range(4)], axis=1)
    spots = dot(jnp.concatenate(thirds(boxes), axis=0).astype(BF16), place_ref[...])
    spots = spots[0:16] + spots[16:32] + spots[32:48]
    rings = lax.dot_general(
        ring_ref[...], spots, (((1,), (0,)), ((), ())), precision=HIGHEST, preferred_element_type=F32
    )
    rings = jnp.concatenate([rings[0:16], rings[16:32]], axis=1)
    parts = jnp.concatenate(halves(rings), axis=0).astype(BF16)
    fine_all = dot(parts, wide_hi[...])
    fine_all = fine_all[0:16] + fine_all[16:32] + dot(parts[0:16], wide_lo[...])
    for num in range(9):
        fine_out[num] = fine_all[:, 128 * num : 128 * (num + 1)]
    for num, side in enumerate(NEAR):
        copy = pltpu.make_async_remote_copy(
            src_ref=fine_out.at[SIDES.index(side)], dst_ref=fine_buf.at[num],
            send_sem=fine_send.at[0], recv_sem=fine_recv.at[0], device_id=near_id(side), device_id_type=MESH,
        )
        copy.start()


    sweep(INNER_PLAN, 0, 2, True)

    relays = []
    for num, (src, dst, step) in enumerate((
        (pl.ds(1, 4), pl.ds(5, 4), -4),
        (pl.ds(laps - 3, 3), pl.ds(laps - 7, 3), 4),
    )):
        landed = lap_buf.at[pl.ds(laps - 4 if num else 1, 4)]
        pltpu.make_async_remote_copy(
            src_ref=landed, dst_ref=landed, send_sem=lap_send.at[0], recv_sem=lap_recv.at[1 - num],
            device_id=lap_id(1), device_id_type=MESH,
        ).wait_recv()
        copy = pltpu.make_async_remote_copy(
            src_ref=lap_buf.at[src], dst_ref=lap_buf.at[dst], send_sem=relay_send.at[num], recv_sem=relay_recv.at[num],
            device_id=lap_id(step), device_id_type=MESH,
        )
        copy.start()
        relays.append(copy)

    halo_all = pltpu.make_async_remote_copy(
        src_ref=seven_ref, dst_ref=seven_ref, send_sem=halo_send.at[0], recv_sem=halo_recv.at[0],
        device_id=near_id((0, 1)), device_id_type=MESH,
    )
    halo_all.wait_recv()
    for column in RIM:
        column_step(jnp.int32(column), 0)
    sweep(OUTER_PLAN, 0, 3, False)

    for num, side in enumerate(AHEAD):
        shift = jnp.where(row_c == 0, 2.0 * SPLIT_RATE * side[0], jnp.where(row_c == 1, 2.0 * SPLIT_RATE * side[1], 0.0))
        for place, (x, y) in enumerate(INTO[num]):
            for z in range(3):
                moments = summed(back_ref[3 * (4 * x + y) + z])
                return_out[num, place, :, 128 * z : 128 * (z + 1)] = (moments - shift * moments[3:4])[0:4]
        count = len(INTO[num])
        copy = pltpu.make_async_remote_copy(
            src_ref=return_out.at[num, pl.ds(0, count)], dst_ref=return_buf.at[num, pl.ds(0, count)],
            send_sem=return_send.at[0], recv_sem=return_recv.at[0], device_id=near_id(side), device_id_type=MESH,
        )
        copy.start()

    for copy in relays:
        copy.wait_recv()
    gathered = jnp.concatenate([lap_buf[num] for num in range(laps)], axis=0)
    along_x = dot(bells_ref[...], jnp.concatenate(halves(gathered), axis=1).astype(BF16))
    along_x = along_x[0:128, 0:128] + along_x[0:128, 128:256] + along_x[128:256, 0:128]
    turned = pltpu.roll(along_x, 64, 1)
    along_x = jnp.where(lane < 64, along_x[0:32] + turned[64:96], turned[32:64] + along_x[96:128])
    parts = jnp.concatenate(halves(jnp.concatenate([along_x[0:16], along_x[16:32]], axis=1)), axis=0).astype(BF16)
    shares = dot(parts, far_hi[...])
    shares = shares[0:16] + shares[16:32] + dot(parts[0:16], far_lo[...])
    for member_num in range(4):
        for step in range(subs):
            plane_out[member_num * subs + step] = shares[4 * member_num : 4 * member_num + 4, 128 * step : 128 * (step + 1)]
    for member_num, step in sorted(members, key=lambda one: -min(one[1], subs - one[1])):
        num = member_num * subs + step
        copy = pltpu.make_async_remote_copy(
            src_ref=plane_out.at[num], dst_ref=plane_buf.at[num], send_sem=plane_send.at[0], recv_sem=plane_recv.at[0],
            device_id=plane_id(member_num, step), device_id_type=MESH,
        )
        copy.start()


    sweep(INNER_PLAN, 2, 3, False)
    grouped(6, tables_step, 0)

    fine_all_in = pltpu.make_async_remote_copy(
        src_ref=fine_buf, dst_ref=fine_buf, send_sem=fine_send.at[0], recv_sem=fine_recv.at[0], device_id=near_id((0, 1)), device_id_type=MESH,
    )
    fine_all_in.wait_recv()
    fine = fine_out[SIDES.index((0, 0))]
    for num in range(8):
        fine = fine + fine_buf[num]
    pieces = thirds(fine)
    points = dot_rows(select_ref[...], jnp.concatenate(pieces + pieces, axis=0).astype(BF16)).astype(BF16)
    fine_sum_rows = points

    def interpolate(cell, x, y):
        start = 96 * y + 32 * x
        spread = dot(fine_sum_rows[start : start + 64], wz_ref[cell])
        tables = by_ref[cell]
        u1 = jnp.zeros((8, 128), F32)
        u2 = jnp.zeros((8, 128), F32)
        u3 = jnp.zeros((8, 128), F32)
        for e in range(7):
            at = spread[8 * e : 8 * e + 8]
            u1 = u1 + tables[8 + e : 9 + e] * at[:, 0:128]
            u2 = u2 + tables[e : e + 1] * at[:, 0:128]
            u3 = u3 + tables[e : e + 1] * at[:, 128:256]
        by, sy = tables[16:24], tables[24:32]
        return [jnp.sum(one * other, axis=0, keepdims=True) for one, other in ((by, u1), (sy, u2), (by, u3))]

    fine_forces = [interpolate(cell, cell // 6, (cell // 3) % 2) for cell in range(CELLS)]

    return_all = pltpu.make_async_remote_copy(
        src_ref=seven_ref, dst_ref=seven_ref, send_sem=return_send.at[0], recv_sem=return_recv.at[0],
        device_id=near_id((0, 1)), device_id_type=MESH,
    )
    return_all.wait_recv()
    for cell in range(CELLS):
        finish(cell)
        x, y, z = cell // 6, (cell // 3) % 2, cell % 3
        pull = -4.0 * ext[1 + x, 1 + y, pl.ds(3, 1), pl.ds(128 * z, 128)]
        for k in range(3):
            force_ref[cell, pl.ds(k, 1), :] += pull * fine_forces[cell][k]

    plane_all_in = pltpu.make_async_remote_copy(
        src_ref=plane_out.at[pl.ds(1, 4 * subs - 1)], dst_ref=plane_buf.at[pl.ds(1, 4 * subs - 1)], send_sem=plane_send.at[0], recv_sem=plane_recv.at[0], device_id=plane_id(0, 1), device_id_type=MESH,
    )
    plane_all_in.wait_recv()
    pieces = [plane_out[0]] + [plane_buf[member_num * subs + step] for member_num, step in members]
    while len(pieces) > 1:
        pieces = [sum(pieces[num : num + 2][1:], pieces[num]) for num in range(0, len(pieces), 2)]
    window = pieces[0]
    window = jnp.concatenate([window, pltpu.roll(window, 64, 1)], axis=0)
    parts = jnp.concatenate(halves(window), axis=0).astype(BF16)[:, 0:48]
    for cell in range(CELLS):
        x, y, z = cell // 6, (cell // 3) % 2, cell % 3
        lanes = pl.ds(384 * cell, 384)
        spread = dot(parts, pair_hi[:, lanes])
        spread = spread[0:8] + spread[8:16] + dot(parts, pair_lo[:, lanes])[0:8]
        spread = jnp.sum(spread * vx_ref[:, lanes], axis=0, keepdims=True)
        for k in range(3):
            out_ref[k, x, z, pl.ds(y, 1), :] = force_ref[cell, pl.ds(k, 1), :] + spread[:, 128 * k : 128 * (k + 1)]

    lap_all_out = pltpu.make_async_remote_copy(
        src_ref=lap_buf.at[pl.ds(0, 8)], dst_ref=lap_buf.at[pl.ds(0, 8)], send_sem=lap_send.at[0], recv_sem=lap_recv.at[0], device_id=lap_id(1), device_id_type=MESH,
    )
    lap_all_out.wait_send()
    fine_all_in.wait_send()
    plane_all_in.wait_send()
    halo_all.wait_send()
    return_all.wait_send()
    for copy in relays:
        copy.wait_send()


def solution(mesh):
    spaces, subs = mesh.shape["space"], mesh.shape["sub"]
    laps = spaces // 4
    place, spread, ring, select, coarse = constants(subs)

    def body(positions, charges, counts):
        any_spec = pl.BlockSpec(memory_space=pl.ANY)
        vmem_spec = pl.BlockSpec(memory_space=pltpu.VMEM)
        planes = 4 * subs
        positions = jnp.transpose(positions, (0, 1, 3, 2, 4))
        charges = jnp.transpose(charges, (0, 2, 1, 3))
        forces = pl.pallas_call(
            functools.partial(kernel, spaces, subs),
            out_shape=pltpu.VMEM(positions.shape, F32),
            in_specs=[any_spec] * 10,
            out_specs=vmem_spec,
            scratch_shapes=[
                pltpu.VMEM((3, 2, 3, 2, 128), F32),
                pltpu.VMEM((2, 3, 2, 128), F32),
                pltpu.SMEM((2, 2, 3), jnp.int32),
                pltpu.VMEM((32, 16), F32),
                pltpu.VMEM((512, 128), BF16),
                pltpu.VMEM((256, 1152), BF16),
                pltpu.VMEM((256, 1152), BF16),
                pltpu.VMEM((192, 128), BF16),
                pltpu.VMEM((256, 128 * subs), BF16),
                pltpu.VMEM((256, 128 * subs), BF16),
                pltpu.VMEM((4, 4, 4, 384), F32),
                pltpu.VMEM((laps, 4, 128), F32),
                pltpu.VMEM((planes, 4, 128), F32),
                pltpu.VMEM((planes, 4, 128), F32),
                pltpu.VMEM((9, 16, 128), F32),
                pltpu.VMEM((8, 16, 128), F32),
                pltpu.VMEM((4, 32, 128), F32),
                pltpu.VMEM((CELLS, 32, 128), F32),
                pltpu.VMEM((CELLS, 96, 256), BF16),
                pltpu.VMEM((48, CELLS * 384), BF16),
                pltpu.VMEM((48, CELLS * 384), BF16),
                pltpu.VMEM((8, CELLS * 384), F32),
                pltpu.VMEM((256, 64), BF16),
                pltpu.VMEM((CELLS, 128, 128), BF16),
                pltpu.VMEM((16, 48, 640), BF16),
                pltpu.VMEM((16, 32, 640), BF16),
                pltpu.VMEM((2, 128, 3840), F32),
                pltpu.VMEM((CELLS, 128, 32), F32),
                pltpu.VMEM((48, 32, 128), F32),
                pltpu.VMEM((5, 2, 4, 384), F32),
                pltpu.VMEM((5, 2, 4, 384), F32),
                pltpu.VMEM((7, 4, 384), F32),
                pltpu.VMEM((CELLS, 8, 128), F32),
                pltpu.SemaphoreType.DMA((3,)),
                pltpu.SemaphoreType.DMA((7,)),
                pltpu.SemaphoreType.DMA((1,)),
                pltpu.SemaphoreType.DMA((1,)),
                pltpu.SemaphoreType.DMA((1,)),
                pltpu.SemaphoreType.DMA((2,)),
                pltpu.SemaphoreType.DMA((2,)),
                pltpu.SemaphoreType.DMA((2,)),
                pltpu.SemaphoreType.DMA((1,)),
                pltpu.SemaphoreType.DMA((1,)),
                pltpu.SemaphoreType.DMA((1,)),
                pltpu.SemaphoreType.DMA((1,)),
                pltpu.SemaphoreType.DMA((1,)),
                pltpu.SemaphoreType.DMA((1,)),
            ],
            compiler_params=pltpu.CompilerParams(collective_id=0, has_side_effects=True),
        )(
            positions, charges, counts,
            jnp.asarray(place), jnp.asarray(spread[0]), jnp.asarray(spread[1]), jnp.asarray(ring), jnp.asarray(select),
            jnp.asarray(coarse[0]), jnp.asarray(coarse[1]),
        )
        return jnp.transpose(forces, (0, 1, 3, 2, 4))

    in_specs = (
        P(None, "space", "sub", None, None),
        P("space", "sub", None, None),
        P("space", "sub", None),
    )
    out_specs = P(None, "space", "sub", None, None)
    return jax.shard_map(body, mesh=mesh, in_specs=in_specs, out_specs=out_specs, check_vma=False)
```

```python
import functools
import math

import jax
import jax.numpy as jnp
import numpy as np
from jax import lax
from jax.experimental import pallas as pl
from jax.experimental.pallas import tpu as pltpu
from jax.sharding import PartitionSpec as P

F32 = jnp.float32
BF16 = jnp.bfloat16
MESH = pl.DeviceIdType.MESH
HIGHEST = lax.Precision.HIGHEST
SPLIT_RATE = 0.8
SOFT_SQUARE = 0.0625
FINE_WIDTHS = (1.0, 2.0)
FINE_WEIGHTS = (2.0, 0.5)
COARSE_FRACTIONS = (8.0, 4.0)
COARSE_WEIGHTS = (4.0, 2.0)
REACH = 4
SIDES = [(dx, dy) for dx in (-1, 0, 1) for dy in (-1, 0, 1)]
NEAR = [side for side in SIDES if side != (0, 0)]
LAPS = (1, 2, 3, 4, -1, -2, -3, -4)
CELLS = 12
INNER = (5, 6, 9, 10)
AHEAD = ((1, 0), (0, 1), (1, 1), (1, -1), (0, -1))
FROM = (((1, 1), (1, 2)), ((1, 1), (2, 1)), ((1, 1),), ((1, 2),), ((2, 2),))
INTO = (((3, 1), (3, 2)), ((1, 3), (2, 3)), ((3, 3),), ((3, 0),), ((2, 0),))
RIM = tuple(4 * x + y for group in INTO for x, y in group)
INNER_PLAN = [
    [(INNER[one], (1, 2))] + [(INNER[other], (0, 1, 2)) for other in range(one + 1, 4)] for one in range(4)
]
OUTER_PLAN = [
    [
        (4 * (1 + x + dx) + 1 + y + dy, (0, 1, 2))
        for dx, dy in ((1, -1), (1, 0), (1, 1), (0, 1))
        if x + dx > 1 or not 0 <= y + dy <= 1
    ]
    for x in range(2)
    for y in range(2)
]
LOG2E = math.log2(math.e)


def two_parts(table):
    table = np.asarray(table, np.float32)
    high = table.astype(jnp.bfloat16)
    low = (table - high.astype(np.float32)).astype(jnp.bfloat16)
    return high, low


def constants(sub_size):
    place = np.zeros((4, 2, 64, 128), np.float32)
    for x in range(2):
        for y in range(2):
            for e in range(7):
                for f in range(7):
                    place[2 * x + y, :, 8 * e + f, 11 * (4 * x + e) + 4 * y + f] = 1.0
    place = place.reshape(512, 128).astype(jnp.bfloat16)
    tap = np.arange(11)
    spread = np.zeros((2, 128, 9, 128), np.float32)
    for number, (width, weight) in enumerate(zip(FINE_WIDTHS, FINE_WEIGHTS)):
        for place_num, (dx, dy) in enumerate(SIDES):
            per_axis = []
            for step in (dx, dy):
                dist = np.abs(tap[None, :] + 8 * step - tap[:, None]).astype(np.float64)
                per_axis.append(np.where(dist <= REACH, np.exp(-dist * dist / (2 * width * width)), 0.0))
            both = weight * np.kron(per_axis[0], per_axis[1])
            spread[number, :121, place_num, :121] = both
    spread = two_parts(spread.reshape(256, 9 * 128))
    ring = np.zeros((2, 16, 16), np.float32)
    for number, width in enumerate(FINE_WIDTHS):
        dist = np.abs(np.arange(12)[:, None] - np.arange(12)[None, :])
        dist = np.minimum(dist, 12 - dist).astype(np.float64)
        ring[number, :12, :12] = np.where(dist <= REACH, np.exp(-dist * dist / (2 * width * width)), 0.0)
    ring = ring.reshape(32, 16)
    select = np.zeros((2, 12, 8, 128), np.float32)
    for y in range(2):
        for x in range(11):
            for f in range(7):
                select[y, x, f, 11 * x + 4 * y + f] = 1.0
    select = select.reshape(192, 128).astype(jnp.bfloat16)
    total_y = 4 * sub_size
    coarse = np.zeros((2, 2, 8, 8, sub_size, 2, 8, 8), np.float32)
    for number, (fraction, weight) in enumerate(zip(COARSE_FRACTIONS, COARSE_WEIGHTS)):
        dist = np.abs(np.arange(6)[:, None] - np.arange(6)[None, :])
        dist = np.minimum(dist, 6 - dist).astype(np.float64)
        along_z = np.exp(-dist * dist / (2 * (6 / fraction) ** 2))
        for step in range(sub_size):
            dist = np.mod(4 * step + np.arange(6)[None, :] - np.arange(6)[:, None], total_y)
            dist = np.minimum(dist, total_y - dist).astype(np.float64)
            along_y = np.exp(-dist * dist / (2 * (total_y / fraction) ** 2))
            both = 0.125 * weight * along_z[:, None, :, None] * along_y[None, :, None, :]
            for half in range(2):
                coarse[half, number, :6, :6, step, half, :6, :6] = both
    coarse = two_parts(coarse.reshape(256, sub_size * 128))
    return place, spread, ring, select, coarse


def halves(value):
    high = value.astype(BF16).astype(F32)
    return high, value - high


def thirds(value):
    high, rest = halves(value)
    middle, low = halves(rest)
    return high, middle, low


def dot(left, right):
    return lax.dot_general(left, right, (((1,), (0,)), ((), ())), preferred_element_type=F32)


def dot_rows(left, right):
    return lax.dot_general(left, right, (((1,), (1,)), ((), ())), preferred_element_type=F32)


def spline(shifted):
    size = jnp.abs(shifted)
    outer = jnp.maximum(2.0 - size, 0.0)
    inner = jnp.maximum(1.0 - size, 0.0)
    return outer * outer * outer * (1.0 / 6.0) - inner * inner * inner * (2.0 / 3.0)


def spline_slope(shifted):
    size = jnp.abs(shifted)
    outer = jnp.maximum(2.0 - size, 0.0)
    inner = jnp.maximum(1.0 - size, 0.0)
    slope = 2.0 * inner * inner - 0.5 * outer * outer
    return jnp.where(shifted < 0.0, -slope, slope)


def wrapped(shifted):
    return jnp.where(shifted > 6.0, shifted - 12.0, jnp.where(shifted < -6.0, shifted + 12.0, shifted))


def grouped(size, step, start, cells=CELLS):
    def group(number, carry):
        for num in range(size):
            carry = step(number * size + num, carry)
        return carry

    return lax.fori_loop(0, cells // size, group, start)


def row_iota(rows, lanes=128):
    return lax.broadcasted_iota(jnp.int32, (rows, lanes), 0)


def kernel(
    spaces, subs,
    pos_hbm, charge_hbm, count_hbm, place_hbm, wide_hi_hbm, wide_lo_hbm, ring_hbm, select_hbm, far_hi_hbm, far_lo_hbm,
    out_ref,
    pos_ref, charge_ref, count_ref, ring_ref, place_ref, wide_hi, wide_lo, select_ref, far_hi, far_lo,
    ext, lap_buf, plane_out, plane_buf, fine_out, fine_buf,
    fine_sum, by_ref, wz_ref, pair_hi, pair_lo, vx_ref, bells_ref, left_ref, right_ref, mom_ref, square_ref, raw_ref, back_ref, return_out, return_buf, seven_ref, force_ref,
    input_sem, const_sem, halo_send, halo_recv, lap_send, lap_recv, relay_send, relay_recv, return_send, return_recv, fine_send, fine_recv, plane_send, plane_recv,
):
    laps = spaces // 4
    space = lax.axis_index("space")
    sub = lax.axis_index("sub")
    outer_x = space // (2 * laps)
    lap = (space // 2) % laps
    core = space % 2

    loads = [
        pltpu.make_async_copy(src, dst, const_sem.at[num])
        for num, (src, dst) in enumerate((
            (place_hbm, place_ref), (wide_hi_hbm, wide_hi), (wide_lo_hbm, wide_lo),
            (select_hbm, select_ref), (far_hi_hbm, far_hi), (far_lo_hbm, far_lo), (ring_hbm, ring_ref),
        ))
    ]
    inputs = [
        pltpu.make_async_copy(src, dst, input_sem.at[num])
        for num, (src, dst) in enumerate(((pos_hbm, pos_ref), (charge_hbm, charge_ref), (count_hbm, count_ref)))
    ]
    for load in inputs:
        load.start()

    def near_id(side):
        return {"space": (space + side[0] + spaces) % spaces, "sub": (sub + side[1] + subs) % subs}

    def lap_id(step):
        return {"space": outer_x * 2 * laps + ((lap + step + laps) % laps) * 2 + core, "sub": sub}

    def plane_id(member, step):
        return {
            "space": ((outer_x + member // 2) % 2) * 2 * laps + lap * 2 + (core + member % 2) % 2,
            "sub": (sub + step) % subs,
        }

    members = [(member, step) for member in range(4) for step in range(subs) if (member, step) != (0, 0)]
    barrier = pltpu.get_barrier_semaphore()
    for step in sorted(LAPS, key=abs, reverse=True):
        pl.semaphore_signal(barrier, inc=1, device_id=lap_id(step), device_id_type=MESH)
    for member, step in sorted(members, key=lambda one: min(one[1], subs - one[1]), reverse=True):
        pl.semaphore_signal(barrier, inc=1, device_id=plane_id(member, step), device_id_type=MESH)
    for side in NEAR:
        pl.semaphore_signal(barrier, inc=1, device_id=near_id(side), device_id_type=MESH)

    for load in loads:
        load.start()
    for load in inputs:
        load.wait()
    lane = lax.broadcasted_iota(jnp.int32, (1, 128), 1)
    for x in range(2):
        for y in range(2):
            for z in range(3):
                lanes = pl.ds(128 * z, 128)
                for k in range(3):
                    ext[1 + x, 1 + y, pl.ds(k, 1), lanes] = pos_ref[k, x, z, pl.ds(y, 1), :]
                live = lane < count_ref[x, y, z]
                ext[1 + x, 1 + y, pl.ds(3, 1), lanes] = jnp.where(live, charge_ref[x, z, pl.ds(y, 1), :], 0.0)

    def cell_rows(cell):
        x, y, z = cell // 6, (cell // 3) % 2, cell % 3
        at = 128 * z if isinstance(z, int) else pl.multiple_of(z * 128, 128)
        return x, y, z, ext[1 + x, 1 + y, :, pl.ds(at, 128)]

    def real(value):
        return float(value) if isinstance(value, int) else value.astype(F32)

    def padded(block):
        return jnp.concatenate([block, jnp.zeros_like(block)], axis=0)

    row8 = row_iota(8).astype(F32)
    row16 = row_iota(16).astype(F32)

    row_map = jnp.where(row8 > 3.0, row8 - 1.0, row8)
    row_live = (row8 != 3.0) & (row8 != 7.0)

    def coarse_weights(cell, shape):
        x, y, z, block = cell_rows(cell)
        at_x = 4.0 * block[0:1] + real(4 * x + 2) - 2.0 * row_map
        at_y = 4.0 * block[1:2] + real(4 * y + 2) - 2.0 * row8
        at_z = 4.0 * block[2:3] + real(4 * z) - 2.0 * row8
        vx = jnp.where(row_live, shape(at_x) + shape(at_x - 1.0), 0.0)
        vy = shape(at_y) + shape(at_y - 1.0)
        vz = jnp.where(row8 < 6.0, shape(wrapped(at_z)) + shape(wrapped(at_z - 1.0)), 0.0)
        return vx, vy, vz, block[3:4]

    pad = jnp.zeros((16, 128), F32)
    total = jnp.zeros((16, 128), F32)
    for cell in range(CELLS):
        vx, vy, vz, charge = coarse_weights(cell, spline)
        vz = vz * charge
        high, low = halves(jnp.concatenate([vz[k : k + 1] * vy for k in range(6)], axis=0))
        right = jnp.concatenate([high, pad, low, pad], axis=0).astype(BF16)
        total = total + dot_rows(jnp.concatenate(halves(vx), axis=0).astype(BF16), right)
    total = total[0:8] + total[8:16]
    total = total + pltpu.roll(total, 64, 1)
    lap_buf[0] = jnp.where(lane < 64, total[0:4], total[4:8])

    def tables_step(cell, carry):
        vx, vy, vz, charge = coarse_weights(cell, spline)
        sx, sy, sz, charge = coarse_weights(cell, spline_slope)
        lanes = pl.ds(pl.multiple_of(cell * 384, 128), 384)
        tables = jnp.concatenate(
            [
                jnp.concatenate([one[k : k + 1] * other for k in range(6)], axis=0)
                for one, other in ((vz, vy), (vz, sy), (sz, vy))
            ],
            axis=1,
        )
        high, low = halves(tables)
        pair_hi[:, lanes] = high.astype(BF16)
        pair_lo[:, lanes] = low.astype(BF16)
        vx_ref[:, lanes] = jnp.concatenate([sx, vx, vx], axis=1)
        return carry

    row_w = row_iota(8, 640)
    slot_w = lax.broadcasted_iota(jnp.int32, (8, 640), 1) // 128

    def column_step(column, carry):
        x, y = column // 4, column % 4
        block = ext[x, y]
        block = padded(jnp.concatenate([block[:, 256:384], block, block[:, 0:128]], axis=1))
        shift = jnp.where(
            row_w == 0, (x - 2).astype(F32), jnp.where(row_w == 1, (y - 2).astype(F32), slot_w.astype(F32) - 2.5)
        )
        coords = jnp.where(row_w < 3, SPLIT_RATE * (block + shift), 0.0)
        square = jnp.sum(coords * coords, axis=0, keepdims=True) + SPLIT_RATE * SPLIT_RATE * SOFT_SQUARE
        ones = jnp.where(row_w == 3, 1.0, 0.0)
        p1, p2, p3 = thirds(coords)
        squares_of = thirds(square)

        def with_square(part, num):
            return jnp.where(row_w == 4, squares_of[num], part + ones)

        right_ref[column] = jnp.concatenate(
            [with_square(p1, 0), with_square(p2, 1), with_square(p1, 2), p3, p2, p1], axis=0
        ).astype(BF16)
        moments = (coords + ones) * block[3:4]
        m1, m2, m3 = thirds(moments)
        mom_ref[column] = jnp.concatenate([m1, m2, m3, jnp.zeros_like(m1)], axis=0).astype(BF16)
        return carry

    for column in (5, 6, 9, 10):
        column_step(jnp.int32(column), 0)

    row_c = row_iota(8)

    def left_step(cell, carry):
        x, y, z, block = cell_rows(cell)
        block = padded(block)
        shift = jnp.where(
            row_c == 0, real(x - 1), jnp.where(row_c == 1, real(y - 1), real(z) - 1.5)
        )
        coords = jnp.where(row_c < 3, SPLIT_RATE * (block + shift), 0.0)
        square = jnp.sum(coords * coords, axis=0, keepdims=True)

        ones = jnp.where(row_c == 4, 1.0, 0.0)
        p1, p2, p3 = thirds(-2.0 * coords)
        q1, q2, q3 = [jnp.where(row_c == 3, part, ones) for part in thirds(square)]
        stacked = jnp.concatenate([p1 + q1, p1 + q2, p2 + q3, p1, p2, p3, jnp.zeros((80, 128), F32)], axis=0)
        left_ref[cell] = jnp.transpose(stacked).astype(BF16)
        return carry

    for cell in range(CELLS):
        left_step(cell, 0)

    def slot_lanes(slot, count=1):
        return pl.ds(pl.multiple_of(slot * 128, 128), 128 * count)

    def squares(plan, z, half):
        at = 0
        for one in range(4):
            left = left_ref[3 * one + z][:, 0:48]
            for column, slots in plan[one]:
                square_ref[half, :, 128 * at : 128 * (at + len(slots))] = dot(
                    left, right_ref[column, :, slot_lanes(z + slots[0], len(slots))]
                )
                at += len(slots)

    def pulls(plan, z, half, first):
        at = 0
        for one in range(4):
            own = INNER[one]
            moments = jnp.zeros((128, 32), F32) if first else raw_ref[3 * one + z]
            for column, slot in [(column, slot) for column, slots in plan[one] for slot in slots]:
                square = square_ref[half, :, 128 * at : 128 * (at + 1)]
                inverse = lax.rsqrt(square)
                far = 1.0 - lax.erf(square * inverse)
                bell = (2.0 / math.sqrt(math.pi)) * jnp.exp2(square * -LOG2E)
                factor = (inverse * inverse) * (far * inverse + bell)
                high = factor.astype(BF16)
                low = (factor - high.astype(F32)).astype(BF16)
                other = mom_ref[column, :, slot_lanes(z + slot)]
                moments = moments + dot_rows(jnp.concatenate([high, low], axis=1), jnp.concatenate([other, other], axis=1))
                if (column, slot) != (own, 1):
                    z_other = (z + slot + 2) % 3
                    back = mom_ref[own, :, slot_lanes(z_other + 2 - slot)]
                    back_ref[3 * column + z_other] += dot(
                        jnp.concatenate([back, back], axis=1), jnp.concatenate([high, low], axis=0)
                    )
                at += 1
            raw_ref[3 * one + z] = moments

    def sweep(plan, start, stop, first):
        squares(plan, start, 0)
        for z in range(start, stop):
            if z + 1 < stop:
                squares(plan, z + 1, (z + 1 - start) % 2)
            pulls(plan, z, (z - start) % 2, first)

    def summed(rows):
        return rows[0:8] + rows[8:16] + rows[16:24]

    def finish(cell):
        x, y, z = cell // 6, (cell // 3) % 2, cell % 3
        block = padded(ext[1 + x, 1 + y, :, 128 * z : 128 * (z + 1)])
        moments = summed(jnp.transpose(raw_ref[cell]) + back_ref[3 * INNER[2 * x + y] + z])
        for num, group in enumerate(FROM):
            for place, column in enumerate(group):
                if column == (1 + x, 1 + y):
                    moments = moments + padded(return_buf[num, place, :, 128 * z : 128 * (z + 1)])
        shift = jnp.where(row_c == 0, x - 1.0, jnp.where(row_c == 1, y - 1.0, z - 1.5))
        coords = SPLIT_RATE * (block + shift)
        force_ref[cell] = (SPLIT_RATE * SPLIT_RATE) * block[3:4] * (coords * moments[3:4] - moments)

    rows = lax.broadcasted_iota(jnp.int32, (128, 64), 0)
    cols = lax.broadcasted_iota(jnp.int32, (128, 64), 1)
    member = (rows // 4) % 4
    to_space = ((outer_x + member // 2) % 2) * 2 * laps + lap * 2 + (core + member % 2) % 2
    from_space = outer_x * 2 * laps + ((lap + cols // 4) % laps) * 2 + core
    total_x = 4 * spaces
    to_row = 3 * ((rows // 16) % 2) + rows % 4
    from_row = 3 * (rows // 64) + cols % 4
    dist = (4 * (to_space - from_space) + to_row - from_row + 2 * total_x) % total_x
    dist = jnp.minimum(dist, total_x - dist).astype(F32)
    wide = [2.0 * (total_x / fraction) ** 2 for fraction in COARSE_FRACTIONS]
    bells = jnp.exp(-dist * dist * jnp.where((rows // 32) % 2 == 0, 1.0 / wide[0], 1.0 / wide[1]))
    bells_ref[...] = jnp.concatenate(halves(bells), axis=0).astype(BF16)

    back_ref[...] = jnp.zeros_like(back_ref)
    for one in range(4):
        raw_ref[3 * one + 2] = jnp.zeros((128, 32), F32)

    pl.semaphore_wait(barrier, len(NEAR) + len(LAPS) + len(members))

    for num, step in sorted(enumerate(LAPS), key=lambda one: -abs(one[1])):
        copy = pltpu.make_async_remote_copy(
            src_ref=lap_buf.at[0], dst_ref=lap_buf.at[(-step) % laps], send_sem=lap_send.at[0], recv_sem=lap_recv.at[num // 4],
            device_id=lap_id(step), device_id_type=MESH,
        )
        copy.start()

    for num, side in enumerate(AHEAD):
        (x, y), (to_x, to_y) = FROM[num][0], INTO[num][0]
        span_x, span_y = FROM[num][-1][0] - x + 1, FROM[num][-1][1] - y + 1
        copy = pltpu.make_async_remote_copy(
            src_ref=ext.at[pl.ds(x, span_x), pl.ds(y, span_y)], dst_ref=ext.at[pl.ds(to_x, span_x), pl.ds(to_y, span_y)],
            send_sem=halo_send.at[0], recv_sem=halo_recv.at[0],
            device_id=near_id((-side[0], -side[1])), device_id_type=MESH,
        )
        copy.start()

    fine_sum[...] = jnp.zeros_like(fine_sum)

    def fine_step(cell, carry):
        x, y, z, block = cell_rows(cell)
        at_x = 4.0 * block[0:1] - (row8 - 1.0)
        at_y = 4.0 * block[1:2] - (row8 - 1.0)
        at_z = wrapped(4.0 * block[2:3] + real(4 * z) - row16)
        bx, by = spline(at_x), spline(at_y)
        bz = jnp.where(row16 < 12.0, spline(at_z), 0.0)
        sz = jnp.where(row16 < 12.0, spline_slope(at_z), 0.0)
        by_ref[cell] = jnp.concatenate([bx, spline_slope(at_x), by, spline_slope(at_y)], axis=0)
        bx_charge = bx * block[3:4]
        product = jnp.concatenate([bx_charge[e : e + 1] * by for e in range(7)] + [jnp.zeros((8, 128), F32)], axis=0)
        right = jnp.concatenate(halves(product), axis=0).astype(BF16)
        high, low = halves(jnp.concatenate([bz, sz], axis=1))
        left = jnp.concatenate([high[:, 0:128], low[:, 0:128]], axis=0).astype(BF16)
        wz_ref[cell] = jnp.concatenate([high, high, high, low, low, low], axis=0).astype(BF16)
        fine_sum[cell // 3] += dot_rows(left, right)
        return carry

    for cell in range(CELLS):
        fine_step(cell, 0)
    for load in loads:
        load.wait()
    boxes = jnp.concatenate([fine_sum[num, 0:16] + fine_sum[num, 16:32] for num in range(4)], axis=1)
    spots = dot(jnp.concatenate(thirds(boxes), axis=0).astype(BF16), place_ref[...])
    spots = spots[0:16] + spots[16:32] + spots[32:48]
    rings = lax.dot_general(
        ring_ref[...], spots, (((1,), (0,)), ((), ())), precision=HIGHEST, preferred_element_type=F32
    )
    rings = jnp.concatenate([rings[0:16], rings[16:32]], axis=1)
    parts = jnp.concatenate(halves(rings), axis=0).astype(BF16)
    fine_all = dot(parts, wide_hi[...])
    fine_all = fine_all[0:16] + fine_all[16:32] + dot(parts[0:16], wide_lo[...])
    for num in range(9):
        fine_out[num] = fine_all[:, 128 * num : 128 * (num + 1)]
    for num, side in enumerate(NEAR):
        copy = pltpu.make_async_remote_copy(
            src_ref=fine_out.at[SIDES.index(side)], dst_ref=fine_buf.at[num],
            send_sem=fine_send.at[0], recv_sem=fine_recv.at[0], device_id=near_id(side), device_id_type=MESH,
        )
        copy.start()


    sweep(INNER_PLAN, 0, 2, True)

    relays = []
    for num, (src, dst, step) in enumerate((
        (pl.ds(1, 4), pl.ds(5, 4), -4),
        (pl.ds(laps - 3, 3), pl.ds(laps - 7, 3), 4),
    )):
        landed = lap_buf.at[pl.ds(laps - 4 if num else 1, 4)]
        pltpu.make_async_remote_copy(
            src_ref=landed, dst_ref=landed, send_sem=lap_send.at[0], recv_sem=lap_recv.at[1 - num],
            device_id=lap_id(1), device_id_type=MESH,
        ).wait_recv()
        copy = pltpu.make_async_remote_copy(
            src_ref=lap_buf.at[src], dst_ref=lap_buf.at[dst], send_sem=relay_send.at[num], recv_sem=relay_recv.at[num],
            device_id=lap_id(step), device_id_type=MESH,
        )
        copy.start()
        relays.append(copy)

    halo_all = pltpu.make_async_remote_copy(
        src_ref=seven_ref, dst_ref=seven_ref, send_sem=halo_send.at[0], recv_sem=halo_recv.at[0],
        device_id=near_id((0, 1)), device_id_type=MESH,
    )
    halo_all.wait_recv()
    for column in RIM:
        column_step(jnp.int32(column), 0)
    sweep(OUTER_PLAN, 0, 3, False)

    for num, side in enumerate(AHEAD):
        shift = jnp.where(row_c == 0, 2.0 * SPLIT_RATE * side[0], jnp.where(row_c == 1, 2.0 * SPLIT_RATE * side[1], 0.0))
        for place, (x, y) in enumerate(INTO[num]):
            for z in range(3):
                moments = summed(back_ref[3 * (4 * x + y) + z])
                return_out[num, place, :, 128 * z : 128 * (z + 1)] = (moments - shift * moments[3:4])[0:4]
        count = len(INTO[num])
        copy = pltpu.make_async_remote_copy(
            src_ref=return_out.at[num, pl.ds(0, count)], dst_ref=return_buf.at[num, pl.ds(0, count)],
            send_sem=return_send.at[0], recv_sem=return_recv.at[0], device_id=near_id(side), device_id_type=MESH,
        )
        copy.start()

    for copy in relays:
        copy.wait_recv()
    gathered = jnp.concatenate([lap_buf[num] for num in range(laps)], axis=0)
    along_x = dot(bells_ref[...], jnp.concatenate(halves(gathered), axis=1).astype(BF16))
    along_x = along_x[0:128, 0:128] + along_x[0:128, 128:256] + along_x[128:256, 0:128]
    turned = pltpu.roll(along_x, 64, 1)
    along_x = jnp.where(lane < 64, along_x[0:32] + turned[64:96], turned[32:64] + along_x[96:128])
    parts = jnp.concatenate(halves(jnp.concatenate([along_x[0:16], along_x[16:32]], axis=1)), axis=0).astype(BF16)
    shares = dot(parts, far_hi[...])
    shares = shares[0:16] + shares[16:32] + dot(parts[0:16], far_lo[...])
    for member_num in range(4):
        for step in range(subs):
            plane_out[member_num * subs + step] = shares[4 * member_num : 4 * member_num + 4, 128 * step : 128 * (step + 1)]
    for member_num, step in sorted(members, key=lambda one: -min(one[1], subs - one[1])):
        num = member_num * subs + step
        copy = pltpu.make_async_remote_copy(
            src_ref=plane_out.at[num], dst_ref=plane_buf.at[num], send_sem=plane_send.at[0], recv_sem=plane_recv.at[0],
            device_id=plane_id(member_num, step), device_id_type=MESH,
        )
        copy.start()


    sweep(INNER_PLAN, 2, 3, False)
    grouped(6, tables_step, 0)

    fine_all_in = pltpu.make_async_remote_copy(
        src_ref=fine_buf, dst_ref=fine_buf, send_sem=fine_send.at[0], recv_sem=fine_recv.at[0], device_id=near_id((0, 1)), device_id_type=MESH,
    )
    fine_all_in.wait_recv()
    fine = fine_out[SIDES.index((0, 0))]
    for num in range(8):
        fine = fine + fine_buf[num]
    pieces = thirds(fine)
    points = dot_rows(select_ref[...], jnp.concatenate(pieces + pieces, axis=0).astype(BF16)).astype(BF16)
    fine_sum_rows = points

    def interpolate(cell, x, y):
        start = 96 * y + 32 * x
        spread = dot(fine_sum_rows[start : start + 64], wz_ref[cell])
        tables = by_ref[cell]
        u1 = jnp.zeros((8, 128), F32)
        u2 = jnp.zeros((8, 128), F32)
        u3 = jnp.zeros((8, 128), F32)
        for e in range(7):
            at = spread[8 * e : 8 * e + 8]
            u1 = u1 + tables[8 + e : 9 + e] * at[:, 0:128]
            u2 = u2 + tables[e : e + 1] * at[:, 0:128]
            u3 = u3 + tables[e : e + 1] * at[:, 128:256]
        by, sy = tables[16:24], tables[24:32]
        return [jnp.sum(one * other, axis=0, keepdims=True) for one, other in ((by, u1), (sy, u2), (by, u3))]

    fine_forces = [interpolate(cell, cell // 6, (cell // 3) % 2) for cell in range(CELLS)]

    return_all = pltpu.make_async_remote_copy(
        src_ref=seven_ref, dst_ref=seven_ref, send_sem=return_send.at[0], recv_sem=return_recv.at[0],
        device_id=near_id((0, 1)), device_id_type=MESH,
    )
    return_all.wait_recv()
    for cell in range(CELLS):
        finish(cell)

    plane_all_in = pltpu.make_async_remote_copy(
        src_ref=plane_out.at[pl.ds(1, 4 * subs - 1)], dst_ref=plane_buf.at[pl.ds(1, 4 * subs - 1)], send_sem=plane_send.at[0], recv_sem=plane_recv.at[0], device_id=plane_id(0, 1), device_id_type=MESH,
    )
    plane_all_in.wait_recv()
    pieces = [plane_out[0]] + [plane_buf[member_num * subs + step] for member_num, step in members]
    while len(pieces) > 1:
        pieces = [sum(pieces[num : num + 2][1:], pieces[num]) for num in range(0, len(pieces), 2)]
    window = pieces[0]
    window = jnp.concatenate([window, pltpu.roll(window, 64, 1)], axis=0)
    parts = jnp.concatenate(halves(window), axis=0).astype(BF16)[:, 0:48]
    for cell in range(CELLS):
        x, y, z = cell // 6, (cell // 3) % 2, cell % 3
        lanes = pl.ds(384 * cell, 384)
        spread = dot(parts, pair_hi[:, lanes])
        spread = spread[0:8] + spread[8:16] + dot(parts, pair_lo[:, lanes])[0:8]
        spread = jnp.sum(spread * vx_ref[:, lanes], axis=0, keepdims=True)
        charge = ext[1 + x, 1 + y, pl.ds(3, 1), pl.ds(128 * z, 128)]
        for k in range(3):
            far = fine_forces[cell][k] + spread[:, 128 * k : 128 * (k + 1)]
            out_ref[k, x, z, pl.ds(y, 1), :] = force_ref[cell, pl.ds(k, 1), :] - 4.0 * charge * far

    lap_all_out = pltpu.make_async_remote_copy(
        src_ref=lap_buf.at[pl.ds(0, 8)], dst_ref=lap_buf.at[pl.ds(0, 8)], send_sem=lap_send.at[0], recv_sem=lap_recv.at[0], device_id=lap_id(1), device_id_type=MESH,
    )
    lap_all_out.wait_send()
    fine_all_in.wait_send()
    plane_all_in.wait_send()
    halo_all.wait_send()
    return_all.wait_send()
    for copy in relays:
        copy.wait_send()


def solution(mesh):
    spaces, subs = mesh.shape["space"], mesh.shape["sub"]
    laps = spaces // 4
    place, spread, ring, select, coarse = constants(subs)

    def body(positions, charges, counts):
        any_spec = pl.BlockSpec(memory_space=pl.ANY)
        vmem_spec = pl.BlockSpec(memory_space=pltpu.VMEM)
        planes = 4 * subs
        positions = jnp.transpose(positions, (0, 1, 3, 2, 4))
        charges = jnp.transpose(charges, (0, 2, 1, 3))
        forces = pl.pallas_call(
            functools.partial(kernel, spaces, subs),
            out_shape=pltpu.VMEM(positions.shape, F32),
            in_specs=[any_spec] * 10,
            out_specs=vmem_spec,
            scratch_shapes=[
                pltpu.VMEM((3, 2, 3, 2, 128), F32),
                pltpu.VMEM((2, 3, 2, 128), F32),
                pltpu.SMEM((2, 2, 3), jnp.int32),
                pltpu.VMEM((32, 16), F32),
                pltpu.VMEM((512, 128), BF16),
                pltpu.VMEM((256, 1152), BF16),
                pltpu.VMEM((256, 1152), BF16),
                pltpu.VMEM((192, 128), BF16),
                pltpu.VMEM((256, 128 * subs), BF16),
                pltpu.VMEM((256, 128 * subs), BF16),
                pltpu.VMEM((4, 4, 4, 384), F32),
                pltpu.VMEM((laps, 4, 128), F32),
                pltpu.VMEM((planes, 4, 128), F32),
                pltpu.VMEM((planes, 4, 128), F32),
                pltpu.VMEM((9, 16, 128), F32),
                pltpu.VMEM((8, 16, 128), F32),
                pltpu.VMEM((4, 32, 128), F32),
                pltpu.VMEM((CELLS, 32, 128), F32),
                pltpu.VMEM((CELLS, 96, 256), BF16),
                pltpu.VMEM((48, CELLS * 384), BF16),
                pltpu.VMEM((48, CELLS * 384), BF16),
                pltpu.VMEM((8, CELLS * 384), F32),
                pltpu.VMEM((256, 64), BF16),
                pltpu.VMEM((CELLS, 128, 128), BF16),
                pltpu.VMEM((16, 48, 640), BF16),
                pltpu.VMEM((16, 32, 640), BF16),
                pltpu.VMEM((2, 128, 3840), F32),
                pltpu.VMEM((CELLS, 128, 32), F32),
                pltpu.VMEM((48, 32, 128), F32),
                pltpu.VMEM((5, 2, 4, 384), F32),
                pltpu.VMEM((5, 2, 4, 384), F32),
                pltpu.VMEM((7, 4, 384), F32),
                pltpu.VMEM((CELLS, 8, 128), F32),
                pltpu.SemaphoreType.DMA((3,)),
                pltpu.SemaphoreType.DMA((7,)),
                pltpu.SemaphoreType.DMA((1,)),
                pltpu.SemaphoreType.DMA((1,)),
                pltpu.SemaphoreType.DMA((1,)),
                pltpu.SemaphoreType.DMA((2,)),
                pltpu.SemaphoreType.DMA((2,)),
                pltpu.SemaphoreType.DMA((2,)),
                pltpu.SemaphoreType.DMA((1,)),
                pltpu.SemaphoreType.DMA((1,)),
                pltpu.SemaphoreType.DMA((1,)),
                pltpu.SemaphoreType.DMA((1,)),
                pltpu.SemaphoreType.DMA((1,)),
                pltpu.SemaphoreType.DMA((1,)),
            ],
            compiler_params=pltpu.CompilerParams(collective_id=0, has_side_effects=True),
        )(
            positions, charges, counts,
            jnp.asarray(place), jnp.asarray(spread[0]), jnp.asarray(spread[1]), jnp.asarray(ring), jnp.asarray(select),
            jnp.asarray(coarse[0]), jnp.asarray(coarse[1]),
        )
        return jnp.transpose(forces, (0, 1, 3, 2, 4))

    in_specs = (
        P(None, "space", "sub", None, None),
        P("space", "sub", None, None),
        P("space", "sub", None),
    )
    out_specs = P(None, "space", "sub", None, None)
    return jax.shard_map(body, mesh=mesh, in_specs=in_specs, out_specs=out_specs, check_vma=False)
```
